32 devices in a mesh: tile: 8 (over z, x), section: 4 (over y, core).
Axes of the slice: x: 2, y: 2, z: 4, core: 2. Of those that a mesh axis runs over, the one named last changes fastest.
Arguments:
- states: bfloat16 [2, 192, 8, 8, 256], P(None, 'tile'), may hold values from -6 to 6
- conv_weight: bfloat16 [4, 2, 3, 3, 256, 256], P('section'), may hold values from -0.1875 to 0.1875
- skip_weight: bfloat16 [4, 256, 256], P('section'), may hold values from -0.375 to 0.375
- bias: bfloat16 [4, 2, 256], P('section'), may hold values from -3 to 3
- placement: int32 [8], replicated, may hold values from 0 to 7, each once
Outputs:
- activations: bfloat16 [4, 2, 192, 8, 8, 256], P('section', None, 'tile')
The draws below stay inside these ranges and needn't reach their ends.
Inputs may be any that keep to these rules, and one draw needn't show every extreme that they name: placement is a permutation of 0 .. 7.
All inputs are finite; a program needn't handle non-finite values.
Results may differ from the reference program's by a relative error of at most 0.017.
Values may be sent and summed in bfloat16 or wider, within the bound.
A program may use at most 64 MiB of HBM per device.

```python
import jax
import jax.numpy as jnp
import numpy as np
from jax import lax

C = 256
LAYERS = 2
MB = 2
PR = 4
TILE = 8
PATCHES = 192
BLOCKS = 8
SECTIONS = 4


def steps_of(own_key, dims, cuts, smallest, high):
    def one(dim, shards_of):
        heights = jax.random.uniform(jax.random.fold_in(jax.random.fold_in(own_key, 6), dim), (shards_of,), jnp.float32, smallest / len(cuts), high / len(cuts))
        return jnp.repeat(jnp.exp(heights), dims[dim] // shards_of).reshape((-1,) + (1,) * (len(dims) - dim - 1))

    loudness = one(*cuts[0])
    for cut in cuts[1:]:
        loudness = loudness * one(*cut)
    return loudness


def normal_values(key, dims, spread, bound, cuts=(), held_as=jnp.bfloat16):
    values = jax.random.normal(key, dims, jnp.float32) * spread
    if len(cuts) > 0:
        values = steps_of(key, dims, cuts, -0.22, 0.18) * values
    return jnp.clip(values, min=-bound, max=bound).astype(held_as)


def setup_inputs(seed: int = 0) -> dict:
    key_list = jax.random.split(jax.random.key(seed), 6)
    states = normal_values(key_list[0], (MB, PATCHES, TILE, TILE, C), 1.0, 6.0, ((1, 8),))
    conv_weight = normal_values(key_list[1], (SECTIONS, LAYERS, 3, 3, C, C), (9 * C // 2) ** -0.5, 0.1875, ((0, 4),))
    skip_weight = normal_values(key_list[2], (SECTIONS, C, C), C ** -0.5, 0.375, ((0, 4),))
    bias = normal_values(key_list[3], (SECTIONS, LAYERS, C), 0.5, 3.0, ((0, 4),))
    placement = jax.random.permutation(key_list[4], BLOCKS).astype(jnp.int32)
    return dict(states=states, conv_weight=conv_weight, skip_weight=skip_weight, bias=bias, placement=placement)


def face_across(face_num, direction):
    cycle = face_num // 4
    column = face_num % 4
    if cycle == 0:
        table = [4 + column, 4 + (column + 1) % 4, (column + 1) % 4, (column + 3) % 4]
    elif cycle == 1:
        table = [8 + (column + 3) % 4, 8 + column, column, (column + 3) % 4]
    else:
        table = [8 + (column + 3) % 4, 8 + (column + 1) % 4, 4 + (column + 1) % 4, 4 + column]
    return table[direction]


def locate(face_num, coord_x, coord_y, face_span):
    if 0 <= coord_x < face_span and 0 <= coord_y < face_span:
        return face_num, coord_x, coord_y
    if coord_x < 0:
        direction = 0
    elif coord_y < 0:
        direction = 1
    elif coord_x >= face_span:
        direction = 2
    else:
        direction = 3
    cycle = face_num // 4
    target = face_across(face_num, direction)
    coord_x = coord_x % face_span
    coord_y = coord_y % face_span
    if (cycle == 0 and direction == 2) or (cycle == 2 and direction == 0):
        coord_x, coord_y = coord_y, face_span - 1 - coord_x
    elif (cycle == 0 and direction == 3) or (cycle == 2 and direction == 1):
        coord_x, coord_y = face_span - 1 - coord_y, coord_x
    return target, coord_x, coord_y


def seam_tables(tiles):
    cell_side = 2
    face_span = tiles * cell_side
    face_tiles = tiles * tiles
    total = 12 * face_tiles
    neighbour = np.zeros((total, 4), np.int32)
    rim_side = np.zeros((total, 4), np.int32)
    flip_flag = np.zeros((total, 4), np.int32)
    for patch_num in range(total):
        cycle = patch_num % 3
        rest = patch_num // 3
        column = rest // face_tiles
        tile_y = (rest % face_tiles) // tiles
        tile_x = rest % tiles
        face_num = 4 * cycle + column
        base_x = tile_x * cell_side
        base_y = tile_y * cell_side
        for side_num in range(4):
            found = []
            for step_num in range(2):
                if side_num == 0:
                    point = (base_x - 1, base_y + step_num)
                elif side_num == 1:
                    point = (base_x + cell_side, base_y + step_num)
                elif side_num == 2:
                    point = (base_x + step_num, base_y - 1)
                else:
                    point = (base_x + step_num, base_y + cell_side)
                found.append(locate(face_num, point[0], point[1], face_span))
            face_a, first_x, first_y = found[0]
            face_b, second_x, second_y = found[1]
            neighbour[patch_num, side_num] = 3 * ((face_a % 4) * face_tiles + (first_y // cell_side) * tiles + first_x // cell_side) + face_a // 4
            if first_x == second_x:
                rim_side[patch_num, side_num] = 0 if first_x % cell_side == 0 else 1
                flip_flag[patch_num, side_num] = 1 if second_y < first_y else 0
            else:
                rim_side[patch_num, side_num] = 2 if first_y % cell_side == 0 else 3
                flip_flag[patch_num, side_num] = 1 if second_x < first_x else 0
    return neighbour, rim_side, flip_flag


def side_rims(fields):
    return jnp.stack([fields[:, :, 0], fields[:, :, -1], fields[:, 0], fields[:, -1]], axis=1)


def seam_padded(fields, neighbour, rim_side, flip_flag):
    rim_stack = side_rims(fields)
    padded = jnp.pad(fields, ((0, 0), (1, 1), (1, 1), (0, 0)))
    for side_num in range(4):
        strips = rim_stack[jnp.asarray(neighbour[:, side_num]), jnp.asarray(rim_side[:, side_num])]
        flipped = jnp.asarray(flip_flag[:, side_num] == 1)
        strips = jnp.where(flipped[:, None, None], strips[:, ::-1], strips)
        if side_num == 0:
            padded = padded.at[:, 1:-1, 0].set(strips)
        elif side_num == 1:
            padded = padded.at[:, 1:-1, -1].set(strips)
        elif side_num == 2:
            padded = padded.at[:, 0, 1:-1].set(strips)
        else:
            padded = padded.at[:, -1, 1:-1].set(strips)
    return padded


def section_apply(inputs, skip_in, conv_w, skip_w, biases, tables):
    hidden = inputs
    for layer_num in range(LAYERS):
        summed = lax.conv_general_dilated(
            seam_padded(hidden, tables[0], tables[1], tables[2]).astype(jnp.float32),
            conv_w[layer_num].astype(jnp.float32),
            (1, 1), "VALID",
            dimension_numbers=("NHWC", "HWIO", "NHWC"),
            precision=lax.Precision.HIGHEST)
        if layer_num == 0:
            summed = summed + jnp.einsum("pijc,cd->pijd", skip_in.astype(jnp.float32), skip_w.astype(jnp.float32), precision=lax.Precision.HIGHEST)
        summed = summed + biases[layer_num].astype(jnp.float32)
        hidden = jax.nn.gelu(summed, approximate=False).astype(jnp.bfloat16)
    return hidden


def reference(states, conv_weight, skip_weight, bias, placement):
    tables = seam_tables(PR)
    half_sections = SECTIONS // 2
    block_len = PATCHES // BLOCKS
    patch_of_row = (placement[:, None].astype(jnp.int32) * block_len + jnp.arange(block_len, dtype=jnp.int32)[None, :]).reshape(-1)
    natural = jnp.zeros_like(states).at[:, patch_of_row].set(states)
    per_batch = []
    for mb_num in range(MB):
        window_in = natural[mb_num]
        outputs = []
        hidden = window_in
        for section_num in range(SECTIONS):
            skip_in = window_in if section_num < half_sections else outputs[section_num - half_sections]
            hidden = section_apply(hidden, skip_in, conv_weight[section_num], skip_weight[section_num], bias[section_num], tables)
            outputs.append(hidden)
        per_batch.append(jnp.stack(outputs))
    result = jnp.stack(per_batch, axis=1)
    return result[:, :, patch_of_row]
```

```python
import functools

import jax
import jax.numpy as jnp
import numpy as np
from jax import lax
from jax.experimental import pallas as pl
from jax.experimental.pallas import tpu as pltpu
from jax.sharding import PartitionSpec as P

LAYERS = 2
PR = 4


def face_across(face_num, direction):
    cycle = face_num // 4
    column = face_num % 4
    if cycle == 0:
        table = [4 + column, 4 + (column + 1) % 4, (column + 1) % 4, (column + 3) % 4]
    elif cycle == 1:
        table = [8 + (column + 3) % 4, 8 + column, column, (column + 3) % 4]
    else:
        table = [8 + (column + 3) % 4, 8 + (column + 1) % 4, 4 + (column + 1) % 4, 4 + column]
    return table[direction]


def locate(face_num, coord_x, coord_y, face_span):
    if 0 <= coord_x < face_span and 0 <= coord_y < face_span:
        return (face_num, coord_x, coord_y)
    if coord_x < 0:
        direction = 0
    elif coord_y < 0:
        direction = 1
    elif coord_x >= face_span:
        direction = 2
    else:
        direction = 3
    cycle = face_num // 4
    target = face_across(face_num, direction)
    coord_x = coord_x % face_span
    coord_y = coord_y % face_span
    if cycle == 0 and direction == 2 or (cycle == 2 and direction == 0):
        coord_x, coord_y = (coord_y, face_span - 1 - coord_x)
    elif cycle == 0 and direction == 3 or (cycle == 2 and direction == 1):
        coord_x, coord_y = (face_span - 1 - coord_y, coord_x)
    return (target, coord_x, coord_y)


def seam_tables(tiles):
    cell_side = 2
    face_span = tiles * cell_side
    face_tiles = tiles * tiles
    total = 12 * face_tiles
    neighbour = np.zeros((total, 4), np.int32)
    rim_side = np.zeros((total, 4), np.int32)
    flip_flag = np.zeros((total, 4), np.int32)
    for patch_num in range(total):
        cycle = patch_num % 3
        rest = patch_num // 3
        column = rest // face_tiles
        tile_y = rest % face_tiles // tiles
        tile_x = rest % tiles
        face_num = 4 * cycle + column
        base_x = tile_x * cell_side
        base_y = tile_y * cell_side
        for side_num in range(4):
            found = []
            for step_num in range(2):
                if side_num == 0:
                    point = (base_x - 1, base_y + step_num)
                elif side_num == 1:
                    point = (base_x + cell_side, base_y + step_num)
                elif side_num == 2:
                    point = (base_x + step_num, base_y - 1)
                else:
                    point = (base_x + step_num, base_y + cell_side)
                found.append(locate(face_num, point[0], point[1], face_span))
            face_a, first_x, first_y = found[0]
            face_b, second_x, second_y = found[1]
            neighbour[patch_num, side_num] = (
                3 * (face_a % 4 * face_tiles + first_y // cell_side * tiles + first_x // cell_side)
                + face_a // 4
            )
            if first_x == second_x:
                rim_side[patch_num, side_num] = 0 if first_x % cell_side == 0 else 1
                flip_flag[patch_num, side_num] = 1 if second_y < first_y else 0
            else:
                rim_side[patch_num, side_num] = 2 if first_y % cell_side == 0 else 3
                flip_flag[patch_num, side_num] = 1 if second_x < first_x else 0
    return (neighbour, rim_side, flip_flag)


def off_device_routes(neighbour, rim_side, flip_flag, tile_count, per_dev):
    source_dev = (neighbour // per_dev).reshape(-1)
    dest_dev = np.repeat(np.arange(neighbour.shape[0]) // per_dev, 4)
    row = (neighbour % per_dev * 4 + rim_side).reshape(-1)
    away = source_dev != dest_dev
    slot_num = np.zeros(row.shape[0], np.int64)
    counts = np.zeros((tile_count, tile_count), np.int64)
    for e in np.flatnonzero(away):
        slot_num[e] = counts[source_dev[e], dest_dev[e]]
        counts[source_dev[e], dest_dev[e]] += 1
    send_row = np.zeros((tile_count, tile_count, int(counts.max())), np.int32)
    send_row[source_dev[away], dest_dev[away], slot_num[away]] = row[away]
    place = np.where(away, slot_num, row)
    recv_dev = source_dev.reshape(tile_count, per_dev, 4).astype(np.int32)
    recv_slot = place.reshape(tile_count, per_dev, 4).astype(np.int32)
    return (send_row, None, recv_dev, recv_slot)


MESH = pl.DeviceIdType.MESH
LANES = 128


def edge_plan(neighbour, rim_side, patches):
    blocks = neighbour.shape[0] // patches
    near = neighbour.reshape(blocks, patches, 4) // patches
    home = near == np.arange(blocks)[:, None, None]
    inner = [[None] * patches for _ in range(4)]
    outer = [[] for _ in range(4)]
    for p in range(patches):
        for k in range(4):
            local = neighbour.reshape(blocks, patches, 4)[:, p, k] % patches
            same = home[:, p, k].all() and (local == local[0]).all()
            facing = (rim_side.reshape(blocks, patches, 4)[:, p, k] == (k ^ 1)).all()
            if same and facing:
                inner[k][p] = int(local[0])
            else:
                assert not home[:, p, k].any()
                outer[k].append(p)
    for k in (2, 3):
        assert outer[k] == list(range(outer[k][0], outer[k][-1] + 1))
    return inner, outer


def joined(ref, span):
    return jnp.concatenate([ref[b, span, :] for b in range(ref.shape[0])], axis=1)


def split_store(ref, span, value):
    for b in range(ref.shape[0]):
        ref[b, span, :] = value[:, b * LANES:(b + 1) * LANES]


def window_kernel(
    tiles, sections, patches, micro, slots, inner, outer,
    placement, table,
    states, weights, skip_w, biases,
    out,
    held, skip_held, bias_held, bias_own, stage, finished, hidden, summed, padded, rims,
    outgoing, received_a, received_b, behind, send_rows, edge_by, edge_slot,
    halo_send, halo_recv, weight_send, weight_recv, own_sem, out_send, out_recv, ready,
    relay_send, relay_recv, pass_send, pass_recv,
):
    tile = lax.axis_index("tile")
    section = lax.axis_index("section")
    half = sections // 2
    side = states.shape[2]
    chan = states.shape[4]
    rows = stage.shape[2]
    whole = rows // side
    received = (received_a, received_b)
    edges = [(p, k) for k in range(4) for p in outer[k]]
    first_edge = [sum(len(outer[j]) for j in range(k)) for k in range(4)]

    def tile_at(by):
        return lax.rem(tile + by, tiles)

    partner = tile + 1 - 2 * lax.rem(tile, 2)
    barrier = pltpu.get_barrier_semaphore()
    for by in range(1, tiles):
        pl.semaphore_signal(barrier, inc=1, device_id={"tile": tile_at(by)}, device_id_type=MESH)
    for by in range(1, sections):
        pl.semaphore_signal(
            barrier, inc=1, device_id={"section": lax.rem(section + by, sections)}, device_id_type=MESH
        )
        pl.semaphore_signal(
            barrier, inc=1, device_id={"tile": partner, "section": lax.rem(section + by, sections)},
            device_id_type=MESH,
        )

    bias_own[...] = jnp.zeros_like(bias_own)
    bias_own[0:LAYERS, :] = biases[0].astype(jnp.float32)

    group = sections // micro
    works = lax.rem(section, group) == 0
    mine = section // group
    my_block = placement[tile]
    count = len(edges)
    sources = tiles * tiles * slots
    places = sources + tiles * count

    def find(block, _):
        def one(by, found):
            here = placement[lax.rem(tile - by + tiles, tiles)]
            return jnp.where(here == block, by, found)

        behind[block] = lax.fori_loop(0, tiles, one, jnp.int32(0))
        return 0

    lax.fori_loop(0, tiles, find, 0)

    def route(e, _):
        edge_by[e] = behind[table[sources + my_block * count + e]] - 1
        edge_slot[e] = table[places + my_block * count + e]
        return 0

    lax.fori_loop(0, count, route, 0)

    def fill(i, _):
        base = (my_block * tiles + placement[tile_at(i // slots + 1)]) * slots
        send_rows[i] = table[base + lax.rem(i, slots)]
        return 0

    lax.fori_loop(0, (tiles - 1) * slots, fill, 0)

    pl.semaphore_wait(barrier, tiles - 1 + 2 * (sections - 1))

    column = lax.broadcasted_iota(jnp.int32, (whole, 8, chan), 1)
    first = column == 0
    last = column == 7

    def halo_copy(layer, by):
        return pltpu.make_async_remote_copy(
            src_ref=outgoing.at[layer, by - 1],
            dst_ref=received[layer].at[by - 1],
            send_sem=halo_send.at[layer, by - 1],
            recv_sem=halo_recv.at[layer, by - 1],
            device_id={"tile": tile_at(by)},
            device_id_type=MESH,
        )

    pieces = (
        (weights.at[0], held, 0), (weights.at[1], held, 1), (skip_w.at[0], skip_held, None), (bias_own, bias_held, None)
    )

    def weight_copy(piece, source, worker):
        src, dst, layer = pieces[piece]
        return pltpu.make_async_remote_copy(
            src_ref=src,
            dst_ref=dst.at[source] if layer is None else dst.at[source, layer],
            send_sem=weight_send.at[worker, piece],
            recv_sem=weight_recv.at[source, piece],
            device_id={"section": worker * group},
            device_id_type=MESH,
        )

    def own_copy(piece):
        src, dst, layer = pieces[piece]
        return pltpu.make_async_copy(
            src, dst.at[section] if layer is None else dst.at[section, layer], own_sem.at[piece]
        )

    def out_copy(m, sec):
        return pltpu.make_async_remote_copy(
            src_ref=finished.at[sec], dst_ref=out.at[0, m],
            send_sem=out_send.at[sec], recv_sem=out_recv.at[m],
            device_id={"section": sec}, device_id_type=MESH,
        )

    def need(piece, sec):
        @pl.when(sec == section)
        def _():
            own_copy(piece).wait()

        near = sec // group == mine

        @pl.when((sec != section) & (near if piece < 2 else True))
        def _():
            weight_copy(piece, sec, 0).wait_recv()

        if piece < 2:
            @pl.when(jnp.logical_not(near))
            def _():
                for hop in range(2):
                    pass_copy(piece, sec, hop, hop).wait_recv()

    deep = 3 * chan // 2

    def part(other):
        which = lax.rem(tile + other, 2)
        return pl.ds(pl.multiple_of(which * deep, LANES), deep)

    def relay_copy(layer, source, worker):
        return pltpu.make_async_remote_copy(
            src_ref=weights.at[layer, :, part(0)], dst_ref=held.at[source, layer, :, part(0)],
            send_sem=relay_send.at[worker, layer], recv_sem=relay_recv.at[source, layer],
            device_id={"section": worker * group + 1}, device_id_type=MESH,
        )

    def pass_copy(layer, source, hop, other):
        place = held.at[source, layer, :, part(other)]
        device = {"section": mine * group}
        if hop == 1:
            device["tile"] = partner
        return pltpu.make_async_remote_copy(
            src_ref=place, dst_ref=place,
            send_sem=pass_send.at[source, layer, hop], recv_sem=pass_recv.at[source, layer, hop],
            device_id=device, device_id_type=MESH,
        )

    def gelu(z):
        return 0.5 * z * (1.0 + lax.erf(z * np.float32(0.5 ** 0.5)))

    def rolled(values, by):
        return pltpu.roll(values.reshape(values.shape[0] // 8, 8, chan), by, 1)

    def strided(values):
        height = values.shape[0]
        lower = jnp.where(first[:height // 8], 0.0, rolled(values, 1)).reshape(height, chan)
        upper = jnp.where(last[:height // 8], 0.0, rolled(values, 7)).reshape(height, chan)
        return jnp.concatenate([lower, values, upper], axis=1)

    def picked(cells, chosen):
        blank = jnp.zeros((1,) + cells.shape[1:], cells.dtype)
        parts = [blank if q is None else cells[q:q + 1] for q in chosen]
        parts += [blank] * (whole - len(chosen))
        return jnp.concatenate(parts, axis=0)

    def shifted_row(values):
        lower, upper = rolled(values, 1), rolled(values, 7)
        lower = jnp.where(first, picked(lower, inner[0]), lower).reshape(rows, chan)
        upper = jnp.where(last, picked(upper, inner[1]), upper).reshape(rows, chan)
        return jnp.concatenate([lower, values, upper], axis=1).astype(jnp.bfloat16)

    def across_row(values, chosen):
        moved = strided(values).reshape(whole, 8, 3 * chan)
        return picked(moved, chosen).reshape(rows, 3 * chan).astype(jnp.bfloat16)

    def rim_span(p, k):
        if k < 2:
            return pl.ds(p * 8 + 7 * k, 8, stride=rows)
        top = (k - 2) * (side - 1) * rows
        return slice(top + p * 8, top + p * 8 + 8)

    def send_halo(layer):
        for by in range(1, tiles):
            for q in range(slots):
                outgoing[layer, by - 1, q] = rims[send_rows[(by - 1) * slots + q]]
            halo_copy(layer, by).start()

    def keep(sec):
        for r in range(side):
            values = joined(hidden, slice(r * rows, (r + 1) * rows)).astype(jnp.bfloat16)
            stage[half + sec, r] = values
            finished[sec, :, r] = values.reshape(whole, 8, chan)[:patches]

        @pl.when(sec == section)
        def _():
            out[0, mine] = finished[sec]

        @pl.when(sec != section)
        def _():
            out_copy(mine, sec).start()

    def run_layer(sec, layer):
        send_halo(layer)
        if layer == 0:
            @pl.when(sec > 0)
            def _():
                keep(sec - 1)
                for by in range(1, tiles):
                    halo_copy(LAYERS - 1, by).wait_send()
        else:
            for by in range(1, tiles):
                halo_copy(layer - 1, by).wait_send()

        for r in range(side):
            values = joined(hidden, slice(r * rows, (r + 1) * rows))
            padded[r + 1] = shifted_row(values)
            if r == 0:
                padded[side + 1] = across_row(values, inner[3])
            if r == side - 1:
                padded[0] = across_row(values, inner[2])

        step = 2
        if layer == 0:
            need(3, sec)
            need(2, sec)
        need(layer, sec)

        @pl.loop(0, side // step)
        def _(part):
            r = part * step
            total = jnp.broadcast_to(bias_held[sec, layer:layer + 1, :], (step * rows, chan))
            for i in range(3):
                total += jnp.dot(
                    padded[pl.ds(r + i, step)].reshape(step * rows, 3 * chan),
                    held[sec, layer, i],
                    preferred_element_type=jnp.float32,
                )
            if layer == 0:
                total += jnp.dot(
                    stage[sec, pl.ds(r, step)].reshape(step * rows, chan),
                    skip_held[sec],
                    preferred_element_type=jnp.float32,
                )
            span = pl.ds(pl.multiple_of(r * rows, 8), step * rows)
            split_store(summed, span, total)
            split_store(hidden, span, gelu(total))

        for by in range(1, tiles):
            halo_copy(layer, by).wait_recv()

        def strips(k):
            parts = []
            for n in range(len(outer[k])):
                e = first_edge[k] + n
                parts.append(received[layer][edge_by[e], edge_slot[e]].astype(jnp.float32))
            return strided(jnp.concatenate(parts, axis=0)).astype(jnp.bfloat16)

        for k in (0, 1):
            moved = strips(k)
            added = jnp.zeros((len(outer[k]) * 8, chan), jnp.float32)
            for i in range(3):
                added += jnp.dot(
                    moved[:, i * chan:(i + 1) * chan],
                    held[sec, layer, i, k * 2 * chan:(k * 2 + 1) * chan],
                    preferred_element_type=jnp.float32,
                )
            for n, p in enumerate(outer[k]):
                for b in range(chan // LANES):
                    summed[b, rim_span(p, k), :] += added[n * 8:n * 8 + 8, b * LANES:(b + 1) * LANES]
        for k in (2, 3):
            added = jnp.dot(strips(k), held[sec, layer, k * 2 - 4], preferred_element_type=jnp.float32)
            top = (k - 2) * (side - 1) * rows
            span = slice(top + outer[k][0] * 8, top + outer[k][-1] * 8 + 8)
            total = joined(summed, span) + added
            split_store(summed, span, total)
            fresh = gelu(total)
            split_store(hidden, span, fresh)
            for n in range(len(outer[k])):
                rims[first_edge[k] + n] = fresh[n * 8:n * 8 + 8].astype(jnp.bfloat16)
        for k in (0, 1):
            for n, p in enumerate(outer[k]):
                fresh = gelu(joined(summed, rim_span(p, k)))
                split_store(hidden, rim_span(p, k), fresh)
                rims[first_edge[k] + n] = fresh.astype(jnp.bfloat16)

    def send_weights(worker, which):
        for piece in which:
            weight_copy(piece, section, worker).start()

    @pl.when(works)
    def _():
        for piece in (3, 2, 0, 1):
            own_copy(piece).start()

    for worker in range(micro):
        @pl.when(section != worker * group)
        def _():
            send_weights(worker, (3, 2))

        @pl.when((section != worker * group) & (mine == worker))
        def _():
            send_weights(worker, (0, 1))

        @pl.when(works & (mine != worker))
        def _():
            for layer in range(LAYERS):
                relay_copy(layer, section, worker).start()

    relays = lax.rem(section, group) == 1

    def pass_on(source):
        for layer in range(LAYERS):
            relay_copy(layer, source, 0).wait_recv()
            for hop in range(2):
                pass_copy(layer, source, hop, 0).start()

    for rank in range(group):
        for worker in range(micro):
            source = worker * group + rank

            @pl.when(relays & (mine != worker))
            def _():
                pass_on(source)

        if rank + 1 < group:
            for worker in range(micro):
                @pl.when(relays & (mine != worker))
                def _():
                    pl.semaphore_signal(
                        ready.at[mine], inc=1, device_id={"section": worker * group + rank + 1},
                        device_id_type=MESH,
                    )

            for worker in range(micro):
                @pl.when((lax.rem(section, group) == rank + 1) & (mine != worker))
                def _():
                    pl.semaphore_wait(ready.at[worker], 1)
                    for layer in range(LAYERS):
                        relay_copy(layer, section, worker).start()

    @pl.when(works)
    def _():
        for r in range(side):
            values = states[mine, :, r].astype(jnp.float32)
            if whole != patches:
                values = jnp.concatenate([values, jnp.zeros((whole - patches, 8, chan), jnp.float32)], axis=0)
            values = values.reshape(rows, chan)
            split_store(hidden, slice(r * rows, (r + 1) * rows), values)
            for i in range(half):
                stage[i, r] = values.astype(jnp.bfloat16)
        for e, (p, k) in enumerate(edges):
            rims[e] = joined(hidden, rim_span(p, k)).astype(jnp.bfloat16)

        @pl.loop(0, sections)
        def _(sec):
            for layer in range(LAYERS):
                run_layer(sec, layer)

        keep(sections - 1)
        for by in range(1, tiles):
            halo_copy(LAYERS - 1, by).wait_send()

        @pl.loop(0, sections)
        def _(sec):
            @pl.when(sec != section)
            def _():
                out_copy(mine, sec).wait_send()

    for worker in range(micro):
        @pl.when(section != worker * group)
        def _():
            for piece in (2, 3):
                weight_copy(piece, section, worker).wait_send()
            out_copy(worker, section).wait_recv()

        @pl.when((section != worker * group) & (mine == worker))
        def _():
            for piece in (0, 1):
                weight_copy(piece, section, worker).wait_send()

        @pl.when(mine != worker)
        def _():
            for layer in range(LAYERS):
                relay_copy(layer, section, worker).wait_send()

        @pl.when(relays & (mine != worker))
        def _():
            for rank in range(group):
                for layer in range(LAYERS):
                    for hop in range(2):
                        pass_copy(layer, worker * group + rank, hop, 0).wait_send()


def on_device(states, conv_weight, skip_weight, bias, placement):
    sections = lax.axis_size("section")
    tiles = lax.axis_size("tile")
    micro, patches, side, _, chan = states.shape
    neighbour, rim_side, flip_flag = seam_tables(PR)
    assert not flip_flag.any()
    inner, outer = edge_plan(neighbour, rim_side, patches)
    edges = [(p, k) for k in range(4) for p in outer[k]]
    send_row, _, recv_dev, recv_slot = off_device_routes(neighbour, rim_side, flip_flag, tiles, patches)
    slots = send_row.shape[2]
    number = np.zeros(patches * 4, np.int32)
    for e, (p, k) in enumerate(edges):
        number[p * 4 + k] = e
    take = [p * 4 + k for p, k in edges]
    whole = patches + patches % 2
    rows = whole * side
    table = np.concatenate([
        number[send_row].reshape(-1),
        recv_dev.reshape(tiles, -1)[:, take].reshape(-1),
        recv_slot.reshape(tiles, -1)[:, take].reshape(-1),
    ])
    weights = conv_weight[0].reshape(LAYERS, 3, 3 * chan, chan)
    held = sections + sections // 2
    smem = pl.BlockSpec(memory_space=pltpu.SMEM)
    vmem = pl.BlockSpec(memory_space=pltpu.VMEM)
    wide = pltpu.VMEM((chan // LANES, side * rows, LANES), jnp.float32)
    got = pltpu.VMEM((tiles - 1, slots, side, chan), jnp.bfloat16)
    flops = 2 * micro * side * rows * chan * chan * (9 * LAYERS + 1)
    return pl.pallas_call(
        functools.partial(window_kernel, tiles, sections, patches, micro, slots, inner, outer),
        out_shape=jax.ShapeDtypeStruct((1,) + states.shape, jnp.bfloat16),
        in_specs=[smem] * 2 + [vmem, pl.BlockSpec(memory_space=pl.ANY), vmem, vmem],
        out_specs=vmem,
        scratch_shapes=[
            pltpu.VMEM((sections,) + weights.shape, jnp.bfloat16),
            pltpu.VMEM((sections, chan, chan), jnp.bfloat16),
            pltpu.VMEM((sections, 8, chan), jnp.float32),
            pltpu.VMEM((8, chan), jnp.float32),
            pltpu.VMEM((held, side, rows, chan), jnp.bfloat16),
            pltpu.VMEM((sections,) + states.shape[1:], jnp.bfloat16),
            wide, wide,
            pltpu.VMEM((side + 2, rows, 3 * chan), jnp.bfloat16),
            pltpu.VMEM((len(edges), side, chan), jnp.bfloat16),
            pltpu.VMEM((2, tiles - 1, slots, side, chan), jnp.bfloat16),
            got, got,
            pltpu.SMEM((tiles,), jnp.int32),
            pltpu.SMEM(((tiles - 1) * slots,), jnp.int32),
            pltpu.SMEM((len(edges),), jnp.int32),
            pltpu.SMEM((len(edges),), jnp.int32),
            pltpu.SemaphoreType.DMA((2, tiles - 1)),
            pltpu.SemaphoreType.DMA((2, tiles - 1)),
            pltpu.SemaphoreType.DMA((micro, 4)),
            pltpu.SemaphoreType.DMA((sections, 4)),
            pltpu.SemaphoreType.DMA((4,)),
            pltpu.SemaphoreType.DMA((sections,)),
            pltpu.SemaphoreType.DMA((micro,)),
            pltpu.SemaphoreType.REGULAR((micro,)),
            pltpu.SemaphoreType.DMA((micro, LAYERS)),
            pltpu.SemaphoreType.DMA((sections, LAYERS)),
            pltpu.SemaphoreType.DMA((sections, LAYERS, 2)),
            pltpu.SemaphoreType.DMA((sections, LAYERS, 2)),
        ],
        compiler_params=pltpu.CompilerParams(
            collective_id=0, has_side_effects=True, vmem_limit_bytes=56 * 1024 * 1024
        ),
        cost_estimate=pl.CostEstimate(flops=flops, bytes_accessed=2**24, transcendentals=0),
    )(
        placement, jnp.asarray(table, jnp.int32),
        states, weights, skip_weight, bias,
    )


def solution(mesh):
    in_specs = (
        P(None, "tile", None, None, None),
        P("section", None, None, None, None, None),
        P("section", None, None),
        P("section", None, None),
        P(),
    )
    out_specs = P("section", None, "tile", None, None, None)
    return jax.shard_map(
        on_device, mesh=mesh, in_specs=in_specs, out_specs=out_specs, check_vma=False
    )
```

```python
import functools

import jax
import jax.numpy as jnp
import numpy as np
from jax import lax
from jax.experimental import pallas as pl
from jax.experimental.pallas import tpu as pltpu
from jax.sharding import PartitionSpec as P

LAYERS = 2
PR = 4


def face_across(face_num, direction):
    cycle = face_num // 4
    column = face_num % 4
    if cycle == 0:
        table = [4 + column, 4 + (column + 1) % 4, (column + 1) % 4, (column + 3) % 4]
    elif cycle == 1:
        table = [8 + (column + 3) % 4, 8 + column, column, (column + 3) % 4]
    else:
        table = [8 + (column + 3) % 4, 8 + (column + 1) % 4, 4 + (column + 1) % 4, 4 + column]
    return table[direction]


def locate(face_num, coord_x, coord_y, face_span):
    if 0 <= coord_x < face_span and 0 <= coord_y < face_span:
        return (face_num, coord_x, coord_y)
    if coord_x < 0:
        direction = 0
    elif coord_y < 0:
        direction = 1
    elif coord_x >= face_span:
        direction = 2
    else:
        direction = 3
    cycle = face_num // 4
    target = face_across(face_num, direction)
    coord_x = coord_x % face_span
    coord_y = coord_y % face_span
    if cycle == 0 and direction == 2 or (cycle == 2 and direction == 0):
        coord_x, coord_y = (coord_y, face_span - 1 - coord_x)
    elif cycle == 0 and direction == 3 or (cycle == 2 and direction == 1):
        coord_x, coord_y = (face_span - 1 - coord_y, coord_x)
    return (target, coord_x, coord_y)


def seam_tables(tiles):
    cell_side = 2
    face_span = tiles * cell_side
    face_tiles = tiles * tiles
    total = 12 * face_tiles
    neighbour = np.zeros((total, 4), np.int32)
    rim_side = np.zeros((total, 4), np.int32)
    flip_flag = np.zeros((total, 4), np.int32)
    for patch_num in range(total):
        cycle = patch_num % 3
        rest = patch_num // 3
        column = rest // face_tiles
        tile_y = rest % face_tiles // tiles
        tile_x = rest % tiles
        face_num = 4 * cycle + column
        base_x = tile_x * cell_side
        base_y = tile_y * cell_side
        for side_num in range(4):
            found = []
            for step_num in range(2):
                if side_num == 0:
                    point = (base_x - 1, base_y + step_num)
                elif side_num == 1:
                    point = (base_x + cell_side, base_y + step_num)
                elif side_num == 2:
                    point = (base_x + step_num, base_y - 1)
                else:
                    point = (base_x + step_num, base_y + cell_side)
                found.append(locate(face_num, point[0], point[1], face_span))
            face_a, first_x, first_y = found[0]
            face_b, second_x, second_y = found[1]
            neighbour[patch_num, side_num] = (
                3 * (face_a % 4 * face_tiles + first_y // cell_side * tiles + first_x // cell_side)
                + face_a // 4
            )
            if first_x == second_x:
                rim_side[patch_num, side_num] = 0 if first_x % cell_side == 0 else 1
                flip_flag[patch_num, side_num] = 1 if second_y < first_y else 0
            else:
                rim_side[patch_num, side_num] = 2 if first_y % cell_side == 0 else 3
                flip_flag[patch_num, side_num] = 1 if second_x < first_x else 0
    return (neighbour, rim_side, flip_flag)


def off_device_routes(neighbour, rim_side, flip_flag, tile_count, per_dev):
    source_dev = (neighbour // per_dev).reshape(-1)
    dest_dev = np.repeat(np.arange(neighbour.shape[0]) // per_dev, 4)
    row = (neighbour % per_dev * 4 + rim_side).reshape(-1)
    away = source_dev != dest_dev
    slot_num = np.zeros(row.shape[0], np.int64)
    counts = np.zeros((tile_count, tile_count), np.int64)
    for e in np.flatnonzero(away):
        slot_num[e] = counts[source_dev[e], dest_dev[e]]
        counts[source_dev[e], dest_dev[e]] += 1
    send_row = np.zeros((tile_count, tile_count, int(counts.max())), np.int32)
    send_row[source_dev[away], dest_dev[away], slot_num[away]] = row[away]
    place = np.where(away, slot_num, row)
    recv_dev = source_dev.reshape(tile_count, per_dev, 4).astype(np.int32)
    recv_slot = place.reshape(tile_count, per_dev, 4).astype(np.int32)
    return (send_row, None, recv_dev, recv_slot)


MESH = pl.DeviceIdType.MESH
LANES = 128


def edge_plan(neighbour, rim_side, patches):
    blocks = neighbour.shape[0] // patches
    near = neighbour.reshape(blocks, patches, 4) // patches
    home = near == np.arange(blocks)[:, None, None]
    inner = [[None] * patches for _ in range(4)]
    outer = [[] for _ in range(4)]
    for p in range(patches):
        for k in range(4):
            local = neighbour.reshape(blocks, patches, 4)[:, p, k] % patches
            same = home[:, p, k].all() and (local == local[0]).all()
            facing = (rim_side.reshape(blocks, patches, 4)[:, p, k] == (k ^ 1)).all()
            if same and facing:
                inner[k][p] = int(local[0])
            else:
                assert not home[:, p, k].any()
                outer[k].append(p)
    for k in (2, 3):
        assert outer[k] == list(range(outer[k][0], outer[k][-1] + 1))
    return inner, outer


def tail_plan(patches, side, outer):
    early, late = [], []
    for p in range(patches):
        low = 1 if p in outer[2] else 0
        high = side - 1 if p in outer[3] else side
        clean = p not in outer[0] and p not in outer[1]
        for spans, low_row, high_row in ((early if clean else late, low, high), (late, 0, low), (late, high, side)):
            if low_row < high_row:
                spans.append((p, p + 1, low_row, high_row))
    plans = []
    for spans in (early, late):
        merged = []
        for p, end, low, high in sorted(spans, key=lambda piece: (piece[2], piece[3], piece[0])):
            if merged and merged[-1][1] == p and merged[-1][2:] == (low, high):
                merged[-1] = (merged[-1][0], end, low, high)
            else:
                merged.append((p, end, low, high))
        plans.append(merged)
    return plans


def joined(ref, span):
    return jnp.concatenate([ref[b, span, :] for b in range(ref.shape[0])], axis=1)


def split_store(ref, span, value):
    for b in range(ref.shape[0]):
        ref[b, span, :] = value[:, b * LANES:(b + 1) * LANES]


def window_kernel(
    tiles, sections, patches, micro, slots, inner, outer, early, late,
    placement, table,
    states, weights, skip_w, biases,
    out,
    held, skip_held, bias_held, bias_own, stage, finished, hidden, summed, padded, rims,
    outgoing, received_a, received_b, behind, send_rows, edge_by, edge_slot,
    halo_send, halo_recv, weight_send, weight_recv, own_sem, out_send, out_recv, ready,
    relay_send, relay_recv, pass_send, pass_recv, tail_send, tail_recv,
):
    tile = lax.axis_index("tile")
    section = lax.axis_index("section")
    half = sections // 2
    side = states.shape[2]
    chan = states.shape[4]
    rows = stage.shape[2]
    whole = rows // side
    received = (received_a, received_b)
    edges = [(p, k) for k in range(4) for p in outer[k]]
    first_edge = [sum(len(outer[j]) for j in range(k)) for k in range(4)]

    def tile_at(by):
        return lax.rem(tile + by, tiles)

    partner = tile + 1 - 2 * lax.rem(tile, 2)
    barrier = pltpu.get_barrier_semaphore()
    for by in range(1, tiles):
        pl.semaphore_signal(barrier, inc=1, device_id={"tile": tile_at(by)}, device_id_type=MESH)
    for by in range(1, sections):
        pl.semaphore_signal(
            barrier, inc=1, device_id={"section": lax.rem(section + by, sections)}, device_id_type=MESH
        )
        pl.semaphore_signal(
            barrier, inc=1, device_id={"tile": partner, "section": lax.rem(section + by, sections)},
            device_id_type=MESH,
        )

    bias_own[...] = jnp.zeros_like(bias_own)
    bias_own[0:LAYERS, :] = biases[0].astype(jnp.float32)

    group = sections // micro
    assert group > 1
    works = lax.rem(section, group) == 0
    mine = section // group
    my_block = placement[tile]
    count = len(edges)
    sources = tiles * tiles * slots
    places = sources + tiles * count

    def find(block, _):
        def one(by, found):
            here = placement[lax.rem(tile - by + tiles, tiles)]
            return jnp.where(here == block, by, found)

        behind[block] = lax.fori_loop(0, tiles, one, jnp.int32(0))
        return 0

    lax.fori_loop(0, tiles, find, 0)

    def route(e, _):
        edge_by[e] = behind[table[sources + my_block * count + e]] - 1
        edge_slot[e] = table[places + my_block * count + e]
        return 0

    lax.fori_loop(0, count, route, 0)

    def fill(i, _):
        base = (my_block * tiles + placement[tile_at(i // slots + 1)]) * slots
        send_rows[i] = table[base + lax.rem(i, slots)]
        return 0

    lax.fori_loop(0, (tiles - 1) * slots, fill, 0)

    pl.semaphore_wait(barrier, tiles - 1 + 2 * (sections - 1))

    column = lax.broadcasted_iota(jnp.int32, (whole, 8, chan), 1)
    first = column == 0
    last = column == 7

    def halo_copy(layer, by):
        return pltpu.make_async_remote_copy(
            src_ref=outgoing.at[layer, by - 1],
            dst_ref=received[layer].at[by - 1],
            send_sem=halo_send.at[layer, by - 1],
            recv_sem=halo_recv.at[layer, by - 1],
            device_id={"tile": tile_at(by)},
            device_id_type=MESH,
        )

    pieces = (
        (weights.at[0], held, 0), (weights.at[1], held, 1), (skip_w.at[0], skip_held, None), (bias_own, bias_held, None)
    )

    def weight_copy(piece, source, worker):
        src, dst, layer = pieces[piece]
        return pltpu.make_async_remote_copy(
            src_ref=src,
            dst_ref=dst.at[source] if layer is None else dst.at[source, layer],
            send_sem=weight_send.at[worker, piece],
            recv_sem=weight_recv.at[source, piece],
            device_id={"section": worker * group},
            device_id_type=MESH,
        )

    def own_copy(piece):
        src, dst, layer = pieces[piece]
        return pltpu.make_async_copy(
            src, dst.at[section] if layer is None else dst.at[section, layer], own_sem.at[piece]
        )

    def out_copy(m, sec):
        return pltpu.make_async_remote_copy(
            src_ref=finished.at[sec], dst_ref=out.at[0, m],
            send_sem=out_send.at[sec], recv_sem=out_recv.at[m],
            device_id={"section": sec}, device_id_type=MESH,
        )

    def need(piece, sec):
        @pl.when(sec == section)
        def _():
            own_copy(piece).wait()

        near = sec // group == mine

        @pl.when((sec != section) & (near if piece < 2 else True))
        def _():
            weight_copy(piece, sec, 0).wait_recv()

        if piece < 2:
            @pl.when(jnp.logical_not(near))
            def _():
                for i in range(3):
                    for hop in range(2):
                        pass_copy(piece, i, sec, hop, hop).wait_recv()

    deep = 3 * chan // 2

    def part(other):
        which = lax.rem(tile + other, 2)
        return pl.ds(pl.multiple_of(which * deep, LANES), deep)

    def relay_copy(layer, i, source, worker):
        return pltpu.make_async_remote_copy(
            src_ref=weights.at[layer, i, part(0)], dst_ref=held.at[source, layer, i, part(0)],
            send_sem=relay_send.at[worker, layer, i], recv_sem=relay_recv.at[source, layer, i],
            device_id={"section": worker * group + 1}, device_id_type=MESH,
        )

    def pass_copy(layer, i, source, hop, other):
        place = held.at[source, layer, i, part(other)]
        device = {"section": mine * group}
        if hop == 1:
            device["tile"] = partner
        return pltpu.make_async_remote_copy(
            src_ref=place, dst_ref=place,
            send_sem=pass_send.at[source, layer, hop, i], recv_sem=pass_recv.at[source, layer, hop, i],
            device_id=device, device_id_type=MESH,
        )

    def gelu(z):
        return 0.5 * z * (1.0 + lax.erf(z * np.float32(0.5 ** 0.5)))

    def rolled(values, by):
        return pltpu.roll(values.reshape(values.shape[0] // 8, 8, chan), by, 1)

    def strided(values):
        height = values.shape[0]
        lower = jnp.where(first[:height // 8], 0.0, rolled(values, 1)).reshape(height, chan)
        upper = jnp.where(last[:height // 8], 0.0, rolled(values, 7)).reshape(height, chan)
        return jnp.concatenate([lower, values, upper], axis=1)

    def picked(cells, chosen):
        blank = jnp.zeros((1,) + cells.shape[1:], cells.dtype)
        parts = [blank if q is None else cells[q:q + 1] for q in chosen]
        parts += [blank] * (whole - len(chosen))
        return jnp.concatenate(parts, axis=0)

    def shifted_row(values):
        lower, upper = rolled(values, 1), rolled(values, 7)
        lower = jnp.where(first, picked(lower, inner[0]), lower).reshape(rows, chan)
        upper = jnp.where(last, picked(upper, inner[1]), upper).reshape(rows, chan)
        return jnp.concatenate([lower, values, upper], axis=1).astype(jnp.bfloat16)

    def across_row(values, chosen):
        moved = strided(values).reshape(whole, 8, 3 * chan)
        return picked(moved, chosen).reshape(rows, 3 * chan).astype(jnp.bfloat16)

    def rim_span(p, k):
        if k < 2:
            return pl.ds(p * 8 + 7 * k, 8, stride=rows)
        top = (k - 2) * (side - 1) * rows
        return slice(top + p * 8, top + p * 8 + 8)

    def send_halo(layer):
        for by in range(1, tiles):
            for q in range(slots):
                outgoing[layer, by - 1, q] = rims[send_rows[(by - 1) * slots + q]]
            halo_copy(layer, by).start()

    def keep(sec):
        for r in range(side):
            values = joined(hidden, slice(r * rows, (r + 1) * rows)).astype(jnp.bfloat16)
            stage[half + sec, r] = values
            finished[sec, :, r] = values.reshape(whole, 8, chan)[:patches]

        @pl.when(sec == section)
        def _():
            out[0, mine] = finished[sec]

        @pl.when(sec != section)
        def _():
            out_copy(mine, sec).start()

    def tail_copy(n, m):
        start, end, low, high = (early + late)[n]
        span = (slice(start, end), slice(low, high))
        return pltpu.make_async_remote_copy(
            src_ref=finished.at[(sections - 1,) + span], dst_ref=out.at[(0, m) + span],
            send_sem=tail_send.at[n], recv_sem=tail_recv.at[m, n],
            device_id={"section": sections - 1}, device_id_type=MESH,
        )

    def finish(which, begin):
        for start, end, low, high in which:
            for r in range(low, high):
                values = joined(hidden, slice(r * rows + start * 8, r * rows + end * 8))
                finished[sections - 1, start:end, r] = values.reshape(end - start, 8, chan).astype(jnp.bfloat16)
        for n in range(len(which)):
            tail_copy(begin + n, mine).start()

    def run_layer(sec, layer):
        send_halo(layer)
        if layer == 0:
            @pl.when(sec > 0)
            def _():
                keep(sec - 1)
                for by in range(1, tiles):
                    halo_copy(LAYERS - 1, by).wait_send()
        else:
            for by in range(1, tiles):
                halo_copy(layer - 1, by).wait_send()

        for r in range(side):
            values = joined(hidden, slice(r * rows, (r + 1) * rows))
            padded[r + 1] = shifted_row(values)
            if r == 0:
                padded[side + 1] = across_row(values, inner[3])
            if r == side - 1:
                padded[0] = across_row(values, inner[2])

        step = 2
        if layer == 0:
            need(3, sec)
            need(2, sec)
        need(layer, sec)

        @pl.loop(0, side // step)
        def _(part):
            r = part * step
            total = jnp.broadcast_to(bias_held[sec, layer:layer + 1, :], (step * rows, chan))
            for i in range(3):
                total += jnp.dot(
                    padded[pl.ds(r + i, step)].reshape(step * rows, 3 * chan),
                    held[sec, layer, i],
                    preferred_element_type=jnp.float32,
                )
            if layer == 0:
                total += jnp.dot(
                    stage[sec, pl.ds(r, step)].reshape(step * rows, chan),
                    skip_held[sec],
                    preferred_element_type=jnp.float32,
                )
            span = pl.ds(pl.multiple_of(r * rows, 8), step * rows)
            split_store(summed, span, total)
            split_store(hidden, span, gelu(total))

        if layer == LAYERS - 1:
            @pl.when(sec == sections - 1)
            def _():
                finish(early, 0)

        for by in range(1, tiles):
            halo_copy(layer, by).wait_recv()

        def strips(k):
            parts = []
            for n in range(len(outer[k])):
                e = first_edge[k] + n
                parts.append(received[layer][edge_by[e], edge_slot[e]].astype(jnp.float32))
            return strided(jnp.concatenate(parts, axis=0)).astype(jnp.bfloat16)

        for k in (0, 1):
            moved = strips(k)
            added = jnp.zeros((len(outer[k]) * 8, chan), jnp.float32)
            for i in range(3):
                added += jnp.dot(
                    moved[:, i * chan:(i + 1) * chan],
                    held[sec, layer, i, k * 2 * chan:(k * 2 + 1) * chan],
                    preferred_element_type=jnp.float32,
                )
            for n, p in enumerate(outer[k]):
                for b in range(chan // LANES):
                    summed[b, rim_span(p, k), :] += added[n * 8:n * 8 + 8, b * LANES:(b + 1) * LANES]
        for k in (2, 3):
            added = jnp.dot(strips(k), held[sec, layer, k * 2 - 4], preferred_element_type=jnp.float32)
            top = (k - 2) * (side - 1) * rows
            span = slice(top + outer[k][0] * 8, top + outer[k][-1] * 8 + 8)
            total = joined(summed, span) + added
            split_store(summed, span, total)
            fresh = gelu(total)
            split_store(hidden, span, fresh)
            for n in range(len(outer[k])):
                rims[first_edge[k] + n] = fresh[n * 8:n * 8 + 8].astype(jnp.bfloat16)
        for k in (0, 1):
            for n, p in enumerate(outer[k]):
                fresh = gelu(joined(summed, rim_span(p, k)))
                split_store(hidden, rim_span(p, k), fresh)
                rims[first_edge[k] + n] = fresh.astype(jnp.bfloat16)

    def send_weights(worker, which):
        for piece in which:
            weight_copy(piece, section, worker).start()

    @pl.when(works)
    def _():
        for piece in (3, 2, 0, 1):
            own_copy(piece).start()

    for worker in range(micro):
        @pl.when(section != worker * group)
        def _():
            send_weights(worker, (3, 2))

        @pl.when((section != worker * group) & (mine == worker))
        def _():
            send_weights(worker, (0, 1))

        @pl.when(works & (mine != worker))
        def _():
            for layer in range(LAYERS):
                for i in range(3):
                    relay_copy(layer, i, section, worker).start()

    relays = lax.rem(section, group) == 1

    def pass_on(source):
        for layer in range(LAYERS):
            for i in range(3):
                relay_copy(layer, i, source, 0).wait_recv()
                for hop in (1, 0):
                    pass_copy(layer, i, source, hop, 0).start()

    for rank in range(group):
        for worker in range(micro):
            source = worker * group + rank

            @pl.when(relays & (mine != worker))
            def _():
                pass_on(source)

        if rank + 1 < group:
            for worker in range(micro):
                @pl.when(relays & (mine != worker))
                def _():
                    pl.semaphore_signal(
                        ready.at[mine], inc=1, device_id={"section": worker * group + rank + 1},
                        device_id_type=MESH,
                    )

            for worker in range(micro):
                @pl.when((lax.rem(section, group) == rank + 1) & (mine != worker))
                def _():
                    pl.semaphore_wait(ready.at[worker], 1)
                    for layer in range(LAYERS):
                        for i in range(3):
                            relay_copy(layer, i, section, worker).start()

    @pl.when(works)
    def _():
        for r in range(side):
            values = states[mine, :, r].astype(jnp.float32)
            if whole != patches:
                values = jnp.concatenate([values, jnp.zeros((whole - patches, 8, chan), jnp.float32)], axis=0)
            values = values.reshape(rows, chan)
            split_store(hidden, slice(r * rows, (r + 1) * rows), values)
            for i in range(half):
                stage[i, r] = values.astype(jnp.bfloat16)
        for e, (p, k) in enumerate(edges):
            rims[e] = joined(hidden, rim_span(p, k)).astype(jnp.bfloat16)

        @pl.loop(0, sections)
        def _(sec):
            for layer in range(LAYERS):
                run_layer(sec, layer)

        finish(late, len(early))
        for by in range(1, tiles):
            halo_copy(LAYERS - 1, by).wait_send()

        @pl.loop(0, sections - 1)
        def _(sec):
            @pl.when(sec != section)
            def _():
                out_copy(mine, sec).wait_send()

        for n in range(len(early) + len(late)):
            tail_copy(n, mine).wait_send()

    for worker in range(micro):
        @pl.when(section != worker * group)
        def _():
            for piece in (2, 3):
                weight_copy(piece, section, worker).wait_send()

        @pl.when((section != worker * group) & (section != sections - 1))
        def _():
            out_copy(worker, section).wait_recv()

        @pl.when(section == sections - 1)
        def _():
            for n in range(len(early) + len(late)):
                tail_copy(n, worker).wait_recv()

        @pl.when((section != worker * group) & (mine == worker))
        def _():
            for piece in (0, 1):
                weight_copy(piece, section, worker).wait_send()

        @pl.when(mine != worker)
        def _():
            for layer in range(LAYERS):
                for i in range(3):
                    relay_copy(layer, i, section, worker).wait_send()

        @pl.when(relays & (mine != worker))
        def _():
            for rank in range(group):
                for layer in range(LAYERS):
                    for hop in range(2):
                        for i in range(3):
                            pass_copy(layer, i, worker * group + rank, hop, 0).wait_send()


def on_device(states, conv_weight, skip_weight, bias, placement):
    sections = lax.axis_size("section")
    tiles = lax.axis_size("tile")
    micro, patches, side, _, chan = states.shape
    neighbour, rim_side, flip_flag = seam_tables(PR)
    assert not flip_flag.any()
    inner, outer = edge_plan(neighbour, rim_side, patches)
    early, late = tail_plan(patches, side, outer)
    pieces = early + late
    edges = [(p, k) for k in range(4) for p in outer[k]]
    send_row, _, recv_dev, recv_slot = off_device_routes(neighbour, rim_side, flip_flag, tiles, patches)
    slots = send_row.shape[2]
    number = np.zeros(patches * 4, np.int32)
    for e, (p, k) in enumerate(edges):
        number[p * 4 + k] = e
    take = [p * 4 + k for p, k in edges]
    whole = patches + patches % 2
    rows = whole * side
    table = np.concatenate([
        number[send_row].reshape(-1),
        recv_dev.reshape(tiles, -1)[:, take].reshape(-1),
        recv_slot.reshape(tiles, -1)[:, take].reshape(-1),
    ])
    weights = conv_weight[0].reshape(LAYERS, 3, 3 * chan, chan)
    held = sections + sections // 2
    smem = pl.BlockSpec(memory_space=pltpu.SMEM)
    vmem = pl.BlockSpec(memory_space=pltpu.VMEM)
    wide = pltpu.VMEM((chan // LANES, side * rows, LANES), jnp.float32)
    got = pltpu.VMEM((tiles - 1, slots, side, chan), jnp.bfloat16)
    flops = 2 * micro * side * rows * chan * chan * (9 * LAYERS + 1)
    return pl.pallas_call(
        functools.partial(window_kernel, tiles, sections, patches, micro, slots, inner, outer, early, late),
        out_shape=pltpu.VMEM((1,) + states.shape, jnp.bfloat16),
        in_specs=[smem] * 2 + [vmem, pl.BlockSpec(memory_space=pl.ANY), vmem, vmem],
        out_specs=vmem,
        scratch_shapes=[
            pltpu.VMEM((sections,) + weights.shape, jnp.bfloat16),
            pltpu.VMEM((sections, chan, chan), jnp.bfloat16),
            pltpu.VMEM((sections, 8, chan), jnp.float32),
            pltpu.VMEM((8, chan), jnp.float32),
            pltpu.VMEM((held, side, rows, chan), jnp.bfloat16),
            pltpu.VMEM((sections,) + states.shape[1:], jnp.bfloat16),
            wide, wide,
            pltpu.VMEM((side + 2, rows, 3 * chan), jnp.bfloat16),
            pltpu.VMEM((len(edges), side, chan), jnp.bfloat16),
            pltpu.VMEM((2, tiles - 1, slots, side, chan), jnp.bfloat16),
            got, got,
            pltpu.SMEM((tiles,), jnp.int32),
            pltpu.SMEM(((tiles - 1) * slots,), jnp.int32),
            pltpu.SMEM((len(edges),), jnp.int32),
            pltpu.SMEM((len(edges),), jnp.int32),
            pltpu.SemaphoreType.DMA((2, tiles - 1)),
            pltpu.SemaphoreType.DMA((2, tiles - 1)),
            pltpu.SemaphoreType.DMA((micro, 4)),
            pltpu.SemaphoreType.DMA((sections, 4)),
            pltpu.SemaphoreType.DMA((4,)),
            pltpu.SemaphoreType.DMA((sections,)),
            pltpu.SemaphoreType.DMA((micro,)),
            pltpu.SemaphoreType.REGULAR((micro,)),
            pltpu.SemaphoreType.DMA((micro, LAYERS, 3)),
            pltpu.SemaphoreType.DMA((sections, LAYERS, 3)),
            pltpu.SemaphoreType.DMA((sections, LAYERS, 2, 3)),
            pltpu.SemaphoreType.DMA((sections, LAYERS, 2, 3)),
            pltpu.SemaphoreType.DMA((len(pieces),)),
            pltpu.SemaphoreType.DMA((micro, len(pieces))),
        ],
        compiler_params=pltpu.CompilerParams(
            collective_id=0, has_side_effects=True, vmem_limit_bytes=56 * 1024 * 1024
        ),
        cost_estimate=pl.CostEstimate(flops=flops, bytes_accessed=2**24, transcendentals=0),
    )(
        placement, jnp.asarray(table, jnp.int32),
        states, weights, skip_weight, bias,
    )


def solution(mesh):
    in_specs = (
        P(None, "tile", None, None, None),
        P("section", None, None, None, None, None),
        P("section", None, None),
        P("section", None, None),
        P(),
    )
    out_specs = P("section", None, "tile", None, None, None)
    return jax.shard_map(
        on_device, mesh=mesh, in_specs=in_specs, out_specs=out_specs, check_vma=False
    )
```

```python
import functools

import jax
import jax.numpy as jnp
import numpy as np
from jax import lax
from jax.experimental import pallas as pl
from jax.experimental.pallas import tpu as pltpu
from jax.sharding import PartitionSpec as P

LAYERS = 2
PR = 4


def face_across(face_num, direction):
    cycle = face_num // 4
    column = face_num % 4
    if cycle == 0:
        table = [4 + column, 4 + (column + 1) % 4, (column + 1) % 4, (column + 3) % 4]
    elif cycle == 1:
        table = [8 + (column + 3) % 4, 8 + column, column, (column + 3) % 4]
    else:
        table = [8 + (column + 3) % 4, 8 + (column + 1) % 4, 4 + (column + 1) % 4, 4 + column]
    return table[direction]


def locate(face_num, coord_x, coord_y, face_span):
    if 0 <= coord_x < face_span and 0 <= coord_y < face_span:
        return (face_num, coord_x, coord_y)
    if coord_x < 0:
        direction = 0
    elif coord_y < 0:
        direction = 1
    elif coord_x >= face_span:
        direction = 2
    else:
        direction = 3
    cycle = face_num // 4
    target = face_across(face_num, direction)
    coord_x = coord_x % face_span
    coord_y = coord_y % face_span
    if cycle == 0 and direction == 2 or (cycle == 2 and direction == 0):
        coord_x, coord_y = (coord_y, face_span - 1 - coord_x)
    elif cycle == 0 and direction == 3 or (cycle == 2 and direction == 1):
        coord_x, coord_y = (face_span - 1 - coord_y, coord_x)
    return (target, coord_x, coord_y)


def seam_tables(tiles):
    cell_side = 2
    face_span = tiles * cell_side
    face_tiles = tiles * tiles
    total = 12 * face_tiles
    neighbour = np.zeros((total, 4), np.int32)
    rim_side = np.zeros((total, 4), np.int32)
    flip_flag = np.zeros((total, 4), np.int32)
    for patch_num in range(total):
        cycle = patch_num % 3
        rest = patch_num // 3
        column = rest // face_tiles
        tile_y = rest % face_tiles // tiles
        tile_x = rest % tiles
        face_num = 4 * cycle + column
        base_x = tile_x * cell_side
        base_y = tile_y * cell_side
        for side_num in range(4):
            found = []
            for step_num in range(2):
                if side_num == 0:
                    point = (base_x - 1, base_y + step_num)
                elif side_num == 1:
                    point = (base_x + cell_side, base_y + step_num)
                elif side_num == 2:
                    point = (base_x + step_num, base_y - 1)
                else:
                    point = (base_x + step_num, base_y + cell_side)
                found.append(locate(face_num, point[0], point[1], face_span))
            face_a, first_x, first_y = found[0]
            face_b, second_x, second_y = found[1]
            neighbour[patch_num, side_num] = (
                3 * (face_a % 4 * face_tiles + first_y // cell_side * tiles + first_x // cell_side)
                + face_a // 4
            )
            if first_x == second_x:
                rim_side[patch_num, side_num] = 0 if first_x % cell_side == 0 else 1
                flip_flag[patch_num, side_num] = 1 if second_y < first_y else 0
            else:
                rim_side[patch_num, side_num] = 2 if first_y % cell_side == 0 else 3
                flip_flag[patch_num, side_num] = 1 if second_x < first_x else 0
    return (neighbour, rim_side, flip_flag)


def off_device_routes(neighbour, rim_side, flip_flag, tile_count, per_dev):
    source_dev = (neighbour // per_dev).reshape(-1)
    dest_dev = np.repeat(np.arange(neighbour.shape[0]) // per_dev, 4)
    row = (neighbour % per_dev * 4 + rim_side).reshape(-1)
    away = source_dev != dest_dev
    slot_num = np.zeros(row.shape[0], np.int64)
    counts = np.zeros((tile_count, tile_count), np.int64)
    for e in np.flatnonzero(away):
        slot_num[e] = counts[source_dev[e], dest_dev[e]]
        counts[source_dev[e], dest_dev[e]] += 1
    send_row = np.zeros((tile_count, tile_count, int(counts.max())), np.int32)
    send_row[source_dev[away], dest_dev[away], slot_num[away]] = row[away]
    place = np.where(away, slot_num, row)
    recv_dev = source_dev.reshape(tile_count, per_dev, 4).astype(np.int32)
    recv_slot = place.reshape(tile_count, per_dev, 4).astype(np.int32)
    return (send_row, None, recv_dev, recv_slot)


MESH = pl.DeviceIdType.MESH
LANES = 128


def edge_plan(neighbour, rim_side, patches):
    blocks = neighbour.shape[0] // patches
    near = neighbour.reshape(blocks, patches, 4) // patches
    home = near == np.arange(blocks)[:, None, None]
    inner = [[None] * patches for _ in range(4)]
    outer = [[] for _ in range(4)]
    for p in range(patches):
        for k in range(4):
            local = neighbour.reshape(blocks, patches, 4)[:, p, k] % patches
            same = home[:, p, k].all() and (local == local[0]).all()
            facing = (rim_side.reshape(blocks, patches, 4)[:, p, k] == (k ^ 1)).all()
            if same and facing:
                inner[k][p] = int(local[0])
            else:
                assert not home[:, p, k].any()
                outer[k].append(p)
    for k in (2, 3):
        assert outer[k] == list(range(outer[k][0], outer[k][-1] + 1))
    return inner, outer


def ghost_plan(neighbour, rim_side, patches, outer):
    blocks = neighbour.shape[0] // patches
    edges = [(p, k) for k in range(4) for p in outer[k]]
    number = {edge: e for e, edge in enumerate(edges)}
    facing = np.zeros((blocks, len(edges)), np.int32)
    sent = [[[] for _ in range(blocks)] for _ in range(blocks)]
    found = {}
    for b in range(blocks):
        for e, (p, k) in enumerate(edges):
            q, t = neighbour[b * patches + p, k], rim_side[b * patches + p, k]
            facing[b, e] = t
            for end in range(2):
                across = (2 if t < 2 else 0) + end
                if (q % patches, across) in number:
                    other, side = neighbour[q, across], rim_side[q, across]
                    home = other // patches
                    row = number[(other % patches, side)] * 8 + (0 if t in (0, 2) else 7)
                    found[(b, e, end)] = (home, len(sent[home][b]))
                    sent[home][b].append(row)
    corners = sorted({(e, end) for _, e, end in found})
    most = max(len(x) for line in sent for x in line)
    assert most <= 8
    send = np.zeros((blocks, blocks, most), np.int32)
    for a in range(blocks):
        for b in range(blocks):
            send[a, b, :len(sent[a][b])] = sent[a][b]
    home = np.full((blocks, len(corners)), -1, np.int32)
    place = np.zeros((blocks, len(corners)), np.int32)
    for n, (e, end) in enumerate(corners):
        for b in range(blocks):
            if (b, e, end) in found:
                home[b, n], place[b, n] = found[(b, e, end)]
    choices = [sorted(set(facing[:, e].tolist())) for e in range(len(edges))]
    assert all(len(c) <= 2 for c in choices)
    second = np.stack([(facing[:, e] != choices[e][0]).astype(np.int32) for e in range(len(edges))], axis=1)
    return corners, most, send, home, place, choices, second


def tail_plan(patches, side, outer):
    early, late = [], []
    for p in range(patches):
        low = 1 if p in outer[2] else 0
        high = side - 1 if p in outer[3] else side
        clean = p not in outer[0] and p not in outer[1]
        for spans, low_row, high_row in ((early if clean else late, low, high), (late, 0, low), (late, high, side)):
            if low_row < high_row:
                spans.append((p, p + 1, low_row, high_row))
    plans = []
    for spans in (early, late):
        merged = []
        for p, end, low, high in sorted(spans, key=lambda piece: (piece[2], piece[3], piece[0])):
            if merged and merged[-1][1] == p and merged[-1][2:] == (low, high):
                merged[-1] = (merged[-1][0], end, low, high)
            else:
                merged.append((p, end, low, high))
        plans.append(merged)
    return plans


def joined(ref, span):
    return jnp.concatenate([ref[b, span, :] for b in range(ref.shape[0])], axis=1)


def split_store(ref, span, value):
    for b in range(ref.shape[0]):
        ref[b, span, :] = value[:, b * LANES:(b + 1) * LANES]


def window_kernel(
    tiles, sections, patches, micro, slots, inner, outer, early, late, corners, most, choices, starts,
    placement, table,
    states, weights, skip_w, biases,
    out,
    held, skip_held, bias_held, bias_own, stage, finished, hidden, summed, padded, rims, partial, across, corner_rows,
    outgoing_0, outgoing_1, onward_0, onward_1, received_0, received_1, gotten_0, gotten_1,
    behind, send_rows, edge_by, edge_slot, corner_send, corner_place,
    halo_send, halo_recv, weight_send, weight_recv, own_sem, out_send, out_recv, ready,
    relay_send, relay_recv, pass_send, pass_recv, tail_send, tail_recv,
):
    tile = lax.axis_index("tile")
    section = lax.axis_index("section")
    half = sections // 2
    side = states.shape[2]
    chan = states.shape[4]
    rows = stage.shape[2]
    whole = rows // side
    outgoing, onward = (outgoing_0, outgoing_1), (onward_0, onward_1)
    received, gotten = (received_0, received_1), (gotten_0, gotten_1)
    edges = [(p, k) for k in range(4) for p in outer[k]]
    first_edge = [sum(len(outer[j]) for j in range(k)) for k in range(4)]

    def tile_at(by):
        return lax.rem(tile + by, tiles)

    partner = tile + 1 - 2 * lax.rem(tile, 2)
    barrier = pltpu.get_barrier_semaphore()
    for by in range(1, tiles):
        pl.semaphore_signal(barrier, inc=1, device_id={"tile": tile_at(by)}, device_id_type=MESH)
    for by in range(1, sections):
        pl.semaphore_signal(
            barrier, inc=1, device_id={"section": lax.rem(section + by, sections)}, device_id_type=MESH
        )
        pl.semaphore_signal(
            barrier, inc=1, device_id={"tile": partner, "section": lax.rem(section + by, sections)},
            device_id_type=MESH,
        )

    bias_own[...] = jnp.zeros_like(bias_own)
    bias_own[0:LAYERS, :] = biases[0].astype(jnp.float32)

    group = sections // micro
    assert group > 1 and sections % 2 == 0 and LAYERS == 2
    works = lax.rem(section, group) == 0
    mine = section // group
    my_block = placement[tile]
    count = len(edges)
    sends, sources, places, corner_sends, corner_homes, corner_places, seconds = starts

    def find(block, _):
        def one(by, found):
            here = placement[lax.rem(tile - by + tiles, tiles)]
            return jnp.where(here == block, by, found)

        behind[block] = lax.fori_loop(0, tiles, one, jnp.int32(0))
        return 0

    local_row = (tiles - 1) * 8
    blank_row = local_row + 8
    corner_rows[blank_row:blank_row + 8, :] = jnp.zeros((8, chan), jnp.float32)

    lax.fori_loop(0, tiles, find, 0)

    def route(e, _):
        edge_by[e] = behind[table[sources + my_block * count + e]] - 1
        edge_slot[e] = table[places + my_block * count + e]
        return 0

    lax.fori_loop(0, count, route, 0)

    def fill(i, _):
        other = placement[tile_at(i // slots + 1)]
        send_rows[i] = table[sends + (my_block * tiles + other) * slots + lax.rem(i, slots)]
        return 0

    lax.fori_loop(0, (tiles - 1) * slots, fill, 0)

    def fill_corner(i, _):
        other = placement[tile_at(i // most)]
        corner_send[i] = table[corner_sends + (my_block * tiles + other) * most + lax.rem(i, most)]
        return 0

    lax.fori_loop(0, tiles * most, fill_corner, 0)

    def place_corner(n, _):
        home = table[corner_homes + my_block * len(corners) + n]
        by = behind[jnp.maximum(home, 0)]
        row = table[corner_places + my_block * len(corners) + n]
        row += jnp.where(by == 0, local_row, (by - 1) * 8)
        corner_place[n] = jnp.where(home < 0, blank_row, row)
        return 0

    lax.fori_loop(0, len(corners), place_corner, 0)

    pl.semaphore_wait(barrier, tiles - 1 + 2 * (sections - 1))

    column = lax.broadcasted_iota(jnp.int32, (whole, 8, chan), 1)
    first = column == 0
    last = column == 7

    def halo_copy(wave, turn, by):
        source, target = ((outgoing, received), (onward, gotten))[wave]
        return pltpu.make_async_remote_copy(
            src_ref=source[turn].at[by - 1],
            dst_ref=target[turn].at[by - 1],
            send_sem=halo_send.at[turn, wave, by - 1],
            recv_sem=halo_recv.at[turn, wave, by - 1],
            device_id={"tile": tile_at(by)},
            device_id_type=MESH,
        )

    pieces = (
        (weights.at[0], held, 0), (weights.at[1], held, 1), (skip_w.at[0], skip_held, None), (bias_own, bias_held, None)
    )

    def weight_copy(piece, source, worker):
        src, dst, layer = pieces[piece]
        return pltpu.make_async_remote_copy(
            src_ref=src,
            dst_ref=dst.at[source] if layer is None else dst.at[source, layer],
            send_sem=weight_send.at[worker, piece],
            recv_sem=weight_recv.at[source, piece],
            device_id={"section": worker * group},
            device_id_type=MESH,
        )

    def own_copy(piece):
        src, dst, layer = pieces[piece]
        return pltpu.make_async_copy(
            src, dst.at[section] if layer is None else dst.at[section, layer], own_sem.at[piece]
        )

    def out_copy(m, sec):
        return pltpu.make_async_remote_copy(
            src_ref=finished.at[sec], dst_ref=out.at[0, m],
            send_sem=out_send.at[sec], recv_sem=out_recv.at[m],
            device_id={"section": sec}, device_id_type=MESH,
        )

    def need(piece, sec):
        @pl.when(sec == section)
        def _():
            own_copy(piece).wait()

        near = sec // group == mine

        @pl.when((sec != section) & (near if piece < 2 else True))
        def _():
            weight_copy(piece, sec, 0).wait_recv()

        if piece < 2:
            @pl.when(jnp.logical_not(near))
            def _():
                for i in range(3):
                    for hop in range(2):
                        pass_copy(piece, i, sec, hop, hop).wait_recv()

    deep = 3 * chan // 2

    def part(other):
        which = lax.rem(tile + other, 2)
        return pl.ds(pl.multiple_of(which * deep, LANES), deep)

    def relay_copy(layer, i, source, worker):
        return pltpu.make_async_remote_copy(
            src_ref=weights.at[layer, i, part(0)], dst_ref=held.at[source, layer, i, part(0)],
            send_sem=relay_send.at[worker, layer, i], recv_sem=relay_recv.at[source, layer, i],
            device_id={"section": worker * group + 1}, device_id_type=MESH,
        )

    def pass_copy(layer, i, source, hop, other):
        place = held.at[source, layer, i, part(other)]
        device = {"section": mine * group}
        if hop == 1:
            device["tile"] = partner
        return pltpu.make_async_remote_copy(
            src_ref=place, dst_ref=place,
            send_sem=pass_send.at[source, layer, hop, i], recv_sem=pass_recv.at[source, layer, hop, i],
            device_id=device, device_id_type=MESH,
        )

    def gelu(z):
        return 0.5 * z * (1.0 + lax.erf(z * np.float32(0.5 ** 0.5)))

    def rolled(values, by):
        return pltpu.roll(values.reshape(values.shape[0] // 8, 8, chan), by, 1)

    def strided(values):
        height = values.shape[0]
        lower = jnp.where(first[:height // 8], 0.0, rolled(values, 1)).reshape(height, chan)
        upper = jnp.where(last[:height // 8], 0.0, rolled(values, 7)).reshape(height, chan)
        return jnp.concatenate([lower, values, upper], axis=1)

    def picked(cells, chosen):
        blank = jnp.zeros((1,) + cells.shape[1:], cells.dtype)
        parts = [blank if q is None else cells[q:q + 1] for q in chosen]
        parts += [blank] * (whole - len(chosen))
        return jnp.concatenate(parts, axis=0)

    def shifted_row(values):
        lower, upper = rolled(values, 1), rolled(values, 7)
        lower = jnp.where(first, picked(lower, inner[0]), lower).reshape(rows, chan)
        upper = jnp.where(last, picked(upper, inner[1]), upper).reshape(rows, chan)
        return jnp.concatenate([lower, values, upper], axis=1).astype(jnp.bfloat16)

    def across_row(values, chosen):
        moved = strided(values).reshape(whole, 8, 3 * chan)
        return picked(moved, chosen).reshape(rows, 3 * chan).astype(jnp.bfloat16)

    def rim_span(p, k):
        if k < 2:
            return pl.ds(p * 8 + 7 * k, 8, stride=rows)
        top = (k - 2) * (side - 1) * rows
        return slice(top + p * 8, top + p * 8 + 8)

    def send_rims(turn):
        for by in range(1, tiles):
            for q in range(slots):
                outgoing[turn][by - 1, q] = rims[send_rows[(by - 1) * slots + q]]
            halo_copy(0, turn, by).start()

    def wait_sent(turn):
        for wave in range(2):
            for by in range(1, tiles):
                halo_copy(wave, turn, by).wait_send()

    def side_dot(values, sec, layer, k):
        moved = strided(values).astype(jnp.bfloat16)
        if k >= 2:
            return jnp.dot(moved, held[sec, layer, k * 2 - 4], preferred_element_type=jnp.float32)
        total = jnp.zeros((values.shape[0], chan), jnp.float32)
        for i in range(3):
            total += jnp.dot(
                moved[:, i * chan:(i + 1) * chan],
                held[sec, layer, i, k * 2 * chan:(k * 2 + 1) * chan],
                preferred_element_type=jnp.float32,
            )
        return total

    def cross_seams(sec):
        made = {}
        for t in range(4):
            chosen = [e for e in range(count) if t in choices[e]]
            if chosen:
                values = jnp.concatenate([rims[e].astype(jnp.float32) for e in chosen], axis=0)
                total = side_dot(values, sec, 0, t)
                for n, e in enumerate(chosen):
                    made[e, t] = total[n * 8:n * 8 + 8]
        for e in range(count):
            value = made[e, choices[e][0]]
            if len(choices[e]) > 1:
                value = jnp.where(table[seconds + my_block * count + e] != 0, made[e, choices[e][1]], value)
            across[e * 8:e * 8 + 8, :] = value

    place_in = lax.broadcasted_iota(jnp.int32, (8, chan), 0)

    def corner_block(other):
        block = jnp.zeros((8, chan), jnp.float32)
        for j in range(most):
            row = across[pl.ds(corner_send[other * most + j], 1), :]
            block = jnp.where(place_in == j, row, block)
        return block

    def send_partial(turn):
        for e, (p, k) in enumerate(edges):
            partial[e] = joined(summed, rim_span(p, k)).astype(jnp.bfloat16)
        for by in range(1, tiles):
            for q in range(slots):
                onward[turn][by - 1, q] = partial[send_rows[(by - 1) * slots + q]]
            onward[turn][by - 1, slots] = corner_block(by).astype(jnp.bfloat16)
            halo_copy(1, turn, by).start()

    def take_corners(turn):
        for by in range(1, tiles):
            corner_rows[(by - 1) * 8:by * 8, :] = gotten[turn][by - 1, slots].astype(jnp.float32)
        corner_rows[local_row:local_row + 8, :] = corner_block(0)

    def ghost(turn, e):
        z = gotten[turn][edge_by[e], edge_slot[e]].astype(jnp.float32) + across[e * 8:e * 8 + 8, :]
        for end in range(2):
            if (e, end) in corners:
                row = corner_rows[pl.ds(corner_place[corners.index((e, end))], 1), :]
                z += jnp.where(place_in == 7 * end, row, 0.0)
        return gelu(z)

    def keep(sec):
        for r in range(side):
            values = joined(hidden, slice(r * rows, (r + 1) * rows)).astype(jnp.bfloat16)
            stage[half + sec, r] = values
            finished[sec, :, r] = values.reshape(whole, 8, chan)[:patches]

        @pl.when(sec == section)
        def _():
            out[0, mine] = finished[sec]

        @pl.when(sec != section)
        def _():
            out_copy(mine, sec).start()

    def tail_copy(n, m):
        start, end, low, high = (early + late)[n]
        span = (slice(start, end), slice(low, high))
        return pltpu.make_async_remote_copy(
            src_ref=finished.at[(sections - 1,) + span], dst_ref=out.at[(0, m) + span],
            send_sem=tail_send.at[n], recv_sem=tail_recv.at[m, n],
            device_id={"section": sections - 1}, device_id_type=MESH,
        )

    def finish(which, begin):
        for start, end, low, high in which:
            for r in range(low, high):
                values = joined(hidden, slice(r * rows + start * 8, r * rows + end * 8))
                finished[sections - 1, start:end, r] = values.reshape(end - start, 8, chan).astype(jnp.bfloat16)
        for n in range(len(which)):
            tail_copy(begin + n, mine).start()

    def interior(sec, layer):
        for r in range(side):
            values = joined(hidden, slice(r * rows, (r + 1) * rows))
            padded[r + 1] = shifted_row(values)
            if r == 0:
                padded[side + 1] = across_row(values, inner[3])
            if r == side - 1:
                padded[0] = across_row(values, inner[2])

        step = 2
        if layer == 0:
            need(3, sec)
            need(2, sec)
        need(layer, sec)

        @pl.loop(0, side // step)
        def _(part):
            r = part * step
            total = jnp.broadcast_to(bias_held[sec, layer:layer + 1, :], (step * rows, chan))
            for i in range(3):
                total += jnp.dot(
                    padded[pl.ds(r + i, step)].reshape(step * rows, 3 * chan),
                    held[sec, layer, i],
                    preferred_element_type=jnp.float32,
                )
            if layer == 0:
                total += jnp.dot(
                    stage[sec, pl.ds(r, step)].reshape(step * rows, chan),
                    skip_held[sec],
                    preferred_element_type=jnp.float32,
                )
            span = pl.ds(pl.multiple_of(r * rows, 8), step * rows)
            split_store(summed, span, total)
            split_store(hidden, span, gelu(total))

    def add_strips(sec, layer, strip):
        for k in (0, 1):
            values = [strip(first_edge[k] + n) for n in range(len(outer[k]))]
            added = side_dot(jnp.concatenate(values, axis=0), sec, layer, k)
            for n, p in enumerate(outer[k]):
                for b in range(chan // LANES):
                    summed[b, rim_span(p, k), :] += added[n * 8:n * 8 + 8, b * LANES:(b + 1) * LANES]
        for k in (2, 3):
            values = [strip(first_edge[k] + n) for n in range(len(outer[k]))]
            added = side_dot(jnp.concatenate(values, axis=0), sec, layer, k)
            top = (k - 2) * (side - 1) * rows
            span = slice(top + outer[k][0] * 8, top + outer[k][-1] * 8 + 8)
            total = joined(summed, span) + added
            split_store(summed, span, total)
            fresh = gelu(total)
            split_store(hidden, span, fresh)
            if layer == LAYERS - 1:
                for n in range(len(outer[k])):
                    rims[first_edge[k] + n] = fresh[n * 8:n * 8 + 8].astype(jnp.bfloat16)
        for k in (0, 1):
            for n, p in enumerate(outer[k]):
                fresh = gelu(joined(summed, rim_span(p, k)))
                split_store(hidden, rim_span(p, k), fresh)
                if layer == LAYERS - 1:
                    rims[first_edge[k] + n] = fresh.astype(jnp.bfloat16)

    def run_section(sec, turn):
        send_rims(turn)

        @pl.when(sec > 0)
        def _():
            keep(sec - 1)
            wait_sent(1 - turn)

        interior(sec, 0)
        cross_seams(sec)
        send_partial(turn)

        for by in range(1, tiles):
            halo_copy(0, turn, by).wait_recv()
        add_strips(sec, 0, lambda e: received[turn][edge_by[e], edge_slot[e]].astype(jnp.float32))

        interior(sec, 1)

        if turn == 1:
            @pl.when(sec == sections - 1)
            def _():
                finish(early, 0)

        for by in range(1, tiles):
            halo_copy(1, turn, by).wait_recv()
        take_corners(turn)
        add_strips(sec, 1, lambda e: ghost(turn, e))

    def send_weights(worker, which):
        for piece in which:
            weight_copy(piece, section, worker).start()

    @pl.when(works)
    def _():
        for piece in (3, 2, 0, 1):
            own_copy(piece).start()

    for worker in range(micro):
        @pl.when(section != worker * group)
        def _():
            send_weights(worker, (3, 2))

        @pl.when((section != worker * group) & (mine == worker))
        def _():
            send_weights(worker, (0, 1))

        @pl.when(works & (mine != worker))
        def _():
            for layer in range(LAYERS):
                for i in range(3):
                    relay_copy(layer, i, section, worker).start()

    relays = lax.rem(section, group) == 1

    def pass_on(source):
        for layer in range(LAYERS):
            for i in range(3):
                relay_copy(layer, i, source, 0).wait_recv()
                for hop in (1, 0):
                    pass_copy(layer, i, source, hop, 0).start()

    for rank in range(group):
        for worker in range(micro):
            source = worker * group + rank

            @pl.when(relays & (mine != worker))
            def _():
                pass_on(source)

        if rank + 1 < group:
            for worker in range(micro):
                @pl.when(relays & (mine != worker))
                def _():
                    pl.semaphore_signal(
                        ready.at[mine], inc=1, device_id={"section": worker * group + rank + 1},
                        device_id_type=MESH,
                    )

            for worker in range(micro):
                @pl.when((lax.rem(section, group) == rank + 1) & (mine != worker))
                def _():
                    pl.semaphore_wait(ready.at[worker], 1)
                    for layer in range(LAYERS):
                        for i in range(3):
                            relay_copy(layer, i, section, worker).start()

    @pl.when(works)
    def _():
        for r in range(side):
            values = states[mine, :, r].astype(jnp.float32)
            if whole != patches:
                values = jnp.concatenate([values, jnp.zeros((whole - patches, 8, chan), jnp.float32)], axis=0)
            values = values.reshape(rows, chan)
            split_store(hidden, slice(r * rows, (r + 1) * rows), values)
            for i in range(half):
                stage[i, r] = values.astype(jnp.bfloat16)
        for e, (p, k) in enumerate(edges):
            rims[e] = joined(hidden, rim_span(p, k)).astype(jnp.bfloat16)

        @pl.loop(0, sections // 2)
        def _(pair):
            for turn in range(2):
                run_section(pair * 2 + turn, turn)

        finish(late, len(early))
        wait_sent(1)

        @pl.loop(0, sections - 1)
        def _(sec):
            @pl.when(sec != section)
            def _():
                out_copy(mine, sec).wait_send()

        for n in range(len(early) + len(late)):
            tail_copy(n, mine).wait_send()

    for worker in range(micro):
        @pl.when(section != worker * group)
        def _():
            for piece in (2, 3):
                weight_copy(piece, section, worker).wait_send()

        @pl.when((section != worker * group) & (section != sections - 1))
        def _():
            out_copy(worker, section).wait_recv()

        @pl.when(section == sections - 1)
        def _():
            for n in range(len(early) + len(late)):
                tail_copy(n, worker).wait_recv()

        @pl.when((section != worker * group) & (mine == worker))
        def _():
            for piece in (0, 1):
                weight_copy(piece, section, worker).wait_send()

        @pl.when(mine != worker)
        def _():
            for layer in range(LAYERS):
                for i in range(3):
                    relay_copy(layer, i, section, worker).wait_send()

        @pl.when(relays & (mine != worker))
        def _():
            for rank in range(group):
                for layer in range(LAYERS):
                    for hop in range(2):
                        for i in range(3):
                            pass_copy(layer, i, worker * group + rank, hop, 0).wait_send()


def on_device(states, conv_weight, skip_weight, bias, placement):
    sections = lax.axis_size("section")
    tiles = lax.axis_size("tile")
    micro, patches, side, _, chan = states.shape
    neighbour, rim_side, flip_flag = seam_tables(PR)
    assert not flip_flag.any()
    inner, outer = edge_plan(neighbour, rim_side, patches)
    early, late = tail_plan(patches, side, outer)
    pieces = early + late
    edges = [(p, k) for k in range(4) for p in outer[k]]
    send_row, _, recv_dev, recv_slot = off_device_routes(neighbour, rim_side, flip_flag, tiles, patches)
    slots = send_row.shape[2]
    number = np.zeros(patches * 4, np.int32)
    for e, (p, k) in enumerate(edges):
        number[p * 4 + k] = e
    take = [p * 4 + k for p, k in edges]
    whole = patches + patches % 2
    rows = whole * side
    corners, most, send, home, place, choices, second = ghost_plan(neighbour, rim_side, patches, outer)
    tables = [
        number[send_row].reshape(-1),
        recv_dev.reshape(tiles, -1)[:, take].reshape(-1),
        recv_slot.reshape(tiles, -1)[:, take].reshape(-1),
        send.reshape(-1), home.reshape(-1), place.reshape(-1), second.reshape(-1),
    ]
    starts = [int(x) for x in np.cumsum([0] + [t.size for t in tables])[:-1]]
    table = np.concatenate(tables)
    weights = conv_weight[0].reshape(LAYERS, 3, 3 * chan, chan)
    held = sections + sections // 2
    smem = pl.BlockSpec(memory_space=pltpu.SMEM)
    vmem = pl.BlockSpec(memory_space=pltpu.VMEM)
    wide = pltpu.VMEM((chan // LANES, side * rows, LANES), jnp.float32)
    got = pltpu.VMEM((tiles - 1, slots, side, chan), jnp.bfloat16)
    more = pltpu.VMEM((tiles - 1, slots + 1, side, chan), jnp.bfloat16)
    flops = 2 * micro * side * rows * chan * chan * (9 * LAYERS + 1)
    return pl.pallas_call(
        functools.partial(window_kernel, tiles, sections, patches, micro, slots, inner, outer, early, late, corners, most, choices, starts),
        out_shape=pltpu.VMEM((1,) + states.shape, jnp.bfloat16),
        in_specs=[smem] * 2 + [vmem, pl.BlockSpec(memory_space=pl.ANY), vmem, vmem],
        out_specs=vmem,
        scratch_shapes=[
            pltpu.VMEM((sections,) + weights.shape, jnp.bfloat16),
            pltpu.VMEM((sections, chan, chan), jnp.bfloat16),
            pltpu.VMEM((sections, 8, chan), jnp.float32),
            pltpu.VMEM((8, chan), jnp.float32),
            pltpu.VMEM((held, side, rows, chan), jnp.bfloat16),
            pltpu.VMEM((sections,) + states.shape[1:], jnp.bfloat16),
            wide, wide,
            pltpu.VMEM((side + 2, rows, 3 * chan), jnp.bfloat16),
            pltpu.VMEM((len(edges), side, chan), jnp.bfloat16),
            pltpu.VMEM((len(edges), side, chan), jnp.bfloat16),
            pltpu.VMEM((len(edges) * side, chan), jnp.float32),
            pltpu.VMEM(((tiles - 1) * 8 + 16, chan), jnp.float32),
            got, got, more, more, got, got, more, more,
            pltpu.SMEM((tiles,), jnp.int32),
            pltpu.SMEM(((tiles - 1) * slots,), jnp.int32),
            pltpu.SMEM((len(edges),), jnp.int32),
            pltpu.SMEM((len(edges),), jnp.int32),
            pltpu.SMEM((tiles * most,), jnp.int32),
            pltpu.SMEM((len(corners),), jnp.int32),
            pltpu.SemaphoreType.DMA((2, 2, tiles - 1)),
            pltpu.SemaphoreType.DMA((2, 2, tiles - 1)),
            pltpu.SemaphoreType.DMA((micro, 4)),
            pltpu.SemaphoreType.DMA((sections, 4)),
            pltpu.SemaphoreType.DMA((4,)),
            pltpu.SemaphoreType.DMA((sections,)),
            pltpu.SemaphoreType.DMA((micro,)),
            pltpu.SemaphoreType.REGULAR((micro,)),
            pltpu.SemaphoreType.DMA((micro, LAYERS, 3)),
            pltpu.SemaphoreType.DMA((sections, LAYERS, 3)),
            pltpu.SemaphoreType.DMA((sections, LAYERS, 2, 3)),
            pltpu.SemaphoreType.DMA((sections, LAYERS, 2, 3)),
            pltpu.SemaphoreType.DMA((len(pieces),)),
            pltpu.SemaphoreType.DMA((micro, len(pieces))),
        ],
        compiler_params=pltpu.CompilerParams(
            collective_id=0, has_side_effects=True, vmem_limit_bytes=56 * 1024 * 1024
        ),
        cost_estimate=pl.CostEstimate(flops=flops, bytes_accessed=2**24, transcendentals=0),
    )(
        placement, jnp.asarray(table, jnp.int32),
        states, weights, skip_weight, bias,
    )


def solution(mesh):
    in_specs = (
        P(None, "tile", None, None, None),
        P("section", None, None, None, None, None),
        P("section", None, None),
        P("section", None, None),
        P(),
    )
    out_specs = P("section", None, "tile", None, None, None)
    return jax.shard_map(
        on_device, mesh=mesh, in_specs=in_specs, out_specs=out_specs, check_vma=False
    )
```

```python
import functools

import jax
import jax.numpy as jnp
import numpy as np
from jax import lax
from jax.experimental import pallas as pl
from jax.experimental.pallas import tpu as pltpu
from jax.sharding import PartitionSpec as P

LAYERS = 2
PR = 4


def face_across(face_num, direction):
    cycle = face_num // 4
    column = face_num % 4
    if cycle == 0:
        table = [4 + column, 4 + (column + 1) % 4, (column + 1) % 4, (column + 3) % 4]
    elif cycle == 1:
        table = [8 + (column + 3) % 4, 8 + column, column, (column + 3) % 4]
    else:
        table = [8 + (column + 3) % 4, 8 + (column + 1) % 4, 4 + (column + 1) % 4, 4 + column]
    return table[direction]


def locate(face_num, coord_x, coord_y, face_span):
    if 0 <= coord_x < face_span and 0 <= coord_y < face_span:
        return (face_num, coord_x, coord_y)
    if coord_x < 0:
        direction = 0
    elif coord_y < 0:
        direction = 1
    elif coord_x >= face_span:
        direction = 2
    else:
        direction = 3
    cycle = face_num // 4
    target = face_across(face_num, direction)
    coord_x = coord_x % face_span
    coord_y = coord_y % face_span
    if cycle == 0 and direction == 2 or (cycle == 2 and direction == 0):
        coord_x, coord_y = (coord_y, face_span - 1 - coord_x)
    elif cycle == 0 and direction == 3 or (cycle == 2 and direction == 1):
        coord_x, coord_y = (face_span - 1 - coord_y, coord_x)
    return (target, coord_x, coord_y)


def seam_tables(tiles):
    cell_side = 2
    face_span = tiles * cell_side
    face_tiles = tiles * tiles
    total = 12 * face_tiles
    neighbour = np.zeros((total, 4), np.int32)
    rim_side = np.zeros((total, 4), np.int32)
    flip_flag = np.zeros((total, 4), np.int32)
    for patch_num in range(total):
        cycle = patch_num % 3
        rest = patch_num // 3
        column = rest // face_tiles
        tile_y = rest % face_tiles // tiles
        tile_x = rest % tiles
        face_num = 4 * cycle + column
        base_x = tile_x * cell_side
        base_y = tile_y * cell_side
        for side_num in range(4):
            found = []
            for step_num in range(2):
                if side_num == 0:
                    point = (base_x - 1, base_y + step_num)
                elif side_num == 1:
                    point = (base_x + cell_side, base_y + step_num)
                elif side_num == 2:
                    point = (base_x + step_num, base_y - 1)
                else:
                    point = (base_x + step_num, base_y + cell_side)
                found.append(locate(face_num, point[0], point[1], face_span))
            face_a, first_x, first_y = found[0]
            face_b, second_x, second_y = found[1]
            neighbour[patch_num, side_num] = (
                3 * (face_a % 4 * face_tiles + first_y // cell_side * tiles + first_x // cell_side)
                + face_a // 4
            )
            if first_x == second_x:
                rim_side[patch_num, side_num] = 0 if first_x % cell_side == 0 else 1
                flip_flag[patch_num, side_num] = 1 if second_y < first_y else 0
            else:
                rim_side[patch_num, side_num] = 2 if first_y % cell_side == 0 else 3
                flip_flag[patch_num, side_num] = 1 if second_x < first_x else 0
    return (neighbour, rim_side, flip_flag)


def off_device_routes(neighbour, rim_side, flip_flag, tile_count, per_dev):
    source_dev = (neighbour // per_dev).reshape(-1)
    dest_dev = np.repeat(np.arange(neighbour.shape[0]) // per_dev, 4)
    row = (neighbour % per_dev * 4 + rim_side).reshape(-1)
    away = source_dev != dest_dev
    slot_num = np.zeros(row.shape[0], np.int64)
    counts = np.zeros((tile_count, tile_count), np.int64)
    for e in np.flatnonzero(away):
        slot_num[e] = counts[source_dev[e], dest_dev[e]]
        counts[source_dev[e], dest_dev[e]] += 1
    send_row = np.zeros((tile_count, tile_count, int(counts.max())), np.int32)
    send_row[source_dev[away], dest_dev[away], slot_num[away]] = row[away]
    place = np.where(away, slot_num, row)
    recv_dev = source_dev.reshape(tile_count, per_dev, 4).astype(np.int32)
    recv_slot = place.reshape(tile_count, per_dev, 4).astype(np.int32)
    return (send_row, None, recv_dev, recv_slot)


MESH = pl.DeviceIdType.MESH
LANES = 128


def edge_plan(neighbour, rim_side, patches):
    blocks = neighbour.shape[0] // patches
    near = neighbour.reshape(blocks, patches, 4) // patches
    home = near == np.arange(blocks)[:, None, None]
    inner = [[None] * patches for _ in range(4)]
    outer = [[] for _ in range(4)]
    for p in range(patches):
        for k in range(4):
            local = neighbour.reshape(blocks, patches, 4)[:, p, k] % patches
            same = home[:, p, k].all() and (local == local[0]).all()
            facing = (rim_side.reshape(blocks, patches, 4)[:, p, k] == (k ^ 1)).all()
            if same and facing:
                inner[k][p] = int(local[0])
            else:
                assert not home[:, p, k].any()
                outer[k].append(p)
    for k in (2, 3):
        assert outer[k] == list(range(outer[k][0], outer[k][-1] + 1))
    return inner, outer


def ghost_plan(neighbour, rim_side, patches, outer):
    blocks = neighbour.shape[0] // patches
    edges = [(p, k) for k in range(4) for p in outer[k]]
    number = {edge: e for e, edge in enumerate(edges)}
    facing = np.zeros((blocks, len(edges)), np.int32)
    sent = [[[] for _ in range(blocks)] for _ in range(blocks)]
    found = {}
    for b in range(blocks):
        for e, (p, k) in enumerate(edges):
            q, t = neighbour[b * patches + p, k], rim_side[b * patches + p, k]
            facing[b, e] = t
            for end in range(2):
                across = (2 if t < 2 else 0) + end
                if (q % patches, across) in number:
                    other, side = neighbour[q, across], rim_side[q, across]
                    home = other // patches
                    row = number[(other % patches, side)] * 8 + (0 if t in (0, 2) else 7)
                    found[(b, e, end)] = (home, len(sent[home][b]))
                    sent[home][b].append(row)
    corners = sorted({(e, end) for _, e, end in found})
    most = max(len(x) for line in sent for x in line)
    assert most <= 8
    send = np.zeros((blocks, blocks, most), np.int32)
    for a in range(blocks):
        for b in range(blocks):
            send[a, b, :len(sent[a][b])] = sent[a][b]
    home = np.full((blocks, len(corners)), -1, np.int32)
    place = np.zeros((blocks, len(corners)), np.int32)
    for n, (e, end) in enumerate(corners):
        for b in range(blocks):
            if (b, e, end) in found:
                home[b, n], place[b, n] = found[(b, e, end)]
    choices = [sorted(set(facing[:, e].tolist())) for e in range(len(edges))]
    assert all(len(c) <= 2 for c in choices)
    second = np.stack([(facing[:, e] != choices[e][0]).astype(np.int32) for e in range(len(edges))], axis=1)
    return corners, most, send, home, place, choices, second


def tail_plan(patches, side, outer):
    early, late = [], []
    for p in range(patches):
        low = 1 if p in outer[2] else 0
        high = side - 1 if p in outer[3] else side
        clean = p not in outer[0] and p not in outer[1]
        for spans, low_row, high_row in ((early if clean else late, low, high), (late, 0, low), (late, high, side)):
            if low_row < high_row:
                spans.append((p, p + 1, low_row, high_row))
    plans = []
    for spans in (early, late):
        merged = []
        for p, end, low, high in sorted(spans, key=lambda piece: (piece[2], piece[3], piece[0])):
            if merged and merged[-1][1] == p and merged[-1][2:] == (low, high):
                merged[-1] = (merged[-1][0], end, low, high)
            else:
                merged.append((p, end, low, high))
        plans.append(merged)
    return plans


def joined(ref, span):
    return jnp.concatenate([ref[b, span, :] for b in range(ref.shape[0])], axis=1)


def split_store(ref, span, value):
    for b in range(ref.shape[0]):
        ref[b, span, :] = value[:, b * LANES:(b + 1) * LANES]


def window_kernel(
    tiles, sections, patches, micro, slots, inner, outer, early, late, corners, most, choices, starts,
    placement, table,
    states, weights, skip_w, biases,
    out,
    held, skip_held, bias_held, bias_own, stage, finished, hidden, summed, padded, rims, partial, across, corner_rows,
    outgoing_0, outgoing_1, onward_0, onward_1, received_0, received_1, gotten_0, gotten_1,
    behind, send_rows, edge_by, edge_slot, corner_send, corner_place,
    halo_send, halo_recv, weight_send, weight_recv, own_sem, out_send, out_recv, ready,
    relay_send, relay_recv, pass_send, pass_recv, tail_send, tail_recv,
):
    tile = lax.axis_index("tile")
    section = lax.axis_index("section")
    half = sections // 2
    side = states.shape[2]
    chan = states.shape[4]
    rows = stage.shape[2]
    whole = rows // side
    outgoing, onward = (outgoing_0, outgoing_1), (onward_0, onward_1)
    received, gotten = (received_0, received_1), (gotten_0, gotten_1)
    edges = [(p, k) for k in range(4) for p in outer[k]]
    first_edge = [sum(len(outer[j]) for j in range(k)) for k in range(4)]

    def tile_at(by):
        return lax.rem(tile + by, tiles)

    partner = tile + 1 - 2 * lax.rem(tile, 2)
    barrier = pltpu.get_barrier_semaphore()
    for by in range(1, tiles):
        pl.semaphore_signal(barrier, inc=1, device_id={"tile": tile_at(by)}, device_id_type=MESH)
    for by in range(1, sections):
        pl.semaphore_signal(
            barrier, inc=1, device_id={"section": lax.rem(section + by, sections)}, device_id_type=MESH
        )
        pl.semaphore_signal(
            barrier, inc=1, device_id={"tile": partner, "section": lax.rem(section + by, sections)},
            device_id_type=MESH,
        )

    bias_own[...] = jnp.zeros_like(bias_own)
    bias_own[0:LAYERS, :] = biases[0].astype(jnp.float32)

    group = sections // micro
    assert group > 1 and sections % 2 == 0 and LAYERS == 2
    works = lax.rem(section, group) == 0
    mine = section // group
    my_block = placement[tile]
    count = len(edges)
    sends, sources, places, corner_sends, corner_homes, corner_places, seconds = starts

    def find(block, _):
        def one(by, found):
            here = placement[lax.rem(tile - by + tiles, tiles)]
            return jnp.where(here == block, by, found)

        behind[block] = lax.fori_loop(0, tiles, one, jnp.int32(0))
        return 0

    local_row = (tiles - 1) * 8
    blank_row = local_row + 8
    corner_rows[blank_row:blank_row + 8, :] = jnp.zeros((8, chan), jnp.float32)

    lax.fori_loop(0, tiles, find, 0)

    def route(e, _):
        edge_by[e] = behind[table[sources + my_block * count + e]] - 1
        edge_slot[e] = table[places + my_block * count + e]
        return 0

    lax.fori_loop(0, count, route, 0)

    def fill(i, _):
        other = placement[tile_at(i // slots + 1)]
        send_rows[i] = table[sends + (my_block * tiles + other) * slots + lax.rem(i, slots)]
        return 0

    lax.fori_loop(0, (tiles - 1) * slots, fill, 0)

    def fill_corner(i, _):
        other = placement[tile_at(i // most)]
        corner_send[i] = table[corner_sends + (my_block * tiles + other) * most + lax.rem(i, most)]
        return 0

    lax.fori_loop(0, tiles * most, fill_corner, 0)

    def place_corner(n, _):
        home = table[corner_homes + my_block * len(corners) + n]
        by = behind[jnp.maximum(home, 0)]
        row = table[corner_places + my_block * len(corners) + n]
        row += jnp.where(by == 0, local_row, (by - 1) * 8)
        corner_place[n] = jnp.where(home < 0, blank_row, row)
        return 0

    lax.fori_loop(0, len(corners), place_corner, 0)

    pl.semaphore_wait(barrier, tiles - 1 + 2 * (sections - 1))

    column = lax.broadcasted_iota(jnp.int32, (whole, 8, chan), 1)
    first = column == 0
    last = column == 7

    def halo_copy(wave, turn, by):
        source, target = ((outgoing, received), (onward, gotten))[wave]
        return pltpu.make_async_remote_copy(
            src_ref=source[turn].at[by - 1],
            dst_ref=target[turn].at[by - 1],
            send_sem=halo_send.at[turn, wave, by - 1],
            recv_sem=halo_recv.at[turn, wave, by - 1],
            device_id={"tile": tile_at(by)},
            device_id_type=MESH,
        )

    pieces = (
        (weights.at[0], held, 0), (weights.at[1], held, 1), (skip_w.at[0], skip_held, None), (bias_own, bias_held, None)
    )

    def weight_copy(piece, source, worker):
        src, dst, layer = pieces[piece]
        return pltpu.make_async_remote_copy(
            src_ref=src,
            dst_ref=dst.at[source] if layer is None else dst.at[source, layer],
            send_sem=weight_send.at[worker, piece],
            recv_sem=weight_recv.at[source, piece],
            device_id={"section": worker * group},
            device_id_type=MESH,
        )

    def own_copy(piece):
        src, dst, layer = pieces[piece]
        return pltpu.make_async_copy(
            src, dst.at[section] if layer is None else dst.at[section, layer], own_sem.at[piece]
        )

    def out_copy(m, sec):
        return pltpu.make_async_remote_copy(
            src_ref=finished.at[sec], dst_ref=out.at[0, m],
            send_sem=out_send.at[sec], recv_sem=out_recv.at[m],
            device_id={"section": sec}, device_id_type=MESH,
        )

    units = {0: list(range(7)), 1: list(range(7, 13))}

    def unit_span(unit, other):
        which = lax.rem(tile + other, 2)
        if unit == 0:
            deep = chan // 2
            return (pl.ds(pl.multiple_of(which * deep, LANES), deep),)
        deep = 3 * chan // 4
        layer, rest = (unit - 1) // 6, (unit - 1) % 6
        start = which * 2 * deep + (rest % 2) * deep
        return (layer, rest // 2, pl.ds(pl.multiple_of(start, 64), deep))

    def place_of(unit, source, other):
        return (skip_held if unit == 0 else held).at[(source,) + unit_span(unit, other)]

    def relay_copy(unit, source, worker):
        own = (skip_w.at[0] if unit == 0 else weights).at[unit_span(unit, 0)]
        return pltpu.make_async_remote_copy(
            src_ref=own, dst_ref=place_of(unit, source, 0),
            send_sem=relay_send.at[worker, unit], recv_sem=relay_recv.at[source, unit],
            device_id={"section": worker * group + 1}, device_id_type=MESH,
        )

    def pass_copy(unit, source, hop, other):
        place = place_of(unit, source, other)
        device = {"section": mine * group}
        if hop == 1:
            device["tile"] = partner
        return pltpu.make_async_remote_copy(
            src_ref=place, dst_ref=place,
            send_sem=pass_send.at[source, hop, unit], recv_sem=pass_recv.at[source, hop, unit],
            device_id=device, device_id_type=MESH,
        )

    def need(sec, layer):
        near = sec // group == mine
        for piece in ((3, 2, 0) if layer == 0 else (1,)):
            @pl.when(sec == section)
            def _():
                own_copy(piece).wait()

            @pl.when((sec != section) & (True if piece == 3 else near))
            def _():
                weight_copy(piece, sec, 0).wait_recv()

        @pl.when(jnp.logical_not(near))
        def _():
            for unit in units[layer]:
                for hop in range(2):
                    pass_copy(unit, sec, hop, hop).wait_recv()

    def gelu(z):
        return 0.5 * z * (1.0 + lax.erf(z * np.float32(0.5 ** 0.5)))

    def rolled(values, by):
        return pltpu.roll(values.reshape(values.shape[0] // 8, 8, chan), by, 1)

    def strided(values):
        height = values.shape[0]
        lower = jnp.where(first[:height // 8], 0.0, rolled(values, 1)).reshape(height, chan)
        upper = jnp.where(last[:height // 8], 0.0, rolled(values, 7)).reshape(height, chan)
        return jnp.concatenate([lower, values, upper], axis=1)

    def picked(cells, chosen):
        blank = jnp.zeros((1,) + cells.shape[1:], cells.dtype)
        parts = [blank if q is None else cells[q:q + 1] for q in chosen]
        parts += [blank] * (whole - len(chosen))
        return jnp.concatenate(parts, axis=0)

    def shifted_row(values):
        lower, upper = rolled(values, 1), rolled(values, 7)
        lower = jnp.where(first, picked(lower, inner[0]), lower).reshape(rows, chan)
        upper = jnp.where(last, picked(upper, inner[1]), upper).reshape(rows, chan)
        return jnp.concatenate([lower, values, upper], axis=1).astype(jnp.bfloat16)

    def across_row(values, chosen):
        moved = strided(values).reshape(whole, 8, 3 * chan)
        return picked(moved, chosen).reshape(rows, 3 * chan).astype(jnp.bfloat16)

    def rim_span(p, k):
        if k < 2:
            return pl.ds(p * 8 + 7 * k, 8, stride=rows)
        top = (k - 2) * (side - 1) * rows
        return slice(top + p * 8, top + p * 8 + 8)

    def send_rims(turn):
        for by in range(1, tiles):
            for q in range(slots):
                outgoing[turn][by - 1, q] = rims[send_rows[(by - 1) * slots + q]]
            halo_copy(0, turn, by).start()

    def wait_sent(turn):
        for wave in range(2):
            for by in range(1, tiles):
                halo_copy(wave, turn, by).wait_send()

    def side_dot(values, sec, layer, k):
        moved = strided(values).astype(jnp.bfloat16)
        if k >= 2:
            return jnp.dot(moved, held[sec, layer, k * 2 - 4], preferred_element_type=jnp.float32)
        total = jnp.zeros((values.shape[0], chan), jnp.float32)
        for i in range(3):
            total += jnp.dot(
                moved[:, i * chan:(i + 1) * chan],
                held[sec, layer, i, k * 2 * chan:(k * 2 + 1) * chan],
                preferred_element_type=jnp.float32,
            )
        return total

    def cross_seams(sec):
        made = {}
        for t in range(4):
            chosen = [e for e in range(count) if t in choices[e]]
            if chosen:
                values = jnp.concatenate([rims[e].astype(jnp.float32) for e in chosen], axis=0)
                total = side_dot(values, sec, 0, t)
                for n, e in enumerate(chosen):
                    made[e, t] = total[n * 8:n * 8 + 8]
        for e in range(count):
            value = made[e, choices[e][0]]
            if len(choices[e]) > 1:
                value = jnp.where(table[seconds + my_block * count + e] != 0, made[e, choices[e][1]], value)
            across[e * 8:e * 8 + 8, :] = value

    place_in = lax.broadcasted_iota(jnp.int32, (8, chan), 0)

    def corner_block(other):
        block = jnp.zeros((8, chan), jnp.float32)
        for j in range(most):
            row = across[pl.ds(corner_send[other * most + j], 1), :]
            block = jnp.where(place_in == j, row, block)
        return block

    def send_partial(turn):
        for e, (p, k) in enumerate(edges):
            partial[e] = joined(summed, rim_span(p, k)).astype(jnp.bfloat16)
        for by in range(1, tiles):
            for q in range(slots):
                onward[turn][by - 1, q] = partial[send_rows[(by - 1) * slots + q]]
            onward[turn][by - 1, slots] = corner_block(by).astype(jnp.bfloat16)
            halo_copy(1, turn, by).start()

    def take_corners(turn):
        for by in range(1, tiles):
            corner_rows[(by - 1) * 8:by * 8, :] = gotten[turn][by - 1, slots].astype(jnp.float32)
        corner_rows[local_row:local_row + 8, :] = corner_block(0)

    def ghost(turn, e):
        z = gotten[turn][edge_by[e], edge_slot[e]].astype(jnp.float32) + across[e * 8:e * 8 + 8, :]
        for end in range(2):
            if (e, end) in corners:
                row = corner_rows[pl.ds(corner_place[corners.index((e, end))], 1), :]
                z += jnp.where(place_in == 7 * end, row, 0.0)
        return gelu(z)

    def keep(sec):
        for r in range(side):
            values = joined(hidden, slice(r * rows, (r + 1) * rows)).astype(jnp.bfloat16)
            stage[half + sec, r] = values
            finished[sec, :, r] = values.reshape(whole, 8, chan)[:patches]

        @pl.when(sec == section)
        def _():
            out[0, mine] = finished[sec]

        @pl.when(sec != section)
        def _():
            out_copy(mine, sec).start()

    def tail_copy(n, m):
        start, end, low, high = (early + late)[n]
        span = (slice(start, end), slice(low, high))
        return pltpu.make_async_remote_copy(
            src_ref=finished.at[(sections - 1,) + span], dst_ref=out.at[(0, m) + span],
            send_sem=tail_send.at[n], recv_sem=tail_recv.at[m, n],
            device_id={"section": sections - 1}, device_id_type=MESH,
        )

    def finish(which, begin):
        for start, end, low, high in which:
            for r in range(low, high):
                values = joined(hidden, slice(r * rows + start * 8, r * rows + end * 8))
                finished[sections - 1, start:end, r] = values.reshape(end - start, 8, chan).astype(jnp.bfloat16)
        for n in range(len(which)):
            tail_copy(begin + n, mine).start()

    def interior(sec, layer):
        for r in range(side):
            values = joined(hidden, slice(r * rows, (r + 1) * rows))
            padded[r + 1] = shifted_row(values)
            if r == 0:
                padded[side + 1] = across_row(values, inner[3])
            if r == side - 1:
                padded[0] = across_row(values, inner[2])

        step = 2
        need(sec, layer)

        @pl.loop(0, side // step)
        def _(part):
            r = part * step
            total = jnp.broadcast_to(bias_held[sec, layer:layer + 1, :], (step * rows, chan))
            for i in range(3):
                total += jnp.dot(
                    padded[pl.ds(r + i, step)].reshape(step * rows, 3 * chan),
                    held[sec, layer, i],
                    preferred_element_type=jnp.float32,
                )
            if layer == 0:
                total += jnp.dot(
                    stage[sec, pl.ds(r, step)].reshape(step * rows, chan),
                    skip_held[sec],
                    preferred_element_type=jnp.float32,
                )
            span = pl.ds(pl.multiple_of(r * rows, 8), step * rows)
            split_store(summed, span, total)
            split_store(hidden, span, gelu(total))

    def add_strips(sec, layer, strip):
        for k in (0, 1):
            values = [strip(first_edge[k] + n) for n in range(len(outer[k]))]
            added = side_dot(jnp.concatenate(values, axis=0), sec, layer, k)
            for n, p in enumerate(outer[k]):
                for b in range(chan // LANES):
                    summed[b, rim_span(p, k), :] += added[n * 8:n * 8 + 8, b * LANES:(b + 1) * LANES]
        for k in (2, 3):
            values = [strip(first_edge[k] + n) for n in range(len(outer[k]))]
            added = side_dot(jnp.concatenate(values, axis=0), sec, layer, k)
            top = (k - 2) * (side - 1) * rows
            span = slice(top + outer[k][0] * 8, top + outer[k][-1] * 8 + 8)
            total = joined(summed, span) + added
            split_store(summed, span, total)
            fresh = gelu(total)
            split_store(hidden, span, fresh)
            if layer == LAYERS - 1:
                for n in range(len(outer[k])):
                    rims[first_edge[k] + n] = fresh[n * 8:n * 8 + 8].astype(jnp.bfloat16)
        for k in (0, 1):
            for n, p in enumerate(outer[k]):
                fresh = gelu(joined(summed, rim_span(p, k)))
                split_store(hidden, rim_span(p, k), fresh)
                if layer == LAYERS - 1:
                    rims[first_edge[k] + n] = fresh.astype(jnp.bfloat16)

    def run_section(sec, turn):
        send_rims(turn)

        @pl.when(sec > 0)
        def _():
            keep(sec - 1)
            wait_sent(1 - turn)

        interior(sec, 0)
        cross_seams(sec)
        send_partial(turn)

        for by in range(1, tiles):
            halo_copy(0, turn, by).wait_recv()
        add_strips(sec, 0, lambda e: received[turn][edge_by[e], edge_slot[e]].astype(jnp.float32))

        interior(sec, 1)

        if turn == 1:
            @pl.when(sec == sections - 1)
            def _():
                finish(early, 0)

        for by in range(1, tiles):
            halo_copy(1, turn, by).wait_recv()
        take_corners(turn)
        add_strips(sec, 1, lambda e: ghost(turn, e))

    def send_weights(worker, which):
        for piece in which:
            weight_copy(piece, section, worker).start()

    @pl.when(works)
    def _():
        for piece in (3, 2, 0, 1):
            own_copy(piece).start()

    def send_units(worker):
        for unit in units[0] + units[1]:
            relay_copy(unit, section, worker).start()

    for worker in range(micro):
        @pl.when((section != worker * group) & (mine == worker))
        def _():
            send_weights(worker, (3, 2, 0, 1))

        @pl.when(mine != worker)
        def _():
            send_weights(worker, (3,))

        @pl.when(works & (mine != worker))
        def _():
            send_units(worker)

    relays = lax.rem(section, group) == 1

    def pass_on(source, wanted):
        for unit in wanted:
            relay_copy(unit, source, 0).wait_recv()
            for hop in (1, 0):
                pass_copy(unit, source, hop, 0).start()

    for rank in range(group):
        for worker in range(micro):
            source = worker * group + rank

            @pl.when(relays & (mine != worker))
            def _():
                pass_on(source, (units[0] + units[1])[:-3])
                if rank + 1 < group:
                    pl.semaphore_signal(
                        ready.at[mine], inc=1, device_id={"section": worker * group + rank + 1},
                        device_id_type=MESH,
                    )
                pass_on(source, (units[0] + units[1])[-3:])

        if rank + 1 < group:
            for worker in range(micro):
                @pl.when((lax.rem(section, group) == rank + 1) & (mine != worker))
                def _():
                    pl.semaphore_wait(ready.at[worker], 1)
                    send_units(worker)

    @pl.when(works)
    def _():
        for r in range(side):
            values = states[mine, :, r].astype(jnp.float32)
            if whole != patches:
                values = jnp.concatenate([values, jnp.zeros((whole - patches, 8, chan), jnp.float32)], axis=0)
            values = values.reshape(rows, chan)
            split_store(hidden, slice(r * rows, (r + 1) * rows), values)
            for i in range(half):
                stage[i, r] = values.astype(jnp.bfloat16)
        for e, (p, k) in enumerate(edges):
            rims[e] = joined(hidden, rim_span(p, k)).astype(jnp.bfloat16)

        @pl.loop(0, sections // 2)
        def _(pair):
            for turn in range(2):
                run_section(pair * 2 + turn, turn)

        finish(late, len(early))
        wait_sent(1)

        @pl.loop(0, sections - 1)
        def _(sec):
            @pl.when(sec != section)
            def _():
                out_copy(mine, sec).wait_send()

        for n in range(len(early) + len(late)):
            tail_copy(n, mine).wait_send()

    for worker in range(micro):
        @pl.when(section != worker * group)
        def _():
            weight_copy(3, section, worker).wait_send()

        @pl.when((section != worker * group) & (section != sections - 1))
        def _():
            out_copy(worker, section).wait_recv()

        @pl.when(section == sections - 1)
        def _():
            for n in range(len(early) + len(late)):
                tail_copy(n, worker).wait_recv()

        @pl.when((section != worker * group) & (mine == worker))
        def _():
            for piece in (2, 0, 1):
                weight_copy(piece, section, worker).wait_send()

        @pl.when(mine != worker)
        def _():
            for unit in units[0] + units[1]:
                relay_copy(unit, section, worker).wait_send()

        @pl.when(relays & (mine != worker))
        def _():
            for rank in range(group):
                for unit in units[0] + units[1]:
                    for hop in range(2):
                        pass_copy(unit, worker * group + rank, hop, 0).wait_send()


def on_device(states, conv_weight, skip_weight, bias, placement):
    sections = lax.axis_size("section")
    tiles = lax.axis_size("tile")
    micro, patches, side, _, chan = states.shape
    neighbour, rim_side, flip_flag = seam_tables(PR)
    assert not flip_flag.any()
    inner, outer = edge_plan(neighbour, rim_side, patches)
    early, late = tail_plan(patches, side, outer)
    pieces = early + late
    edges = [(p, k) for k in range(4) for p in outer[k]]
    send_row, _, recv_dev, recv_slot = off_device_routes(neighbour, rim_side, flip_flag, tiles, patches)
    slots = send_row.shape[2]
    number = np.zeros(patches * 4, np.int32)
    for e, (p, k) in enumerate(edges):
        number[p * 4 + k] = e
    take = [p * 4 + k for p, k in edges]
    whole = patches + patches % 2
    rows = whole * side
    corners, most, send, home, place, choices, second = ghost_plan(neighbour, rim_side, patches, outer)
    tables = [
        number[send_row].reshape(-1),
        recv_dev.reshape(tiles, -1)[:, take].reshape(-1),
        recv_slot.reshape(tiles, -1)[:, take].reshape(-1),
        send.reshape(-1), home.reshape(-1), place.reshape(-1), second.reshape(-1),
    ]
    starts = [int(x) for x in np.cumsum([0] + [t.size for t in tables])[:-1]]
    table = np.concatenate(tables)
    weights = conv_weight[0].reshape(LAYERS, 3, 3 * chan, chan)
    held = sections + sections // 2
    smem = pl.BlockSpec(memory_space=pltpu.SMEM)
    vmem = pl.BlockSpec(memory_space=pltpu.VMEM)
    wide = pltpu.VMEM((chan // LANES, side * rows, LANES), jnp.float32)
    got = pltpu.VMEM((tiles - 1, slots, side, chan), jnp.bfloat16)
    more = pltpu.VMEM((tiles - 1, slots + 1, side, chan), jnp.bfloat16)
    flops = 2 * micro * side * rows * chan * chan * (9 * LAYERS + 1)
    return pl.pallas_call(
        functools.partial(window_kernel, tiles, sections, patches, micro, slots, inner, outer, early, late, corners, most, choices, starts),
        out_shape=pltpu.VMEM((1,) + states.shape, jnp.bfloat16),
        in_specs=[smem] * 2 + [vmem, pl.BlockSpec(memory_space=pl.ANY), vmem, vmem],
        out_specs=vmem,
        scratch_shapes=[
            pltpu.VMEM((sections,) + weights.shape, jnp.bfloat16),
            pltpu.VMEM((sections, chan, chan), jnp.bfloat16),
            pltpu.VMEM((sections, 8, chan), jnp.float32),
            pltpu.VMEM((8, chan), jnp.float32),
            pltpu.VMEM((held, side, rows, chan), jnp.bfloat16),
            pltpu.VMEM((sections,) + states.shape[1:], jnp.bfloat16),
            wide, wide,
            pltpu.VMEM((side + 2, rows, 3 * chan), jnp.bfloat16),
            pltpu.VMEM((len(edges), side, chan), jnp.bfloat16),
            pltpu.VMEM((len(edges), side, chan), jnp.bfloat16),
            pltpu.VMEM((len(edges) * side, chan), jnp.float32),
            pltpu.VMEM(((tiles - 1) * 8 + 16, chan), jnp.float32),
            got, got, more, more, got, got, more, more,
            pltpu.SMEM((tiles,), jnp.int32),
            pltpu.SMEM(((tiles - 1) * slots,), jnp.int32),
            pltpu.SMEM((len(edges),), jnp.int32),
            pltpu.SMEM((len(edges),), jnp.int32),
            pltpu.SMEM((tiles * most,), jnp.int32),
            pltpu.SMEM((len(corners),), jnp.int32),
            pltpu.SemaphoreType.DMA((2, 2, tiles - 1)),
            pltpu.SemaphoreType.DMA((2, 2, tiles - 1)),
            pltpu.SemaphoreType.DMA((micro, 4)),
            pltpu.SemaphoreType.DMA((sections, 4)),
            pltpu.SemaphoreType.DMA((4,)),
            pltpu.SemaphoreType.DMA((sections,)),
            pltpu.SemaphoreType.DMA((micro,)),
            pltpu.SemaphoreType.REGULAR((micro,)),
            pltpu.SemaphoreType.DMA((micro, 13)),
            pltpu.SemaphoreType.DMA((sections, 13)),
            pltpu.SemaphoreType.DMA((sections, 2, 13)),
            pltpu.SemaphoreType.DMA((sections, 2, 13)),
            pltpu.SemaphoreType.DMA((len(pieces),)),
            pltpu.SemaphoreType.DMA((micro, len(pieces))),
        ],
        compiler_params=pltpu.CompilerParams(
            collective_id=0, has_side_effects=True, vmem_limit_bytes=56 * 1024 * 1024
        ),
        cost_estimate=pl.CostEstimate(flops=flops, bytes_accessed=2**24, transcendentals=0),
    )(
        placement, jnp.asarray(table, jnp.int32),
        states, weights, skip_weight, bias,
    )


def solution(mesh):
    in_specs = (
        P(None, "tile", None, None, None),
        P("section", None, None, None, None, None),
        P("section", None, None),
        P("section", None, None),
        P(),
    )
    out_specs = P("section", None, "tile", None, None, None)
    return jax.shard_map(
        on_device, mesh=mesh, in_specs=in_specs, out_specs=out_specs, check_vma=False
    )
```

```python
import functools

import jax
import jax.numpy as jnp
import numpy as np
from jax import lax
from jax.experimental import pallas as pl
from jax.experimental.pallas import tpu as pltpu
from jax.sharding import PartitionSpec as P

LAYERS = 2
PR = 4


def face_across(face_num, direction):
    cycle = face_num // 4
    column = face_num % 4
    if cycle == 0:
        table = [4 + column, 4 + (column + 1) % 4, (column + 1) % 4, (column + 3) % 4]
    elif cycle == 1:
        table = [8 + (column + 3) % 4, 8 + column, column, (column + 3) % 4]
    else:
        table = [8 + (column + 3) % 4, 8 + (column + 1) % 4, 4 + (column + 1) % 4, 4 + column]
    return table[direction]


def locate(face_num, coord_x, coord_y, face_span):
    if 0 <= coord_x < face_span and 0 <= coord_y < face_span:
        return (face_num, coord_x, coord_y)
    if coord_x < 0:
        direction = 0
    elif coord_y < 0:
        direction = 1
    elif coord_x >= face_span:
        direction = 2
    else:
        direction = 3
    cycle = face_num // 4
    target = face_across(face_num, direction)
    coord_x = coord_x % face_span
    coord_y = coord_y % face_span
    if cycle == 0 and direction == 2 or (cycle == 2 and direction == 0):
        coord_x, coord_y = (coord_y, face_span - 1 - coord_x)
    elif cycle == 0 and direction == 3 or (cycle == 2 and direction == 1):
        coord_x, coord_y = (face_span - 1 - coord_y, coord_x)
    return (target, coord_x, coord_y)


def seam_tables(tiles):
    cell_side = 2
    face_span = tiles * cell_side
    face_tiles = tiles * tiles
    total = 12 * face_tiles
    neighbour = np.zeros((total, 4), np.int32)
    rim_side = np.zeros((total, 4), np.int32)
    flip_flag = np.zeros((total, 4), np.int32)
    for patch_num in range(total):
        cycle = patch_num % 3
        rest = patch_num // 3
        column = rest // face_tiles
        tile_y = rest % face_tiles // tiles
        tile_x = rest % tiles
        face_num = 4 * cycle + column
        base_x = tile_x * cell_side
        base_y = tile_y * cell_side
        for side_num in range(4):
            found = []
            for step_num in range(2):
                if side_num == 0:
                    point = (base_x - 1, base_y + step_num)
                elif side_num == 1:
                    point = (base_x + cell_side, base_y + step_num)
                elif side_num == 2:
                    point = (base_x + step_num, base_y - 1)
                else:
                    point = (base_x + step_num, base_y + cell_side)
                found.append(locate(face_num, point[0], point[1], face_span))
            face_a, first_x, first_y = found[0]
            face_b, second_x, second_y = found[1]
            neighbour[patch_num, side_num] = (
                3 * (face_a % 4 * face_tiles + first_y // cell_side * tiles + first_x // cell_side)
                + face_a // 4
            )
            if first_x == second_x:
                rim_side[patch_num, side_num] = 0 if first_x % cell_side == 0 else 1
                flip_flag[patch_num, side_num] = 1 if second_y < first_y else 0
            else:
                rim_side[patch_num, side_num] = 2 if first_y % cell_side == 0 else 3
                flip_flag[patch_num, side_num] = 1 if second_x < first_x else 0
    return (neighbour, rim_side, flip_flag)


def off_device_routes(neighbour, rim_side, flip_flag, tile_count, per_dev):
    source_dev = (neighbour // per_dev).reshape(-1)
    dest_dev = np.repeat(np.arange(neighbour.shape[0]) // per_dev, 4)
    row = (neighbour % per_dev * 4 + rim_side).reshape(-1)
    away = source_dev != dest_dev
    slot_num = np.zeros(row.shape[0], np.int64)
    counts = np.zeros((tile_count, tile_count), np.int64)
    for e in np.flatnonzero(away):
        slot_num[e] = counts[source_dev[e], dest_dev[e]]
        counts[source_dev[e], dest_dev[e]] += 1
    send_row = np.zeros((tile_count, tile_count, int(counts.max())), np.int32)
    send_row[source_dev[away], dest_dev[away], slot_num[away]] = row[away]
    place = np.where(away, slot_num, row)
    recv_dev = source_dev.reshape(tile_count, per_dev, 4).astype(np.int32)
    recv_slot = place.reshape(tile_count, per_dev, 4).astype(np.int32)
    return (send_row, None, recv_dev, recv_slot)


MESH = pl.DeviceIdType.MESH
LANES = 128


def edge_plan(neighbour, rim_side, patches):
    blocks = neighbour.shape[0] // patches
    near = neighbour.reshape(blocks, patches, 4) // patches
    home = near == np.arange(blocks)[:, None, None]
    inner = [[None] * patches for _ in range(4)]
    outer = [[] for _ in range(4)]
    for p in range(patches):
        for k in range(4):
            local = neighbour.reshape(blocks, patches, 4)[:, p, k] % patches
            same = home[:, p, k].all() and (local == local[0]).all()
            facing = (rim_side.reshape(blocks, patches, 4)[:, p, k] == (k ^ 1)).all()
            if same and facing:
                inner[k][p] = int(local[0])
            else:
                assert not home[:, p, k].any()
                outer[k].append(p)
    for k in (2, 3):
        assert outer[k] == list(range(outer[k][0], outer[k][-1] + 1))
    return inner, outer


def ghost_plan(neighbour, rim_side, patches, outer):
    blocks = neighbour.shape[0] // patches
    edges = [(p, k) for k in range(4) for p in outer[k]]
    number = {edge: e for e, edge in enumerate(edges)}
    facing = np.zeros((blocks, len(edges)), np.int32)
    sent = [[[] for _ in range(blocks)] for _ in range(blocks)]
    found = {}
    for b in range(blocks):
        for e, (p, k) in enumerate(edges):
            q, t = neighbour[b * patches + p, k], rim_side[b * patches + p, k]
            facing[b, e] = t
            for end in range(2):
                across = (2 if t < 2 else 0) + end
                if (q % patches, across) in number:
                    other, side = neighbour[q, across], rim_side[q, across]
                    home = other // patches
                    row = number[(other % patches, side)] * 8 + (0 if t in (0, 2) else 7)
                    found[(b, e, end)] = (home, len(sent[home][b]))
                    sent[home][b].append(row)
    corners = sorted({(e, end) for _, e, end in found})
    most = max(len(x) for line in sent for x in line)
    assert most <= 8
    send = np.zeros((blocks, blocks, most), np.int32)
    for a in range(blocks):
        for b in range(blocks):
            send[a, b, :len(sent[a][b])] = sent[a][b]
    home = np.full((blocks, len(corners)), -1, np.int32)
    place = np.zeros((blocks, len(corners)), np.int32)
    for n, (e, end) in enumerate(corners):
        for b in range(blocks):
            if (b, e, end) in found:
                home[b, n], place[b, n] = found[(b, e, end)]
    choices = [sorted(set(facing[:, e].tolist())) for e in range(len(edges))]
    assert all(len(c) <= 2 for c in choices)
    second = np.stack([(facing[:, e] != choices[e][0]).astype(np.int32) for e in range(len(edges))], axis=1)
    return corners, most, send, home, place, choices, second


def tail_plan(patches, side, outer):
    early, late = [], []
    for p in range(patches):
        low = 1 if p in outer[2] else 0
        high = side - 1 if p in outer[3] else side
        clean = p not in outer[0] and p not in outer[1]
        for spans, low_row, high_row in ((early if clean else late, low, high), (late, 0, low), (late, high, side)):
            if low_row < high_row:
                spans.append((p, p + 1, low_row, high_row))
    plans = []
    for spans in (early, late):
        merged = []
        for p, end, low, high in sorted(spans, key=lambda piece: (piece[2], piece[3], piece[0])):
            if merged and merged[-1][1] == p and merged[-1][2:] == (low, high):
                merged[-1] = (merged[-1][0], end, low, high)
            else:
                merged.append((p, end, low, high))
        plans.append(merged)
    return plans


def joined(ref, span):
    return jnp.concatenate([ref[b, span, :] for b in range(ref.shape[0])], axis=1)


def split_store(ref, span, value):
    for b in range(ref.shape[0]):
        ref[b, span, :] = value[:, b * LANES:(b + 1) * LANES]


def window_kernel(
    tiles, sections, patches, micro, slots, inner, outer, early, late, corners, most, choices, starts,
    placement, table,
    states, weights, skip_w, biases,
    out,
    held, skip_held, bias_held, bias_own, stage, finished, hidden, summed, padded, rims, partial, across, corner_rows,
    outgoing_0, outgoing_1, onward_0, onward_1, received_0, received_1, gotten_0, gotten_1,
    behind, send_rows, edge_by, edge_slot, corner_send, corner_place,
    halo_send, halo_recv, weight_send, weight_recv, own_sem, out_send, out_recv, ready,
    relay_send, relay_recv, pass_send, pass_recv, tail_send, tail_recv,
):
    tile = lax.axis_index("tile")
    section = lax.axis_index("section")
    half = sections // 2
    side = states.shape[2]
    chan = states.shape[4]
    rows = stage.shape[2]
    whole = rows // side
    outgoing, onward = (outgoing_0, outgoing_1), (onward_0, onward_1)
    received, gotten = (received_0, received_1), (gotten_0, gotten_1)
    edges = [(p, k) for k in range(4) for p in outer[k]]
    first_edge = [sum(len(outer[j]) for j in range(k)) for k in range(4)]

    def tile_at(by):
        return lax.rem(tile + by, tiles)

    partner = tile + 1 - 2 * lax.rem(tile, 2)
    partner_z = tile + 2 - 4 * lax.rem(tile // 2, 2)
    barrier = pltpu.get_barrier_semaphore()
    for by in range(1, tiles):
        pl.semaphore_signal(barrier, inc=1, device_id={"tile": tile_at(by)}, device_id_type=MESH)
    for by in range(1, sections):
        pl.semaphore_signal(
            barrier, inc=1, device_id={"section": lax.rem(section + by, sections)}, device_id_type=MESH
        )
        pl.semaphore_signal(
            barrier, inc=1, device_id={"tile": partner, "section": lax.rem(section + by, sections)},
            device_id_type=MESH,
        )
        pl.semaphore_signal(
            barrier, inc=1, device_id={"tile": partner_z, "section": lax.rem(section + by, sections)},
            device_id_type=MESH,
        )

    bias_own[...] = jnp.zeros_like(bias_own)
    bias_own[0:LAYERS, :] = biases[0].astype(jnp.float32)

    group = sections // micro
    assert group > 1 and tiles % 4 == 0 and sections % 2 == 0 and LAYERS == 2
    works = lax.rem(section, group) == 0
    mine = section // group
    my_block = placement[tile]
    count = len(edges)
    sends, sources, places, corner_sends, corner_homes, corner_places, seconds = starts

    def find(block, _):
        def one(by, found):
            here = placement[lax.rem(tile - by + tiles, tiles)]
            return jnp.where(here == block, by, found)

        behind[block] = lax.fori_loop(0, tiles, one, jnp.int32(0))
        return 0

    local_row = (tiles - 1) * 8
    blank_row = local_row + 8
    corner_rows[blank_row:blank_row + 8, :] = jnp.zeros((8, chan), jnp.float32)

    lax.fori_loop(0, tiles, find, 0)

    def route(e, _):
        edge_by[e] = behind[table[sources + my_block * count + e]] - 1
        edge_slot[e] = table[places + my_block * count + e]
        return 0

    lax.fori_loop(0, count, route, 0)

    def fill(i, _):
        other = placement[tile_at(i // slots + 1)]
        send_rows[i] = table[sends + (my_block * tiles + other) * slots + lax.rem(i, slots)]
        return 0

    lax.fori_loop(0, (tiles - 1) * slots, fill, 0)

    def fill_corner(i, _):
        other = placement[tile_at(i // most)]
        corner_send[i] = table[corner_sends + (my_block * tiles + other) * most + lax.rem(i, most)]
        return 0

    lax.fori_loop(0, tiles * most, fill_corner, 0)

    def place_corner(n, _):
        home = table[corner_homes + my_block * len(corners) + n]
        by = behind[jnp.maximum(home, 0)]
        row = table[corner_places + my_block * len(corners) + n]
        row += jnp.where(by == 0, local_row, (by - 1) * 8)
        corner_place[n] = jnp.where(home < 0, blank_row, row)
        return 0

    lax.fori_loop(0, len(corners), place_corner, 0)

    pl.semaphore_wait(barrier, tiles - 1 + 3 * (sections - 1))

    column = lax.broadcasted_iota(jnp.int32, (whole, 8, chan), 1)
    first = column == 0
    last = column == 7

    def halo_copy(wave, turn, by):
        source, target = ((outgoing, received), (onward, gotten))[wave]
        return pltpu.make_async_remote_copy(
            src_ref=source[turn].at[by - 1],
            dst_ref=target[turn].at[by - 1],
            send_sem=halo_send.at[turn, wave, by - 1],
            recv_sem=halo_recv.at[turn, wave, by - 1],
            device_id={"tile": tile_at(by)},
            device_id_type=MESH,
        )

    pieces = (
        (weights.at[0], held, 0), (weights.at[1], held, 1), (skip_w.at[0], skip_held, None), (bias_own, bias_held, None)
    )

    def weight_copy(piece, source, worker):
        src, dst, layer = pieces[piece]
        return pltpu.make_async_remote_copy(
            src_ref=src,
            dst_ref=dst.at[source] if layer is None else dst.at[source, layer],
            send_sem=weight_send.at[worker, piece],
            recv_sem=weight_recv.at[source, piece],
            device_id={"section": worker * group},
            device_id_type=MESH,
        )

    def own_copy(piece):
        src, dst, layer = pieces[piece]
        return pltpu.make_async_copy(
            src, dst.at[section] if layer is None else dst.at[section, layer], own_sem.at[piece]
        )

    def out_copy(m, sec):
        return pltpu.make_async_remote_copy(
            src_ref=finished.at[sec], dst_ref=out.at[0, m],
            send_sem=out_send.at[sec], recv_sem=out_recv.at[m],
            device_id={"section": sec}, device_id_type=MESH,
        )

    units = {0: list(range(7)), 1: list(range(7, 13))}

    def unit_span(unit, other):
        if unit == 0:
            deep = chan // 2
            return (pl.ds(pl.multiple_of(lax.rem(tile + other, 2) * deep, LANES), deep),)
        layer, rest = (unit - 1) // 6, (unit - 1) % 6
        deep = 3 * chan // 4
        if by_z(unit):
            start = lax.rem(tile // 2 + other, 2) * deep
        else:
            start = 2 * deep + lax.rem(tile + other, 2) * deep
        return (layer, rest // 2, pl.ds(pl.multiple_of(start, 64), deep))

    def by_z(unit):
        return unit > 0 and unit % 2 == 0

    def place_of(unit, source, other):
        return (skip_held if unit == 0 else held).at[(source,) + unit_span(unit, other)]

    def relay_copy(unit, source, worker):
        own = (skip_w.at[0] if unit == 0 else weights).at[unit_span(unit, 0)]
        return pltpu.make_async_remote_copy(
            src_ref=own, dst_ref=place_of(unit, source, 0),
            send_sem=relay_send.at[worker, unit], recv_sem=relay_recv.at[source, unit],
            device_id={"section": worker * group + 1}, device_id_type=MESH,
        )

    def pass_copy(unit, source, hop, other):
        place = place_of(unit, source, other)
        device = {"section": mine * group}
        if hop == 1:
            device["tile"] = partner_z if by_z(unit) else partner
        return pltpu.make_async_remote_copy(
            src_ref=place, dst_ref=place,
            send_sem=pass_send.at[source, hop, unit], recv_sem=pass_recv.at[source, hop, unit],
            device_id=device, device_id_type=MESH,
        )

    def need(sec, layer):
        near = sec // group == mine
        for piece in ((3, 2, 0) if layer == 0 else (1,)):
            @pl.when(sec == section)
            def _():
                own_copy(piece).wait()

            @pl.when((sec != section) & (True if piece == 3 else near))
            def _():
                weight_copy(piece, sec, 0).wait_recv()

        @pl.when(jnp.logical_not(near))
        def _():
            for unit in units[layer]:
                for hop in range(2):
                    pass_copy(unit, sec, hop, hop).wait_recv()

    def gelu(z):
        return 0.5 * z * (1.0 + lax.erf(z * np.float32(0.5 ** 0.5)))

    def rolled(values, by):
        return pltpu.roll(values.reshape(values.shape[0] // 8, 8, chan), by, 1)

    def strided(values):
        height = values.shape[0]
        lower = jnp.where(first[:height // 8], 0.0, rolled(values, 1)).reshape(height, chan)
        upper = jnp.where(last[:height // 8], 0.0, rolled(values, 7)).reshape(height, chan)
        return jnp.concatenate([lower, values, upper], axis=1)

    def picked(cells, chosen):
        blank = jnp.zeros((1,) + cells.shape[1:], cells.dtype)
        parts = [blank if q is None else cells[q:q + 1] for q in chosen]
        parts += [blank] * (whole - len(chosen))
        return jnp.concatenate(parts, axis=0)

    def shifted_row(values):
        lower, upper = rolled(values, 1), rolled(values, 7)
        lower = jnp.where(first, picked(lower, inner[0]), lower).reshape(rows, chan)
        upper = jnp.where(last, picked(upper, inner[1]), upper).reshape(rows, chan)
        return jnp.concatenate([lower, values, upper], axis=1).astype(jnp.bfloat16)

    def across_row(values, chosen):
        moved = strided(values).reshape(whole, 8, 3 * chan)
        return picked(moved, chosen).reshape(rows, 3 * chan).astype(jnp.bfloat16)

    def rim_span(p, k):
        if k < 2:
            return pl.ds(p * 8 + 7 * k, 8, stride=rows)
        top = (k - 2) * (side - 1) * rows
        return slice(top + p * 8, top + p * 8 + 8)

    def send_rims(turn):
        for by in range(1, tiles):
            for q in range(slots):
                outgoing[turn][by - 1, q] = rims[send_rows[(by - 1) * slots + q]]
            halo_copy(0, turn, by).start()

    def wait_sent(turn):
        for wave in range(2):
            for by in range(1, tiles):
                halo_copy(wave, turn, by).wait_send()

    def side_dot(values, sec, layer, k):
        moved = strided(values).astype(jnp.bfloat16)
        if k >= 2:
            return jnp.dot(moved, held[sec, layer, k * 2 - 4], preferred_element_type=jnp.float32)
        total = jnp.zeros((values.shape[0], chan), jnp.float32)
        for i in range(3):
            total += jnp.dot(
                moved[:, i * chan:(i + 1) * chan],
                held[sec, layer, i, k * 2 * chan:(k * 2 + 1) * chan],
                preferred_element_type=jnp.float32,
            )
        return total

    def cross_seams(sec):
        made = {}
        for t in range(4):
            chosen = [e for e in range(count) if t in choices[e]]
            if chosen:
                values = jnp.concatenate([rims[e].astype(jnp.float32) for e in chosen], axis=0)
                total = side_dot(values, sec, 0, t)
                for n, e in enumerate(chosen):
                    made[e, t] = total[n * 8:n * 8 + 8]
        for e in range(count):
            value = made[e, choices[e][0]]
            if len(choices[e]) > 1:
                value = jnp.where(table[seconds + my_block * count + e] != 0, made[e, choices[e][1]], value)
            across[e * 8:e * 8 + 8, :] = value

    place_in = lax.broadcasted_iota(jnp.int32, (8, chan), 0)

    def corner_block(other):
        block = jnp.zeros((8, chan), jnp.float32)
        for j in range(most):
            row = across[pl.ds(corner_send[other * most + j], 1), :]
            block = jnp.where(place_in == j, row, block)
        return block

    def send_partial(turn):
        for e, (p, k) in enumerate(edges):
            partial[e] = joined(summed, rim_span(p, k)).astype(jnp.bfloat16)
        for by in range(1, tiles):
            for q in range(slots):
                onward[turn][by - 1, q] = partial[send_rows[(by - 1) * slots + q]]
            onward[turn][by - 1, slots] = corner_block(by).astype(jnp.bfloat16)
            halo_copy(1, turn, by).start()

    def take_corners(turn):
        for by in range(1, tiles):
            corner_rows[(by - 1) * 8:by * 8, :] = gotten[turn][by - 1, slots].astype(jnp.float32)
        corner_rows[local_row:local_row + 8, :] = corner_block(0)

    def ghost(turn, e):
        z = gotten[turn][edge_by[e], edge_slot[e]].astype(jnp.float32) + across[e * 8:e * 8 + 8, :]
        for end in range(2):
            if (e, end) in corners:
                row = corner_rows[pl.ds(corner_place[corners.index((e, end))], 1), :]
                z += jnp.where(place_in == 7 * end, row, 0.0)
        return gelu(z)

    def keep(sec):
        for r in range(side):
            values = joined(hidden, slice(r * rows, (r + 1) * rows)).astype(jnp.bfloat16)
            stage[half + sec, r] = values
            finished[sec, :, r] = values.reshape(whole, 8, chan)[:patches]

        @pl.when(sec == section)
        def _():
            out[0, mine] = finished[sec]

        @pl.when(sec != section)
        def _():
            out_copy(mine, sec).start()

    def tail_copy(n, m):
        start, end, low, high = (early + late)[n]
        span = (slice(start, end), slice(low, high))
        return pltpu.make_async_remote_copy(
            src_ref=finished.at[(sections - 1,) + span], dst_ref=out.at[(0, m) + span],
            send_sem=tail_send.at[n], recv_sem=tail_recv.at[m, n],
            device_id={"section": sections - 1}, device_id_type=MESH,
        )

    def finish(which, begin):
        for start, end, low, high in which:
            for r in range(low, high):
                values = joined(hidden, slice(r * rows + start * 8, r * rows + end * 8))
                finished[sections - 1, start:end, r] = values.reshape(end - start, 8, chan).astype(jnp.bfloat16)
        for n in range(len(which)):
            tail_copy(begin + n, mine).start()

    def interior(sec, layer):
        for r in range(side):
            values = joined(hidden, slice(r * rows, (r + 1) * rows))
            padded[r + 1] = shifted_row(values)
            if r == 0:
                padded[side + 1] = across_row(values, inner[3])
            if r == side - 1:
                padded[0] = across_row(values, inner[2])

        step = 2
        need(sec, layer)

        @pl.loop(0, side // step)
        def _(part):
            r = part * step
            total = jnp.broadcast_to(bias_held[sec, layer:layer + 1, :], (step * rows, chan))
            for i in range(3):
                total += jnp.dot(
                    padded[pl.ds(r + i, step)].reshape(step * rows, 3 * chan),
                    held[sec, layer, i],
                    preferred_element_type=jnp.float32,
                )
            if layer == 0:
                total += jnp.dot(
                    stage[sec, pl.ds(r, step)].reshape(step * rows, chan),
                    skip_held[sec],
                    preferred_element_type=jnp.float32,
                )
            span = pl.ds(pl.multiple_of(r * rows, 8), step * rows)
            split_store(summed, span, total)
            split_store(hidden, span, gelu(total))

    def add_strips(sec, layer, strip):
        for k in (0, 1):
            values = [strip(first_edge[k] + n) for n in range(len(outer[k]))]
            added = side_dot(jnp.concatenate(values, axis=0), sec, layer, k)
            for n, p in enumerate(outer[k]):
                for b in range(chan // LANES):
                    summed[b, rim_span(p, k), :] += added[n * 8:n * 8 + 8, b * LANES:(b + 1) * LANES]
        for k in (2, 3):
            values = [strip(first_edge[k] + n) for n in range(len(outer[k]))]
            added = side_dot(jnp.concatenate(values, axis=0), sec, layer, k)
            top = (k - 2) * (side - 1) * rows
            span = slice(top + outer[k][0] * 8, top + outer[k][-1] * 8 + 8)
            total = joined(summed, span) + added
            split_store(summed, span, total)
            fresh = gelu(total)
            split_store(hidden, span, fresh)
            if layer == LAYERS - 1:
                for n in range(len(outer[k])):
                    rims[first_edge[k] + n] = fresh[n * 8:n * 8 + 8].astype(jnp.bfloat16)
        for k in (0, 1):
            for n, p in enumerate(outer[k]):
                fresh = gelu(joined(summed, rim_span(p, k)))
                split_store(hidden, rim_span(p, k), fresh)
                if layer == LAYERS - 1:
                    rims[first_edge[k] + n] = fresh.astype(jnp.bfloat16)

    def run_section(sec, turn):
        send_rims(turn)

        @pl.when(sec > 0)
        def _():
            keep(sec - 1)
            wait_sent(1 - turn)

        interior(sec, 0)
        cross_seams(sec)
        send_partial(turn)

        for by in range(1, tiles):
            halo_copy(0, turn, by).wait_recv()
        add_strips(sec, 0, lambda e: received[turn][edge_by[e], edge_slot[e]].astype(jnp.float32))

        interior(sec, 1)

        if turn == 1:
            @pl.when(sec == sections - 1)
            def _():
                finish(early, 0)

        for by in range(1, tiles):
            halo_copy(1, turn, by).wait_recv()
        take_corners(turn)
        add_strips(sec, 1, lambda e: ghost(turn, e))

    def send_weights(worker, which):
        for piece in which:
            weight_copy(piece, section, worker).start()

    @pl.when(works)
    def _():
        for piece in (3, 2, 0, 1):
            own_copy(piece).start()

    def send_units(worker):
        for unit in units[0] + units[1]:
            relay_copy(unit, section, worker).start()

    for worker in range(micro):
        @pl.when((section != worker * group) & (mine == worker))
        def _():
            send_weights(worker, (3, 2, 0, 1))

        @pl.when(mine != worker)
        def _():
            send_weights(worker, (3,))

        @pl.when(works & (mine != worker))
        def _():
            send_units(worker)

    relays = lax.rem(section, group) == 1

    def pass_on(source, wanted):
        for unit in wanted:
            relay_copy(unit, source, 0).wait_recv()
            for hop in (1, 0):
                pass_copy(unit, source, hop, 0).start()

    for rank in range(group):
        for worker in range(micro):
            source = worker * group + rank

            @pl.when(relays & (mine != worker))
            def _():
                pass_on(source, (units[0] + units[1])[:-3])
                if rank + 1 < group:
                    pl.semaphore_signal(
                        ready.at[mine], inc=1, device_id={"section": worker * group + rank + 1},
                        device_id_type=MESH,
                    )
                pass_on(source, (units[0] + units[1])[-3:])

        if rank + 1 < group:
            for worker in range(micro):
                @pl.when((lax.rem(section, group) == rank + 1) & (mine != worker))
                def _():
                    pl.semaphore_wait(ready.at[worker], 1)
                    send_units(worker)

    @pl.when(works)
    def _():
        for r in range(side):
            values = states[mine, :, r].astype(jnp.float32)
            if whole != patches:
                values = jnp.concatenate([values, jnp.zeros((whole - patches, 8, chan), jnp.float32)], axis=0)
            values = values.reshape(rows, chan)
            split_store(hidden, slice(r * rows, (r + 1) * rows), values)
            for i in range(half):
                stage[i, r] = values.astype(jnp.bfloat16)
        for e, (p, k) in enumerate(edges):
            rims[e] = joined(hidden, rim_span(p, k)).astype(jnp.bfloat16)

        @pl.loop(0, sections // 2)
        def _(pair):
            for turn in range(2):
                run_section(pair * 2 + turn, turn)

        finish(late, len(early))
        wait_sent(1)

        @pl.loop(0, sections - 1)
        def _(sec):
            @pl.when(sec != section)
            def _():
                out_copy(mine, sec).wait_send()

        for n in range(len(early) + len(late)):
            tail_copy(n, mine).wait_send()

    for worker in range(micro):
        @pl.when(section != worker * group)
        def _():
            weight_copy(3, section, worker).wait_send()

        @pl.when((section != worker * group) & (section != sections - 1))
        def _():
            out_copy(worker, section).wait_recv()

        @pl.when(section == sections - 1)
        def _():
            for n in range(len(early) + len(late)):
                tail_copy(n, worker).wait_recv()

        @pl.when((section != worker * group) & (mine == worker))
        def _():
            for piece in (2, 0, 1):
                weight_copy(piece, section, worker).wait_send()

        @pl.when(mine != worker)
        def _():
            for unit in units[0] + units[1]:
                relay_copy(unit, section, worker).wait_send()

        @pl.when(relays & (mine != worker))
        def _():
            for rank in range(group):
                for unit in units[0] + units[1]:
                    for hop in range(2):
                        pass_copy(unit, worker * group + rank, hop, 0).wait_send()


def on_device(states, conv_weight, skip_weight, bias, placement):
    sections = lax.axis_size("section")
    tiles = lax.axis_size("tile")
    micro, patches, side, _, chan = states.shape
    neighbour, rim_side, flip_flag = seam_tables(PR)
    assert not flip_flag.any()
    inner, outer = edge_plan(neighbour, rim_side, patches)
    early, late = tail_plan(patches, side, outer)
    pieces = early + late
    edges = [(p, k) for k in range(4) for p in outer[k]]
    send_row, _, recv_dev, recv_slot = off_device_routes(neighbour, rim_side, flip_flag, tiles, patches)
    slots = send_row.shape[2]
    number = np.zeros(patches * 4, np.int32)
    for e, (p, k) in enumerate(edges):
        number[p * 4 + k] = e
    take = [p * 4 + k for p, k in edges]
    whole = patches + patches % 2
    rows = whole * side
    corners, most, send, home, place, choices, second = ghost_plan(neighbour, rim_side, patches, outer)
    tables = [
        number[send_row].reshape(-1),
        recv_dev.reshape(tiles, -1)[:, take].reshape(-1),
        recv_slot.reshape(tiles, -1)[:, take].reshape(-1),
        send.reshape(-1), home.reshape(-1), place.reshape(-1), second.reshape(-1),
    ]
    starts = [int(x) for x in np.cumsum([0] + [t.size for t in tables])[:-1]]
    table = np.concatenate(tables)
    weights = conv_weight[0].reshape(LAYERS, 3, 3 * chan, chan)
    held = sections + sections // 2
    smem = pl.BlockSpec(memory_space=pltpu.SMEM)
    vmem = pl.BlockSpec(memory_space=pltpu.VMEM)
    wide = pltpu.VMEM((chan // LANES, side * rows, LANES), jnp.float32)
    got = pltpu.VMEM((tiles - 1, slots, side, chan), jnp.bfloat16)
    more = pltpu.VMEM((tiles - 1, slots + 1, side, chan), jnp.bfloat16)
    flops = 2 * micro * side * rows * chan * chan * (9 * LAYERS + 1)
    return pl.pallas_call(
        functools.partial(window_kernel, tiles, sections, patches, micro, slots, inner, outer, early, late, corners, most, choices, starts),
        out_shape=pltpu.VMEM((1,) + states.shape, jnp.bfloat16),
        in_specs=[smem] * 2 + [vmem, pl.BlockSpec(memory_space=pl.ANY), vmem, vmem],
        out_specs=vmem,
        scratch_shapes=[
            pltpu.VMEM((sections,) + weights.shape, jnp.bfloat16),
            pltpu.VMEM((sections, chan, chan), jnp.bfloat16),
            pltpu.VMEM((sections, 8, chan), jnp.float32),
            pltpu.VMEM((8, chan), jnp.float32),
            pltpu.VMEM((held, side, rows, chan), jnp.bfloat16),
            pltpu.VMEM((sections,) + states.shape[1:], jnp.bfloat16),
            wide, wide,
            pltpu.VMEM((side + 2, rows, 3 * chan), jnp.bfloat16),
            pltpu.VMEM((len(edges), side, chan), jnp.bfloat16),
            pltpu.VMEM((len(edges), side, chan), jnp.bfloat16),
            pltpu.VMEM((len(edges) * side, chan), jnp.float32),
            pltpu.VMEM(((tiles - 1) * 8 + 16, chan), jnp.float32),
            got, got, more, more, got, got, more, more,
            pltpu.SMEM((tiles,), jnp.int32),
            pltpu.SMEM(((tiles - 1) * slots,), jnp.int32),
            pltpu.SMEM((len(edges),), jnp.int32),
            pltpu.SMEM((len(edges),), jnp.int32),
            pltpu.SMEM((tiles * most,), jnp.int32),
            pltpu.SMEM((len(corners),), jnp.int32),
            pltpu.SemaphoreType.DMA((2, 2, tiles - 1)),
            pltpu.SemaphoreType.DMA((2, 2, tiles - 1)),
            pltpu.SemaphoreType.DMA((micro, 4)),
            pltpu.SemaphoreType.DMA((sections, 4)),
            pltpu.SemaphoreType.DMA((4,)),
            pltpu.SemaphoreType.DMA((sections,)),
            pltpu.SemaphoreType.DMA((micro,)),
            pltpu.SemaphoreType.REGULAR((micro,)),
            pltpu.SemaphoreType.DMA((micro, 13)),
            pltpu.SemaphoreType.DMA((sections, 13)),
            pltpu.SemaphoreType.DMA((sections, 2, 13)),
            pltpu.SemaphoreType.DMA((sections, 2, 13)),
            pltpu.SemaphoreType.DMA((len(pieces),)),
            pltpu.SemaphoreType.DMA((micro, len(pieces))),
        ],
        compiler_params=pltpu.CompilerParams(
            collective_id=0, has_side_effects=True, vmem_limit_bytes=56 * 1024 * 1024
        ),
        cost_estimate=pl.CostEstimate(flops=flops, bytes_accessed=2**24, transcendentals=0),
    )(
        placement, jnp.asarray(table, jnp.int32),
        states, weights, skip_weight, bias,
    )


def solution(mesh):
    in_specs = (
        P(None, "tile", None, None, None),
        P("section", None, None, None, None, None),
        P("section", None, None),
        P("section", None, None),
        P(),
    )
    out_specs = P("section", None, "tile", None, None, None)
    return jax.shard_map(
        on_device, mesh=mesh, in_specs=in_specs, out_specs=out_specs, check_vma=False
    )
```

```python
import functools

import jax
import jax.numpy as jnp
import numpy as np
from jax import lax
from jax.experimental import pallas as pl
from jax.experimental.pallas import tpu as pltpu
from jax.sharding import PartitionSpec as P

LAYERS = 2
PR = 4


def face_across(face_num, direction):
    cycle = face_num // 4
    column = face_num % 4
    if cycle == 0:
        table = [4 + column, 4 + (column + 1) % 4, (column + 1) % 4, (column + 3) % 4]
    elif cycle == 1:
        table = [8 + (column + 3) % 4, 8 + column, column, (column + 3) % 4]
    else:
        table = [8 + (column + 3) % 4, 8 + (column + 1) % 4, 4 + (column + 1) % 4, 4 + column]
    return table[direction]


def locate(face_num, coord_x, coord_y, face_span):
    if 0 <= coord_x < face_span and 0 <= coord_y < face_span:
        return (face_num, coord_x, coord_y)
    if coord_x < 0:
        direction = 0
    elif coord_y < 0:
        direction = 1
    elif coord_x >= face_span:
        direction = 2
    else:
        direction = 3
    cycle = face_num // 4
    target = face_across(face_num, direction)
    coord_x = coord_x % face_span
    coord_y = coord_y % face_span
    if cycle == 0 and direction == 2 or (cycle == 2 and direction == 0):
        coord_x, coord_y = (coord_y, face_span - 1 - coord_x)
    elif cycle == 0 and direction == 3 or (cycle == 2 and direction == 1):
        coord_x, coord_y = (face_span - 1 - coord_y, coord_x)
    return (target, coord_x, coord_y)


def seam_tables(tiles):
    cell_side = 2
    face_span = tiles * cell_side
    face_tiles = tiles * tiles
    total = 12 * face_tiles
    neighbour = np.zeros((total, 4), np.int32)
    rim_side = np.zeros((total, 4), np.int32)
    flip_flag = np.zeros((total, 4), np.int32)
    for patch_num in range(total):
        cycle = patch_num % 3
        rest = patch_num // 3
        column = rest // face_tiles
        tile_y = rest % face_tiles // tiles
        tile_x = rest % tiles
        face_num = 4 * cycle + column
        base_x = tile_x * cell_side
        base_y = tile_y * cell_side
        for side_num in range(4):
            found = []
            for step_num in range(2):
                if side_num == 0:
                    point = (base_x - 1, base_y + step_num)
                elif side_num == 1:
                    point = (base_x + cell_side, base_y + step_num)
                elif side_num == 2:
                    point = (base_x + step_num, base_y - 1)
                else:
                    point = (base_x + step_num, base_y + cell_side)
                found.append(locate(face_num, point[0], point[1], face_span))
            face_a, first_x, first_y = found[0]
            face_b, second_x, second_y = found[1]
            neighbour[patch_num, side_num] = (
                3 * (face_a % 4 * face_tiles + first_y // cell_side * tiles + first_x // cell_side)
                + face_a // 4
            )
            if first_x == second_x:
                rim_side[patch_num, side_num] = 0 if first_x % cell_side == 0 else 1
                flip_flag[patch_num, side_num] = 1 if second_y < first_y else 0
            else:
                rim_side[patch_num, side_num] = 2 if first_y % cell_side == 0 else 3
                flip_flag[patch_num, side_num] = 1 if second_x < first_x else 0
    return (neighbour, rim_side, flip_flag)


def off_device_routes(neighbour, rim_side, flip_flag, tile_count, per_dev):
    source_dev = (neighbour // per_dev).reshape(-1)
    dest_dev = np.repeat(np.arange(neighbour.shape[0]) // per_dev, 4)
    row = (neighbour % per_dev * 4 + rim_side).reshape(-1)
    away = source_dev != dest_dev
    slot_num = np.zeros(row.shape[0], np.int64)
    counts = np.zeros((tile_count, tile_count), np.int64)
    for e in np.flatnonzero(away):
        slot_num[e] = counts[source_dev[e], dest_dev[e]]
        counts[source_dev[e], dest_dev[e]] += 1
    send_row = np.zeros((tile_count, tile_count, int(counts.max())), np.int32)
    send_row[source_dev[away], dest_dev[away], slot_num[away]] = row[away]
    place = np.where(away, slot_num, row)
    recv_dev = source_dev.reshape(tile_count, per_dev, 4).astype(np.int32)
    recv_slot = place.reshape(tile_count, per_dev, 4).astype(np.int32)
    return (send_row, None, recv_dev, recv_slot)


MESH = pl.DeviceIdType.MESH
LANES = 128


def edge_plan(neighbour, rim_side, patches):
    blocks = neighbour.shape[0] // patches
    near = neighbour.reshape(blocks, patches, 4) // patches
    home = near == np.arange(blocks)[:, None, None]
    inner = [[None] * patches for _ in range(4)]
    outer = [[] for _ in range(4)]
    for p in range(patches):
        for k in range(4):
            local = neighbour.reshape(blocks, patches, 4)[:, p, k] % patches
            same = home[:, p, k].all() and (local == local[0]).all()
            facing = (rim_side.reshape(blocks, patches, 4)[:, p, k] == (k ^ 1)).all()
            if same and facing:
                inner[k][p] = int(local[0])
            else:
                assert not home[:, p, k].any()
                outer[k].append(p)
    for k in (2, 3):
        assert outer[k] == list(range(outer[k][0], outer[k][-1] + 1))
    return inner, outer


def ghost_plan(neighbour, rim_side, patches, outer):
    blocks = neighbour.shape[0] // patches
    edges = [(p, k) for k in range(4) for p in outer[k]]
    number = {edge: e for e, edge in enumerate(edges)}
    facing = np.zeros((blocks, len(edges)), np.int32)
    sent = [[[] for _ in range(blocks)] for _ in range(blocks)]
    found = {}
    for b in range(blocks):
        for e, (p, k) in enumerate(edges):
            q, t = neighbour[b * patches + p, k], rim_side[b * patches + p, k]
            facing[b, e] = t
            for end in range(2):
                across = (2 if t < 2 else 0) + end
                if (q % patches, across) in number:
                    other, side = neighbour[q, across], rim_side[q, across]
                    home = other // patches
                    row = number[(other % patches, side)] * 8 + (0 if t in (0, 2) else 7)
                    found[(b, e, end)] = (home, len(sent[home][b]))
                    sent[home][b].append(row)
    corners = sorted({(e, end) for _, e, end in found})
    most = max(len(x) for line in sent for x in line)
    assert most <= 8
    send = np.zeros((blocks, blocks, most), np.int32)
    for a in range(blocks):
        for b in range(blocks):
            send[a, b, :len(sent[a][b])] = sent[a][b]
    home = np.full((blocks, len(corners)), -1, np.int32)
    place = np.zeros((blocks, len(corners)), np.int32)
    for n, (e, end) in enumerate(corners):
        for b in range(blocks):
            if (b, e, end) in found:
                home[b, n], place[b, n] = found[(b, e, end)]
    choices = [sorted(set(facing[:, e].tolist())) for e in range(len(edges))]
    assert all(len(c) <= 2 for c in choices)
    second = np.stack([(facing[:, e] != choices[e][0]).astype(np.int32) for e in range(len(edges))], axis=1)
    return corners, most, send, home, place, choices, second


def tail_plan(patches, side, outer):
    early, late = [], []
    for p in range(patches):
        low = 1 if p in outer[2] else 0
        high = side - 1 if p in outer[3] else side
        clean = p not in outer[0] and p not in outer[1]
        for spans, low_row, high_row in ((early if clean else late, low, high), (late, 0, low), (late, high, side)):
            if low_row < high_row:
                spans.append((p, p + 1, low_row, high_row))
    plans = []
    for spans in (early, late):
        merged = []
        for p, end, low, high in sorted(spans, key=lambda piece: (piece[2], piece[3], piece[0])):
            if merged and merged[-1][1] == p and merged[-1][2:] == (low, high):
                merged[-1] = (merged[-1][0], end, low, high)
            else:
                merged.append((p, end, low, high))
        plans.append(merged)
    return plans


def joined(ref, span):
    return jnp.concatenate([ref[b, span, :] for b in range(ref.shape[0])], axis=1)


def split_store(ref, span, value):
    for b in range(ref.shape[0]):
        ref[b, span, :] = value[:, b * LANES:(b + 1) * LANES]


def window_kernel(
    tiles, sections, patches, micro, slots, inner, outer, early, late, corners, most, choices, starts,
    placement, table,
    states, weights, skip_w, biases,
    out,
    held, skip_held, bias_held, bias_own, given, stage, finished, hidden, summed, padded, rims, partial, across, corner_rows,
    outgoing_0, outgoing_1, onward_0, onward_1, received_0, received_1, gotten_0, gotten_1,
    behind, send_rows, edge_by, edge_slot, corner_send, corner_place,
    halo_send, halo_recv, weight_send, weight_recv, own_sem, out_send, out_recv, ready,
    relay_send, relay_recv, pass_send, pass_recv, tail_send, tail_recv, given_sem,
):
    tile = lax.axis_index("tile")
    section = lax.axis_index("section")
    half = sections // 2
    side = states.shape[2]
    chan = states.shape[4]
    rows = stage.shape[2]
    whole = rows // side
    outgoing, onward = (outgoing_0, outgoing_1), (onward_0, onward_1)
    received, gotten = (received_0, received_1), (gotten_0, gotten_1)
    edges = [(p, k) for k in range(4) for p in outer[k]]
    first_edge = [sum(len(outer[j]) for j in range(k)) for k in range(4)]

    def tile_at(by):
        return lax.rem(tile + by, tiles)

    partner = tile + 1 - 2 * lax.rem(tile, 2)
    partner_z = tile + 2 - 4 * lax.rem(tile // 2, 2)
    barrier = pltpu.get_barrier_semaphore()
    for by in range(1, tiles):
        pl.semaphore_signal(barrier, inc=1, device_id={"tile": tile_at(by)}, device_id_type=MESH)
    for by in range(1, sections):
        pl.semaphore_signal(
            barrier, inc=1, device_id={"section": lax.rem(section + by, sections)}, device_id_type=MESH
        )
        pl.semaphore_signal(
            barrier, inc=1, device_id={"tile": partner, "section": lax.rem(section + by, sections)},
            device_id_type=MESH,
        )
        pl.semaphore_signal(
            barrier, inc=1, device_id={"tile": partner_z, "section": lax.rem(section + by, sections)},
            device_id_type=MESH,
        )

    group = sections // micro
    works = lax.rem(section, group) == 0
    mine = section // group
    fetch = pltpu.make_async_copy(states.at[mine], given, given_sem.at[0])

    @pl.when(works)
    def _():
        fetch.start()

    bias_own[...] = jnp.zeros_like(bias_own)
    bias_own[0:LAYERS, :] = biases[0].astype(jnp.float32)

    assert group > 1 and tiles % 4 == 0 and sections % 2 == 0 and LAYERS == 2
    my_block = placement[tile]
    count = len(edges)
    sends, sources, places, corner_sends, corner_homes, corner_places, seconds = starts

    def find(block, _):
        def one(by, found):
            here = placement[lax.rem(tile - by + tiles, tiles)]
            return jnp.where(here == block, by, found)

        behind[block] = lax.fori_loop(0, tiles, one, jnp.int32(0))
        return 0

    local_row = (tiles - 1) * 8
    blank_row = local_row + 8
    corner_rows[blank_row:blank_row + 8, :] = jnp.zeros((8, chan), jnp.float32)

    lax.fori_loop(0, tiles, find, 0)

    def route(e, _):
        edge_by[e] = behind[table[sources + my_block * count + e]] - 1
        edge_slot[e] = table[places + my_block * count + e]
        return 0

    lax.fori_loop(0, count, route, 0)

    def fill(i, _):
        other = placement[tile_at(i // slots + 1)]
        send_rows[i] = table[sends + (my_block * tiles + other) * slots + lax.rem(i, slots)]
        return 0

    lax.fori_loop(0, (tiles - 1) * slots, fill, 0)

    def fill_corner(i, _):
        other = placement[tile_at(i // most)]
        corner_send[i] = table[corner_sends + (my_block * tiles + other) * most + lax.rem(i, most)]
        return 0

    lax.fori_loop(0, tiles * most, fill_corner, 0)

    def place_corner(n, _):
        home = table[corner_homes + my_block * len(corners) + n]
        by = behind[jnp.maximum(home, 0)]
        row = table[corner_places + my_block * len(corners) + n]
        row += jnp.where(by == 0, local_row, (by - 1) * 8)
        corner_place[n] = jnp.where(home < 0, blank_row, row)
        return 0

    lax.fori_loop(0, len(corners), place_corner, 0)

    pl.semaphore_wait(barrier, tiles - 1 + 3 * (sections - 1))

    column = lax.broadcasted_iota(jnp.int32, (whole, 8, chan), 1)
    first = column == 0
    last = column == 7

    def halo_copy(wave, turn, by):
        source, target = ((outgoing, received), (onward, gotten))[wave]
        return pltpu.make_async_remote_copy(
            src_ref=source[turn].at[by - 1],
            dst_ref=target[turn].at[by - 1],
            send_sem=halo_send.at[turn, wave, by - 1],
            recv_sem=halo_recv.at[turn, wave, by - 1],
            device_id={"tile": tile_at(by)},
            device_id_type=MESH,
        )

    pieces = (
        (weights.at[0], held, 0), (weights.at[1], held, 1), (skip_w.at[0], skip_held, None), (bias_own, bias_held, None)
    )

    def weight_copy(piece, source, worker):
        src, dst, layer = pieces[piece]
        return pltpu.make_async_remote_copy(
            src_ref=src,
            dst_ref=dst.at[source] if layer is None else dst.at[source, layer],
            send_sem=weight_send.at[worker, piece],
            recv_sem=weight_recv.at[source, piece],
            device_id={"section": worker * group},
            device_id_type=MESH,
        )

    def own_copy(piece):
        src, dst, layer = pieces[piece]
        return pltpu.make_async_copy(
            src, dst.at[section] if layer is None else dst.at[section, layer], own_sem.at[piece]
        )

    def out_copy(m, sec):
        return pltpu.make_async_remote_copy(
            src_ref=finished.at[sec], dst_ref=out.at[0, m],
            send_sem=out_send.at[sec], recv_sem=out_recv.at[m],
            device_id={"section": sec}, device_id_type=MESH,
        )

    units = {0: list(range(7)), 1: list(range(7, 13))}

    def unit_span(unit, other):
        if unit == 0:
            deep = chan // 2
            return (pl.ds(pl.multiple_of(lax.rem(tile + other, 2) * deep, LANES), deep),)
        layer, rest = (unit - 1) // 6, (unit - 1) % 6
        deep = 3 * chan // 4
        if by_z(unit):
            start = lax.rem(tile // 2 + other, 2) * deep
        else:
            start = 2 * deep + lax.rem(tile + other, 2) * deep
        return (layer, rest // 2, pl.ds(pl.multiple_of(start, 64), deep))

    def by_z(unit):
        return unit > 0 and unit % 2 == 0

    def place_of(unit, source, other):
        return (skip_held if unit == 0 else held).at[(source,) + unit_span(unit, other)]

    def relay_copy(unit, source, worker):
        own = (skip_w.at[0] if unit == 0 else weights).at[unit_span(unit, 0)]
        return pltpu.make_async_remote_copy(
            src_ref=own, dst_ref=place_of(unit, source, 0),
            send_sem=relay_send.at[worker, unit], recv_sem=relay_recv.at[source, unit],
            device_id={"section": worker * group + 1}, device_id_type=MESH,
        )

    def pass_copy(unit, source, hop, other):
        place = place_of(unit, source, other)
        device = {"section": mine * group}
        if hop == 1:
            device["tile"] = partner_z if by_z(unit) else partner
        return pltpu.make_async_remote_copy(
            src_ref=place, dst_ref=place,
            send_sem=pass_send.at[source, hop, unit], recv_sem=pass_recv.at[source, hop, unit],
            device_id=device, device_id_type=MESH,
        )

    def need(sec, layer):
        near = sec // group == mine
        for piece in ((3, 2, 0) if layer == 0 else (1,)):
            @pl.when(sec == section)
            def _():
                own_copy(piece).wait()

            @pl.when((sec != section) & (True if piece == 3 else near))
            def _():
                weight_copy(piece, sec, 0).wait_recv()

        @pl.when(jnp.logical_not(near))
        def _():
            for unit in units[layer]:
                for hop in range(2):
                    pass_copy(unit, sec, hop, hop).wait_recv()

    def gelu(z):
        return 0.5 * z * (1.0 + lax.erf(z * np.float32(0.5 ** 0.5)))

    def rolled(values, by):
        return pltpu.roll(values.reshape(values.shape[0] // 8, 8, chan), by, 1)

    def strided(values):
        height = values.shape[0]
        lower = jnp.where(first[:height // 8], 0.0, rolled(values, 1)).reshape(height, chan)
        upper = jnp.where(last[:height // 8], 0.0, rolled(values, 7)).reshape(height, chan)
        return jnp.concatenate([lower, values, upper], axis=1)

    def picked(cells, chosen):
        blank = jnp.zeros((1,) + cells.shape[1:], cells.dtype)
        parts = [blank if q is None else cells[q:q + 1] for q in chosen]
        parts += [blank] * (whole - len(chosen))
        return jnp.concatenate(parts, axis=0)

    def shifted_row(values):
        lower, upper = rolled(values, 1), rolled(values, 7)
        lower = jnp.where(first, picked(lower, inner[0]), lower).reshape(rows, chan)
        upper = jnp.where(last, picked(upper, inner[1]), upper).reshape(rows, chan)
        return jnp.concatenate([lower, values, upper], axis=1).astype(jnp.bfloat16)

    def across_row(values, chosen):
        moved = strided(values).reshape(whole, 8, 3 * chan)
        return picked(moved, chosen).reshape(rows, 3 * chan).astype(jnp.bfloat16)

    def rim_span(p, k):
        if k < 2:
            return pl.ds(p * 8 + 7 * k, 8, stride=rows)
        top = (k - 2) * (side - 1) * rows
        return slice(top + p * 8, top + p * 8 + 8)

    order = list(range(1, tiles))

    def send_rims(turn):
        for by in order:
            for q in range(slots):
                outgoing[turn][by - 1, q] = rims[send_rows[(by - 1) * slots + q]]
            halo_copy(0, turn, by).start()

    def wait_sent(turn):
        for wave in range(2):
            for by in range(1, tiles):
                halo_copy(wave, turn, by).wait_send()

    def side_dot(values, sec, layer, k):
        moved = strided(values).astype(jnp.bfloat16)
        if k >= 2:
            return jnp.dot(moved, held[sec, layer, k * 2 - 4], preferred_element_type=jnp.float32)
        total = jnp.zeros((values.shape[0], chan), jnp.float32)
        for i in range(3):
            total += jnp.dot(
                moved[:, i * chan:(i + 1) * chan],
                held[sec, layer, i, k * 2 * chan:(k * 2 + 1) * chan],
                preferred_element_type=jnp.float32,
            )
        return total

    def cross_seams(sec):
        made = {}
        for t in range(4):
            chosen = [e for e in range(count) if t in choices[e]]
            if chosen:
                values = jnp.concatenate([rims[e].astype(jnp.float32) for e in chosen], axis=0)
                total = side_dot(values, sec, 0, t)
                for n, e in enumerate(chosen):
                    made[e, t] = total[n * 8:n * 8 + 8]
        for e in range(count):
            value = made[e, choices[e][0]]
            if len(choices[e]) > 1:
                value = jnp.where(table[seconds + my_block * count + e] != 0, made[e, choices[e][1]], value)
            across[e * 8:e * 8 + 8, :] = value

    place_in = lax.broadcasted_iota(jnp.int32, (8, chan), 0)

    def corner_block(other):
        block = jnp.zeros((8, chan), jnp.float32)
        for j in range(most):
            row = across[pl.ds(corner_send[other * most + j], 1), :]
            block = jnp.where(place_in == j, row, block)
        return block

    def send_partial(turn):
        for e, (p, k) in enumerate(edges):
            partial[e] = joined(summed, rim_span(p, k)).astype(jnp.bfloat16)
        for by in order:
            for q in range(slots):
                onward[turn][by - 1, q] = partial[send_rows[(by - 1) * slots + q]]
            onward[turn][by - 1, slots] = corner_block(by).astype(jnp.bfloat16)
            halo_copy(1, turn, by).start()

    def take_corners(turn):
        for by in range(1, tiles):
            corner_rows[(by - 1) * 8:by * 8, :] = gotten[turn][by - 1, slots].astype(jnp.float32)

    def ghost(turn, e):
        z = gotten[turn][edge_by[e], edge_slot[e]].astype(jnp.float32) + across[e * 8:e * 8 + 8, :]
        for end in range(2):
            if (e, end) in corners:
                row = corner_rows[pl.ds(corner_place[corners.index((e, end))], 1), :]
                z += jnp.where(place_in == 7 * end, row, 0.0)
        return gelu(z)

    def keep(sec):
        for r in range(side):
            values = joined(hidden, slice(r * rows, (r + 1) * rows)).astype(jnp.bfloat16)
            stage[half + sec, r] = values
            finished[sec, :, r] = values.reshape(whole, 8, chan)[:patches]

        @pl.when(sec == section)
        def _():
            out[0, mine] = finished[sec]

        @pl.when(sec != section)
        def _():
            out_copy(mine, sec).start()

    def tail_copy(n, m):
        start, end, low, high = (early + late)[n]
        span = (slice(start, end), slice(low, high))
        return pltpu.make_async_remote_copy(
            src_ref=finished.at[(sections - 1,) + span], dst_ref=out.at[(0, m) + span],
            send_sem=tail_send.at[n], recv_sem=tail_recv.at[m, n],
            device_id={"section": sections - 1}, device_id_type=MESH,
        )

    def finish(which, begin):
        for start, end, low, high in which:
            for r in range(low, high):
                values = joined(hidden, slice(r * rows + start * 8, r * rows + end * 8))
                finished[sections - 1, start:end, r] = values.reshape(end - start, 8, chan).astype(jnp.bfloat16)
        for n in range(len(which)):
            tail_copy(begin + n, mine).start()

    def interior(sec, layer):
        for r in range(side):
            values = joined(hidden, slice(r * rows, (r + 1) * rows))
            padded[r + 1] = shifted_row(values)
            if r == 0:
                padded[side + 1] = across_row(values, inner[3])
            if r == side - 1:
                padded[0] = across_row(values, inner[2])

        step = 2
        need(sec, layer)

        @pl.loop(0, side // step)
        def _(part):
            r = part * step
            total = jnp.broadcast_to(bias_held[sec, layer:layer + 1, :], (step * rows, chan))
            for i in range(3):
                total += jnp.dot(
                    padded[pl.ds(r + i, step)].reshape(step * rows, 3 * chan),
                    held[sec, layer, i],
                    preferred_element_type=jnp.float32,
                )
            if layer == 0:
                total += jnp.dot(
                    stage[sec, pl.ds(r, step)].reshape(step * rows, chan),
                    skip_held[sec],
                    preferred_element_type=jnp.float32,
                )
            span = pl.ds(pl.multiple_of(r * rows, 8), step * rows)
            split_store(summed, span, total)
            split_store(hidden, span, gelu(total))

    def add_strips(sec, layer, strip):
        for k in (0, 1):
            values = [strip(first_edge[k] + n) for n in range(len(outer[k]))]
            added = side_dot(jnp.concatenate(values, axis=0), sec, layer, k)
            for n, p in enumerate(outer[k]):
                for b in range(chan // LANES):
                    summed[b, rim_span(p, k), :] += added[n * 8:n * 8 + 8, b * LANES:(b + 1) * LANES]
        for k in (2, 3):
            values = [strip(first_edge[k] + n) for n in range(len(outer[k]))]
            added = side_dot(jnp.concatenate(values, axis=0), sec, layer, k)
            top = (k - 2) * (side - 1) * rows
            span = slice(top + outer[k][0] * 8, top + outer[k][-1] * 8 + 8)
            total = joined(summed, span) + added
            split_store(summed, span, total)
            fresh = gelu(total)
            split_store(hidden, span, fresh)
            if layer == LAYERS - 1:
                for n in range(len(outer[k])):
                    rims[first_edge[k] + n] = fresh[n * 8:n * 8 + 8].astype(jnp.bfloat16)
        for k in (0, 1):
            for n, p in enumerate(outer[k]):
                fresh = gelu(joined(summed, rim_span(p, k)))
                split_store(hidden, rim_span(p, k), fresh)
                if layer == LAYERS - 1:
                    rims[first_edge[k] + n] = fresh.astype(jnp.bfloat16)

    def run_section(sec, turn):
        send_rims(turn)

        @pl.when(sec > 0)
        def _():
            keep(sec - 1)
            wait_sent(1 - turn)

        interior(sec, 0)
        cross_seams(sec)
        send_partial(turn)
        corner_rows[local_row:local_row + 8, :] = corner_block(0)

        for by in range(1, tiles):
            halo_copy(0, turn, by).wait_recv()
        add_strips(sec, 0, lambda e: received[turn][edge_by[e], edge_slot[e]].astype(jnp.float32))

        interior(sec, 1)

        if turn == 1:
            @pl.when(sec == sections - 1)
            def _():
                finish(early, 0)

        for by in range(1, tiles):
            halo_copy(1, turn, by).wait_recv()
        take_corners(turn)
        add_strips(sec, 1, lambda e: ghost(turn, e))

    def send_weights(worker, which):
        for piece in which:
            weight_copy(piece, section, worker).start()

    @pl.when(works)
    def _():
        for piece in (3, 2, 0, 1):
            own_copy(piece).start()

    def send_units(worker):
        for unit in units[0] + units[1]:
            relay_copy(unit, section, worker).start()

    for worker in range(micro):
        @pl.when((section != worker * group) & (mine == worker))
        def _():
            send_weights(worker, (3, 2, 0, 1))

        @pl.when(mine != worker)
        def _():
            send_weights(worker, (3,))

        @pl.when(works & (mine != worker))
        def _():
            send_units(worker)

    relays = lax.rem(section, group) == 1

    def pass_on(source, wanted):
        for unit in wanted:
            relay_copy(unit, source, 0).wait_recv()
            for hop in (1, 0):
                pass_copy(unit, source, hop, 0).start()

    for rank in range(group):
        for worker in range(micro):
            source = worker * group + rank

            @pl.when(relays & (mine != worker))
            def _():
                pass_on(source, (units[0] + units[1])[:-5])
                if rank + 1 < group:
                    pl.semaphore_signal(
                        ready.at[mine], inc=1, device_id={"section": worker * group + rank + 1},
                        device_id_type=MESH,
                    )
                pass_on(source, (units[0] + units[1])[-5:])

        if rank + 1 < group:
            for worker in range(micro):
                @pl.when((lax.rem(section, group) == rank + 1) & (mine != worker))
                def _():
                    pl.semaphore_wait(ready.at[worker], 1)
                    send_units(worker)

    @pl.when(works)
    def _():
        fetch.wait()
        for r in range(side):
            values = given[:, r].astype(jnp.float32)
            if whole != patches:
                values = jnp.concatenate([values, jnp.zeros((whole - patches, 8, chan), jnp.float32)], axis=0)
            values = values.reshape(rows, chan)
            split_store(hidden, slice(r * rows, (r + 1) * rows), values)
            for i in range(half):
                stage[i, r] = values.astype(jnp.bfloat16)
        for e, (p, k) in enumerate(edges):
            rims[e] = joined(hidden, rim_span(p, k)).astype(jnp.bfloat16)

        @pl.loop(0, sections // 2)
        def _(pair):
            for turn in range(2):
                run_section(pair * 2 + turn, turn)

        finish(late, len(early))
        wait_sent(1)

        @pl.loop(0, sections - 1)
        def _(sec):
            @pl.when(sec != section)
            def _():
                out_copy(mine, sec).wait_send()

        for n in range(len(early) + len(late)):
            tail_copy(n, mine).wait_send()

    for worker in range(micro):
        @pl.when(section != worker * group)
        def _():
            weight_copy(3, section, worker).wait_send()

        @pl.when((section != worker * group) & (section != sections - 1))
        def _():
            out_copy(worker, section).wait_recv()

        @pl.when(section == sections - 1)
        def _():
            for n in range(len(early) + len(late)):
                tail_copy(n, worker).wait_recv()

        @pl.when((section != worker * group) & (mine == worker))
        def _():
            for piece in (2, 0, 1):
                weight_copy(piece, section, worker).wait_send()

        @pl.when(mine != worker)
        def _():
            for unit in units[0] + units[1]:
                relay_copy(unit, section, worker).wait_send()

        @pl.when(relays & (mine != worker))
        def _():
            for rank in range(group):
                for unit in units[0] + units[1]:
                    for hop in range(2):
                        pass_copy(unit, worker * group + rank, hop, 0).wait_send()


def on_device(states, conv_weight, skip_weight, bias, placement):
    sections = lax.axis_size("section")
    tiles = lax.axis_size("tile")
    micro, patches, side, _, chan = states.shape
    neighbour, rim_side, flip_flag = seam_tables(PR)
    assert not flip_flag.any()
    inner, outer = edge_plan(neighbour, rim_side, patches)
    early, late = tail_plan(patches, side, outer)
    pieces = early + late
    edges = [(p, k) for k in range(4) for p in outer[k]]
    send_row, _, recv_dev, recv_slot = off_device_routes(neighbour, rim_side, flip_flag, tiles, patches)
    slots = send_row.shape[2]
    number = np.zeros(patches * 4, np.int32)
    for e, (p, k) in enumerate(edges):
        number[p * 4 + k] = e
    take = [p * 4 + k for p, k in edges]
    whole = patches + patches % 2
    rows = whole * side
    corners, most, send, home, place, choices, second = ghost_plan(neighbour, rim_side, patches, outer)
    tables = [
        number[send_row].reshape(-1),
        recv_dev.reshape(tiles, -1)[:, take].reshape(-1),
        recv_slot.reshape(tiles, -1)[:, take].reshape(-1),
        send.reshape(-1), home.reshape(-1), place.reshape(-1), second.reshape(-1),
    ]
    starts = [int(x) for x in np.cumsum([0] + [t.size for t in tables])[:-1]]
    table = np.concatenate(tables)
    weights = conv_weight[0].reshape(LAYERS, 3, 3 * chan, chan)
    held = sections + sections // 2
    smem = pl.BlockSpec(memory_space=pltpu.SMEM)
    vmem = pl.BlockSpec(memory_space=pltpu.VMEM)
    wide = pltpu.VMEM((chan // LANES, side * rows, LANES), jnp.float32)
    got = pltpu.VMEM((tiles - 1, slots, side, chan), jnp.bfloat16)
    more = pltpu.VMEM((tiles - 1, slots + 1, side, chan), jnp.bfloat16)
    flops = 2 * micro * side * rows * chan * chan * (9 * LAYERS + 1)
    return pl.pallas_call(
        functools.partial(window_kernel, tiles, sections, patches, micro, slots, inner, outer, early, late, corners, most, choices, starts),
        out_shape=pltpu.VMEM((1,) + states.shape, jnp.bfloat16),
        in_specs=[smem] * 2 + [pl.BlockSpec(memory_space=pl.ANY)] * 2 + [vmem, vmem],
        out_specs=vmem,
        scratch_shapes=[
            pltpu.VMEM((sections,) + weights.shape, jnp.bfloat16),
            pltpu.VMEM((sections, chan, chan), jnp.bfloat16),
            pltpu.VMEM((sections, 8, chan), jnp.float32),
            pltpu.VMEM((8, chan), jnp.float32),
            pltpu.VMEM(states.shape[1:], jnp.bfloat16),
            pltpu.VMEM((held, side, rows, chan), jnp.bfloat16),
            pltpu.VMEM((sections,) + states.shape[1:], jnp.bfloat16),
            wide, wide,
            pltpu.VMEM((side + 2, rows, 3 * chan), jnp.bfloat16),
            pltpu.VMEM((len(edges), side, chan), jnp.bfloat16),
            pltpu.VMEM((len(edges), side, chan), jnp.bfloat16),
            pltpu.VMEM((len(edges) * side, chan), jnp.float32),
            pltpu.VMEM(((tiles - 1) * 8 + 16, chan), jnp.float32),
            got, got, more, more, got, got, more, more,
            pltpu.SMEM((tiles,), jnp.int32),
            pltpu.SMEM(((tiles - 1) * slots,), jnp.int32),
            pltpu.SMEM((len(edges),), jnp.int32),
            pltpu.SMEM((len(edges),), jnp.int32),
            pltpu.SMEM((tiles * most,), jnp.int32),
            pltpu.SMEM((len(corners),), jnp.int32),
            pltpu.SemaphoreType.DMA((2, 2, tiles - 1)),
            pltpu.SemaphoreType.DMA((2, 2, tiles - 1)),
            pltpu.SemaphoreType.DMA((micro, 4)),
            pltpu.SemaphoreType.DMA((sections, 4)),
            pltpu.SemaphoreType.DMA((4,)),
            pltpu.SemaphoreType.DMA((sections,)),
            pltpu.SemaphoreType.DMA((micro,)),
            pltpu.SemaphoreType.REGULAR((micro,)),
            pltpu.SemaphoreType.DMA((micro, 13)),
            pltpu.SemaphoreType.DMA((sections, 13)),
            pltpu.SemaphoreType.DMA((sections, 2, 13)),
            pltpu.SemaphoreType.DMA((sections, 2, 13)),
            pltpu.SemaphoreType.DMA((len(pieces),)),
            pltpu.SemaphoreType.DMA((micro, len(pieces))),
            pltpu.SemaphoreType.DMA((1,)),
        ],
        compiler_params=pltpu.CompilerParams(
            collective_id=0, has_side_effects=True, vmem_limit_bytes=56 * 1024 * 1024
        ),
        cost_estimate=pl.CostEstimate(flops=flops, bytes_accessed=2**24, transcendentals=0),
    )(
        placement, jnp.asarray(table, jnp.int32),
        states, weights, skip_weight, bias,
    )


def solution(mesh):
    in_specs = (
        P(None, "tile", None, None, None),
        P("section", None, None, None, None, None),
        P("section", None, None),
        P("section", None, None),
        P(),
    )
    out_specs = P("section", None, "tile", None, None, None)
    return jax.shard_map(
        on_device, mesh=mesh, in_specs=in_specs, out_specs=out_specs, check_vma=False
    )
```

```python
import functools

import jax
import jax.numpy as jnp
import numpy as np
from jax import lax
from jax.experimental import pallas as pl
from jax.experimental.pallas import tpu as pltpu
from jax.sharding import PartitionSpec as P

LAYERS = 2
PR = 4


def face_across(face_num, direction):
    cycle = face_num // 4
    column = face_num % 4
    if cycle == 0:
        table = [4 + column, 4 + (column + 1) % 4, (column + 1) % 4, (column + 3) % 4]
    elif cycle == 1:
        table = [8 + (column + 3) % 4, 8 + column, column, (column + 3) % 4]
    else:
        table = [8 + (column + 3) % 4, 8 + (column + 1) % 4, 4 + (column + 1) % 4, 4 + column]
    return table[direction]


def locate(face_num, coord_x, coord_y, face_span):
    if 0 <= coord_x < face_span and 0 <= coord_y < face_span:
        return (face_num, coord_x, coord_y)
    if coord_x < 0:
        direction = 0
    elif coord_y < 0:
        direction = 1
    elif coord_x >= face_span:
        direction = 2
    else:
        direction = 3
    cycle = face_num // 4
    target = face_across(face_num, direction)
    coord_x = coord_x % face_span
    coord_y = coord_y % face_span
    if cycle == 0 and direction == 2 or (cycle == 2 and direction == 0):
        coord_x, coord_y = (coord_y, face_span - 1 - coord_x)
    elif cycle == 0 and direction == 3 or (cycle == 2 and direction == 1):
        coord_x, coord_y = (face_span - 1 - coord_y, coord_x)
    return (target, coord_x, coord_y)


def seam_tables(tiles):
    cell_side = 2
    face_span = tiles * cell_side
    face_tiles = tiles * tiles
    total = 12 * face_tiles
    neighbour = np.zeros((total, 4), np.int32)
    rim_side = np.zeros((total, 4), np.int32)
    flip_flag = np.zeros((total, 4), np.int32)
    for patch_num in range(total):
        cycle = patch_num % 3
        rest = patch_num // 3
        column = rest // face_tiles
        tile_y = rest % face_tiles // tiles
        tile_x = rest % tiles
        face_num = 4 * cycle + column
        base_x = tile_x * cell_side
        base_y = tile_y * cell_side
        for side_num in range(4):
            found = []
            for step_num in range(2):
                if side_num == 0:
                    point = (base_x - 1, base_y + step_num)
                elif side_num == 1:
                    point = (base_x + cell_side, base_y + step_num)
                elif side_num == 2:
                    point = (base_x + step_num, base_y - 1)
                else:
                    point = (base_x + step_num, base_y + cell_side)
                found.append(locate(face_num, point[0], point[1], face_span))
            face_a, first_x, first_y = found[0]
            face_b, second_x, second_y = found[1]
            neighbour[patch_num, side_num] = (
                3 * (face_a % 4 * face_tiles + first_y // cell_side * tiles + first_x // cell_side)
                + face_a // 4
            )
            if first_x == second_x:
                rim_side[patch_num, side_num] = 0 if first_x % cell_side == 0 else 1
                flip_flag[patch_num, side_num] = 1 if second_y < first_y else 0
            else:
                rim_side[patch_num, side_num] = 2 if first_y % cell_side == 0 else 3
                flip_flag[patch_num, side_num] = 1 if second_x < first_x else 0
    return (neighbour, rim_side, flip_flag)


def off_device_routes(neighbour, rim_side, flip_flag, tile_count, per_dev):
    source_dev = (neighbour // per_dev).reshape(-1)
    dest_dev = np.repeat(np.arange(neighbour.shape[0]) // per_dev, 4)
    row = (neighbour % per_dev * 4 + rim_side).reshape(-1)
    away = source_dev != dest_dev
    slot_num = np.zeros(row.shape[0], np.int64)
    counts = np.zeros((tile_count, tile_count), np.int64)
    for e in np.flatnonzero(away):
        slot_num[e] = counts[source_dev[e], dest_dev[e]]
        counts[source_dev[e], dest_dev[e]] += 1
    send_row = np.zeros((tile_count, tile_count, int(counts.max())), np.int32)
    send_row[source_dev[away], dest_dev[away], slot_num[away]] = row[away]
    place = np.where(away, slot_num, row)
    recv_dev = source_dev.reshape(tile_count, per_dev, 4).astype(np.int32)
    recv_slot = place.reshape(tile_count, per_dev, 4).astype(np.int32)
    return (send_row, None, recv_dev, recv_slot)


MESH = pl.DeviceIdType.MESH
LANES = 128


def edge_plan(neighbour, rim_side, patches):
    blocks = neighbour.shape[0] // patches
    near = neighbour.reshape(blocks, patches, 4) // patches
    home = near == np.arange(blocks)[:, None, None]
    inner = [[None] * patches for _ in range(4)]
    outer = [[] for _ in range(4)]
    for p in range(patches):
        for k in range(4):
            local = neighbour.reshape(blocks, patches, 4)[:, p, k] % patches
            same = home[:, p, k].all() and (local == local[0]).all()
            facing = (rim_side.reshape(blocks, patches, 4)[:, p, k] == (k ^ 1)).all()
            if same and facing:
                inner[k][p] = int(local[0])
            else:
                assert not home[:, p, k].any()
                outer[k].append(p)
    for k in (2, 3):
        assert outer[k] == list(range(outer[k][0], outer[k][-1] + 1))
    return inner, outer


def ghost_plan(neighbour, rim_side, patches, outer):
    blocks = neighbour.shape[0] // patches
    edges = [(p, k) for k in range(4) for p in outer[k]]
    number = {edge: e for e, edge in enumerate(edges)}
    facing = np.zeros((blocks, len(edges)), np.int32)
    sent = [[[] for _ in range(blocks)] for _ in range(blocks)]
    found = {}
    for b in range(blocks):
        for e, (p, k) in enumerate(edges):
            q, t = neighbour[b * patches + p, k], rim_side[b * patches + p, k]
            facing[b, e] = t
            for end in range(2):
                across = (2 if t < 2 else 0) + end
                if (q % patches, across) in number:
                    other, side = neighbour[q, across], rim_side[q, across]
                    home = other // patches
                    row = number[(other % patches, side)] * 8 + (0 if t in (0, 2) else 7)
                    found[(b, e, end)] = (home, len(sent[home][b]))
                    sent[home][b].append(row)
    corners = sorted({(e, end) for _, e, end in found})
    most = max(len(x) for line in sent for x in line)
    assert most <= 8
    send = np.zeros((blocks, blocks, most), np.int32)
    for a in range(blocks):
        for b in range(blocks):
            send[a, b, :len(sent[a][b])] = sent[a][b]
    home = np.full((blocks, len(corners)), -1, np.int32)
    place = np.zeros((blocks, len(corners)), np.int32)
    for n, (e, end) in enumerate(corners):
        for b in range(blocks):
            if (b, e, end) in found:
                home[b, n], place[b, n] = found[(b, e, end)]
    choices = [sorted(set(facing[:, e].tolist())) for e in range(len(edges))]
    assert all(len(c) <= 2 for c in choices)
    second = np.stack([(facing[:, e] != choices[e][0]).astype(np.int32) for e in range(len(edges))], axis=1)
    return corners, most, send, home, place, choices, second


def tail_plan(patches, side, outer):
    early, late = [], []
    for p in range(patches):
        low = 1 if p in outer[2] else 0
        high = side - 1 if p in outer[3] else side
        clean = p not in outer[0] and p not in outer[1]
        for spans, low_row, high_row in ((early if clean else late, low, high), (late, 0, low), (late, high, side)):
            if low_row < high_row:
                spans.append((p, p + 1, low_row, high_row))
    plans = []
    for spans in (early, late):
        merged = []
        for p, end, low, high in sorted(spans, key=lambda piece: (piece[2], piece[3], piece[0])):
            if merged and merged[-1][1] == p and merged[-1][2:] == (low, high):
                merged[-1] = (merged[-1][0], end, low, high)
            else:
                merged.append((p, end, low, high))
        plans.append(merged)
    return plans


def joined(ref, span):
    return jnp.concatenate([ref[b, span, :] for b in range(ref.shape[0])], axis=1)


def split_store(ref, span, value):
    for b in range(ref.shape[0]):
        ref[b, span, :] = value[:, b * LANES:(b + 1) * LANES]


def window_kernel(
    tiles, sections, patches, micro, slots, inner, outer, early, late, corners, most, choices, starts,
    placement, table,
    states, weights, skip_w, biases,
    out,
    held, skip_held, bias_held, bias_own, given, stage, finished, hidden, summed, padded, rims, partial, across, corner_rows,
    outgoing_0, outgoing_1, onward_0, onward_1, received_0, received_1, gotten_0, gotten_1,
    behind, send_rows, edge_by, edge_slot, corner_send, corner_place,
    halo_send, halo_recv, weight_send, weight_recv, own_sem, out_send, out_recv, ready,
    relay_send, relay_recv, pass_send, pass_recv, tail_send, tail_recv, given_sem,
):
    tile = lax.axis_index("tile")
    section = lax.axis_index("section")
    half = sections // 2
    side = states.shape[2]
    chan = states.shape[4]
    rows = stage.shape[2]
    whole = rows // side
    outgoing, onward = (outgoing_0, outgoing_1), (onward_0, onward_1)
    received, gotten = (received_0, received_1), (gotten_0, gotten_1)
    edges = [(p, k) for k in range(4) for p in outer[k]]
    first_edge = [sum(len(outer[j]) for j in range(k)) for k in range(4)]

    def tile_at(by):
        return lax.rem(tile + by, tiles)

    partner = tile + 1 - 2 * lax.rem(tile, 2)
    partner_z = tile + 2 - 4 * lax.rem(tile // 2, 2)
    barrier = pltpu.get_barrier_semaphore()
    for by in range(1, tiles):
        pl.semaphore_signal(barrier, inc=1, device_id={"tile": tile_at(by)}, device_id_type=MESH)
    for by in range(1, sections):
        pl.semaphore_signal(
            barrier, inc=1, device_id={"section": lax.rem(section + by, sections)}, device_id_type=MESH
        )
        pl.semaphore_signal(
            barrier, inc=1, device_id={"tile": partner, "section": lax.rem(section + by, sections)},
            device_id_type=MESH,
        )
        pl.semaphore_signal(
            barrier, inc=1, device_id={"tile": partner_z, "section": lax.rem(section + by, sections)},
            device_id_type=MESH,
        )

    group = sections // micro
    works = lax.rem(section, group) == 0
    mine = section // group
    fetch = pltpu.make_async_copy(states.at[mine], given, given_sem.at[0])

    @pl.when(works)
    def _():
        fetch.start()

    bias_own[...] = jnp.zeros_like(bias_own)
    bias_own[0:LAYERS, :] = biases[0].astype(jnp.float32)

    assert group > 1 and tiles % 4 == 0 and sections % 2 == 0 and LAYERS == 2
    my_block = placement[tile]
    count = len(edges)
    sends, sources, places, corner_sends, corner_homes, corner_places, seconds = starts

    def find(block, _):
        def one(by, found):
            here = placement[lax.rem(tile - by + tiles, tiles)]
            return jnp.where(here == block, by, found)

        behind[block] = lax.fori_loop(0, tiles, one, jnp.int32(0))
        return 0

    local_row = (tiles - 1) * 8
    blank_row = local_row + 8
    corner_rows[blank_row:blank_row + 8, :] = jnp.zeros((8, chan), jnp.float32)

    lax.fori_loop(0, tiles, find, 0)

    def route(e, _):
        edge_by[e] = behind[table[sources + my_block * count + e]] - 1
        edge_slot[e] = table[places + my_block * count + e]
        return 0

    lax.fori_loop(0, count, route, 0)

    def fill(i, _):
        other = placement[tile_at(i // slots + 1)]
        send_rows[i] = table[sends + (my_block * tiles + other) * slots + lax.rem(i, slots)]
        return 0

    lax.fori_loop(0, (tiles - 1) * slots, fill, 0)

    def fill_corner(i, _):
        other = placement[tile_at(i // most)]
        corner_send[i] = table[corner_sends + (my_block * tiles + other) * most + lax.rem(i, most)]
        return 0

    lax.fori_loop(0, tiles * most, fill_corner, 0)

    def place_corner(n, _):
        home = table[corner_homes + my_block * len(corners) + n]
        by = behind[jnp.maximum(home, 0)]
        row = table[corner_places + my_block * len(corners) + n]
        row += jnp.where(by == 0, local_row, (by - 1) * 8)
        corner_place[n] = jnp.where(home < 0, blank_row, row)
        return 0

    lax.fori_loop(0, len(corners), place_corner, 0)

    pl.semaphore_wait(barrier, tiles - 1 + 3 * (sections - 1))

    column = lax.broadcasted_iota(jnp.int32, (whole, 8, chan), 1)
    first = column == 0
    last = column == 7

    def halo_copy(wave, turn, by):
        source, target = ((outgoing, received), (onward, gotten))[wave]
        return pltpu.make_async_remote_copy(
            src_ref=source[turn].at[by - 1],
            dst_ref=target[turn].at[by - 1],
            send_sem=halo_send.at[turn, wave, by - 1],
            recv_sem=halo_recv.at[turn, wave, by - 1],
            device_id={"tile": tile_at(by)},
            device_id_type=MESH,
        )

    pieces = (
        (weights.at[0], held, 0), (weights.at[1], held, 1), (skip_w.at[0], skip_held, None), (bias_own, bias_held, None)
    )

    def weight_copy(piece, source, worker):
        src, dst, layer = pieces[piece]
        return pltpu.make_async_remote_copy(
            src_ref=src,
            dst_ref=dst.at[source] if layer is None else dst.at[source, layer],
            send_sem=weight_send.at[worker, piece],
            recv_sem=weight_recv.at[source, piece],
            device_id={"section": worker * group},
            device_id_type=MESH,
        )

    def own_copy(piece):
        src, dst, layer = pieces[piece]
        return pltpu.make_async_copy(
            src, dst.at[section] if layer is None else dst.at[section, layer], own_sem.at[piece]
        )

    def out_copy(m, sec):
        return pltpu.make_async_remote_copy(
            src_ref=finished.at[sec], dst_ref=out.at[0, m],
            send_sem=out_send.at[sec], recv_sem=out_recv.at[m],
            device_id={"section": sec}, device_id_type=MESH,
        )

    units = {0: list(range(7)), 1: list(range(7, 13))}

    def unit_span(unit, other):
        if unit == 0:
            deep = chan // 2
            return (pl.ds(pl.multiple_of(lax.rem(tile + other, 2) * deep, LANES), deep),)
        layer, rest = (unit - 1) // 6, (unit - 1) % 6
        deep = 3 * chan // 4
        if by_z(unit):
            start = lax.rem(tile // 2 + other, 2) * deep
        else:
            start = 2 * deep + lax.rem(tile + other, 2) * deep
        return (layer, rest // 2, pl.ds(pl.multiple_of(start, 64), deep))

    def by_z(unit):
        return unit > 0 and unit % 2 == 0

    def place_of(unit, source, other):
        return (skip_held if unit == 0 else held).at[(source,) + unit_span(unit, other)]

    def relay_copy(unit, source, worker):
        own = (skip_w.at[0] if unit == 0 else weights).at[unit_span(unit, 0)]
        return pltpu.make_async_remote_copy(
            src_ref=own, dst_ref=place_of(unit, source, 0),
            send_sem=relay_send.at[worker, unit], recv_sem=relay_recv.at[source, unit],
            device_id={"section": worker * group + 1}, device_id_type=MESH,
        )

    def pass_copy(unit, source, hop, other):
        place = place_of(unit, source, other)
        device = {"section": mine * group}
        if hop == 1:
            device["tile"] = partner_z if by_z(unit) else partner
        return pltpu.make_async_remote_copy(
            src_ref=place, dst_ref=place,
            send_sem=pass_send.at[source, hop, unit], recv_sem=pass_recv.at[source, hop, unit],
            device_id=device, device_id_type=MESH,
        )

    def need(sec, layer):
        near = sec // group == mine
        for piece in ((3, 2, 0) if layer == 0 else (1,)):
            @pl.when(sec == section)
            def _():
                own_copy(piece).wait()

            @pl.when((sec != section) & (True if piece == 3 else near))
            def _():
                weight_copy(piece, sec, 0).wait_recv()

        @pl.when(jnp.logical_not(near))
        def _():
            for unit in units[layer]:
                for hop in range(2):
                    pass_copy(unit, sec, hop, hop).wait_recv()

    def gelu(z):
        return 0.5 * z * (1.0 + lax.erf(z * np.float32(0.5 ** 0.5)))

    def rolled(values, by):
        return pltpu.roll(values.reshape(values.shape[0] // 8, 8, chan), by, 1)

    def strided(values):
        height = values.shape[0]
        lower = jnp.where(first[:height // 8], 0.0, rolled(values, 1)).reshape(height, chan)
        upper = jnp.where(last[:height // 8], 0.0, rolled(values, 7)).reshape(height, chan)
        return jnp.concatenate([lower, values, upper], axis=1)

    def picked(cells, chosen):
        blank = jnp.zeros((1,) + cells.shape[1:], cells.dtype)
        parts = [blank if q is None else cells[q:q + 1] for q in chosen]
        parts += [blank] * (whole - len(chosen))
        return jnp.concatenate(parts, axis=0)

    def shifted_row(values):
        lower, upper = rolled(values, 1), rolled(values, 7)
        lower = jnp.where(first, picked(lower, inner[0]), lower).reshape(rows, chan)
        upper = jnp.where(last, picked(upper, inner[1]), upper).reshape(rows, chan)
        return jnp.concatenate([lower, values, upper], axis=1).astype(jnp.bfloat16)

    def across_row(values, chosen):
        moved = strided(values).reshape(whole, 8, 3 * chan)
        return picked(moved, chosen).reshape(rows, 3 * chan).astype(jnp.bfloat16)

    def rim_span(p, k):
        if k < 2:
            return pl.ds(p * 8 + 7 * k, 8, stride=rows)
        top = (k - 2) * (side - 1) * rows
        return slice(top + p * 8, top + p * 8 + 8)

    order = list(range(1, tiles))

    def send_rims(turn):
        for by in order:
            for q in range(slots):
                outgoing[turn][by - 1, q] = rims[send_rows[(by - 1) * slots + q]]
            halo_copy(0, turn, by).start()

    def wait_sent(turn):
        for wave in range(2):
            for by in range(1, tiles):
                halo_copy(wave, turn, by).wait_send()

    def side_dot(values, sec, layer, k):
        moved = strided(values).astype(jnp.bfloat16)
        if k >= 2:
            return jnp.dot(moved, held[sec, layer, k * 2 - 4], preferred_element_type=jnp.float32)
        total = jnp.zeros((values.shape[0], chan), jnp.float32)
        for i in range(3):
            total += jnp.dot(
                moved[:, i * chan:(i + 1) * chan],
                held[sec, layer, i, k * 2 * chan:(k * 2 + 1) * chan],
                preferred_element_type=jnp.float32,
            )
        return total

    def cross_seams(sec):
        made = {}
        for t in range(4):
            chosen = [e for e in range(count) if t in choices[e]]
            if chosen:
                values = jnp.concatenate([rims[e].astype(jnp.float32) for e in chosen], axis=0)
                total = side_dot(values, sec, 0, t)
                for n, e in enumerate(chosen):
                    made[e, t] = total[n * 8:n * 8 + 8]
        for e in range(count):
            value = made[e, choices[e][0]]
            if len(choices[e]) > 1:
                value = jnp.where(table[seconds + my_block * count + e] != 0, made[e, choices[e][1]], value)
            across[e * 8:e * 8 + 8, :] = value

    place_in = lax.broadcasted_iota(jnp.int32, (8, chan), 0)

    def corner_block(other):
        block = jnp.zeros((8, chan), jnp.float32)
        for j in range(most):
            row = across[pl.ds(corner_send[other * most + j], 1), :]
            block = jnp.where(place_in == j, row, block)
        return block

    def send_partial(turn):
        for e, (p, k) in enumerate(edges):
            partial[e] = joined(summed, rim_span(p, k)).astype(jnp.bfloat16)
        for by in order:
            for q in range(slots):
                onward[turn][by - 1, q] = partial[send_rows[(by - 1) * slots + q]]
            onward[turn][by - 1, slots] = corner_block(by).astype(jnp.bfloat16)
            halo_copy(1, turn, by).start()

    def take_corners(turn):
        for by in range(1, tiles):
            corner_rows[(by - 1) * 8:by * 8, :] = gotten[turn][by - 1, slots].astype(jnp.float32)

    def ghost(turn, e):
        z = gotten[turn][edge_by[e], edge_slot[e]].astype(jnp.float32) + across[e * 8:e * 8 + 8, :]
        for end in range(2):
            if (e, end) in corners:
                row = corner_rows[pl.ds(corner_place[corners.index((e, end))], 1), :]
                z += jnp.where(place_in == 7 * end, row, 0.0)
        return gelu(z)

    def keep(sec):
        for r in range(side):
            values = joined(hidden, slice(r * rows, (r + 1) * rows)).astype(jnp.bfloat16)
            stage[half + sec, r] = values
            finished[sec, :, r] = values.reshape(whole, 8, chan)[:patches]

        @pl.when(sec == section)
        def _():
            out[0, mine] = finished[sec]

        @pl.when(sec != section)
        def _():
            out_copy(mine, sec).start()

    def tail_copy(n, m):
        start, end, low, high = (early + late)[n]
        span = (slice(start, end), slice(low, high))
        return pltpu.make_async_remote_copy(
            src_ref=finished.at[(sections - 1,) + span], dst_ref=out.at[(0, m) + span],
            send_sem=tail_send.at[n], recv_sem=tail_recv.at[m, n],
            device_id={"section": sections - 1}, device_id_type=MESH,
        )

    def finish(which, begin):
        for start, end, low, high in which:
            for r in range(low, high):
                values = joined(hidden, slice(r * rows + start * 8, r * rows + end * 8))
                finished[sections - 1, start:end, r] = values.reshape(end - start, 8, chan).astype(jnp.bfloat16)
        for n in range(len(which)):
            tail_copy(begin + n, mine).start()

    def interior(sec, layer):
        for r in range(side):
            values = joined(hidden, slice(r * rows, (r + 1) * rows))
            padded[r + 1] = shifted_row(values)
            if r == 0:
                padded[side + 1] = across_row(values, inner[3])
            if r == side - 1:
                padded[0] = across_row(values, inner[2])

        step = 2
        need(sec, layer)

        @pl.loop(0, side // step)
        def _(part):
            r = part * step
            total = jnp.broadcast_to(bias_held[sec, layer:layer + 1, :], (step * rows, chan))
            for i in range(3):
                total += jnp.dot(
                    padded[pl.ds(r + i, step)].reshape(step * rows, 3 * chan),
                    held[sec, layer, i],
                    preferred_element_type=jnp.float32,
                )
            if layer == 0:
                total += jnp.dot(
                    stage[sec, pl.ds(r, step)].reshape(step * rows, chan),
                    skip_held[sec],
                    preferred_element_type=jnp.float32,
                )
            span = pl.ds(pl.multiple_of(r * rows, 8), step * rows)
            split_store(summed, span, total)
            split_store(hidden, span, gelu(total))

    def add_strips(sec, layer, strip):
        for k in (0, 1):
            values = [strip(first_edge[k] + n) for n in range(len(outer[k]))]
            added = side_dot(jnp.concatenate(values, axis=0), sec, layer, k)
            for n, p in enumerate(outer[k]):
                for b in range(chan // LANES):
                    summed[b, rim_span(p, k), :] += added[n * 8:n * 8 + 8, b * LANES:(b + 1) * LANES]
        for k in (2, 3):
            values = [strip(first_edge[k] + n) for n in range(len(outer[k]))]
            added = side_dot(jnp.concatenate(values, axis=0), sec, layer, k)
            top = (k - 2) * (side - 1) * rows
            span = slice(top + outer[k][0] * 8, top + outer[k][-1] * 8 + 8)
            total = joined(summed, span) + added
            split_store(summed, span, total)
            fresh = gelu(total)
            split_store(hidden, span, fresh)
            if layer == LAYERS - 1:
                for n in range(len(outer[k])):
                    rims[first_edge[k] + n] = fresh[n * 8:n * 8 + 8].astype(jnp.bfloat16)
        for k in (0, 1):
            for n, p in enumerate(outer[k]):
                fresh = gelu(joined(summed, rim_span(p, k)))
                split_store(hidden, rim_span(p, k), fresh)
                if layer == LAYERS - 1:
                    rims[first_edge[k] + n] = fresh.astype(jnp.bfloat16)

    def run_section(sec, turn):
        send_rims(turn)

        @pl.when(sec > 0)
        def _():
            keep(sec - 1)

        interior(sec, 0)
        cross_seams(sec)
        send_partial(turn)

        @pl.when(sec > 0)
        def _():
            wait_sent(1 - turn)

        corner_rows[local_row:local_row + 8, :] = corner_block(0)

        for by in range(1, tiles):
            halo_copy(0, turn, by).wait_recv()
        add_strips(sec, 0, lambda e: received[turn][edge_by[e], edge_slot[e]].astype(jnp.float32))

        interior(sec, 1)

        if turn == 1:
            @pl.when(sec == sections - 1)
            def _():
                finish(early, 0)

        for by in range(1, tiles):
            halo_copy(1, turn, by).wait_recv()
        take_corners(turn)
        add_strips(sec, 1, lambda e: ghost(turn, e))

    def send_weights(worker, which):
        for piece in which:
            weight_copy(piece, section, worker).start()

    @pl.when(works)
    def _():
        for piece in (3, 2, 0, 1):
            own_copy(piece).start()

    def send_units(worker):
        for unit in units[0] + units[1]:
            relay_copy(unit, section, worker).start()

    for worker in range(micro):
        @pl.when((section != worker * group) & (mine == worker))
        def _():
            send_weights(worker, (3, 2, 0, 1))

        @pl.when(mine != worker)
        def _():
            send_weights(worker, (3,))

        @pl.when(works & (mine != worker))
        def _():
            send_units(worker)

    relays = lax.rem(section, group) == 1

    def pass_on(source, wanted):
        for unit in wanted:
            relay_copy(unit, source, 0).wait_recv()
            for hop in (1, 0):
                pass_copy(unit, source, hop, 0).start()

    for rank in range(group):
        for worker in range(micro):
            source = worker * group + rank

            @pl.when(relays & (mine != worker))
            def _():
                pass_on(source, (units[0] + units[1])[:-5])
                if rank + 1 < group:
                    pl.semaphore_signal(
                        ready.at[mine], inc=1, device_id={"section": worker * group + rank + 1},
                        device_id_type=MESH,
                    )
                pass_on(source, (units[0] + units[1])[-5:])

        if rank + 1 < group:
            for worker in range(micro):
                @pl.when((lax.rem(section, group) == rank + 1) & (mine != worker))
                def _():
                    pl.semaphore_wait(ready.at[worker], 1)
                    send_units(worker)

    @pl.when(works)
    def _():
        fetch.wait()
        for r in range(side):
            values = given[:, r].astype(jnp.float32)
            if whole != patches:
                values = jnp.concatenate([values, jnp.zeros((whole - patches, 8, chan), jnp.float32)], axis=0)
            values = values.reshape(rows, chan)
            split_store(hidden, slice(r * rows, (r + 1) * rows), values)
            for i in range(half):
                stage[i, r] = values.astype(jnp.bfloat16)
        for e, (p, k) in enumerate(edges):
            rims[e] = joined(hidden, rim_span(p, k)).astype(jnp.bfloat16)

        @pl.loop(0, sections // 2)
        def _(pair):
            for turn in range(2):
                run_section(pair * 2 + turn, turn)

        finish(late, len(early))
        wait_sent(1)

        @pl.loop(0, sections - 1)
        def _(sec):
            @pl.when(sec != section)
            def _():
                out_copy(mine, sec).wait_send()

        for n in range(len(early) + len(late)):
            tail_copy(n, mine).wait_send()

    for worker in range(micro):
        @pl.when(section != worker * group)
        def _():
            weight_copy(3, section, worker).wait_send()

        @pl.when((section != worker * group) & (section != sections - 1))
        def _():
            out_copy(worker, section).wait_recv()

        @pl.when(section == sections - 1)
        def _():
            for n in range(len(early) + len(late)):
                tail_copy(n, worker).wait_recv()

        @pl.when((section != worker * group) & (mine == worker))
        def _():
            for piece in (2, 0, 1):
                weight_copy(piece, section, worker).wait_send()

        @pl.when(mine != worker)
        def _():
            for unit in units[0] + units[1]:
                relay_copy(unit, section, worker).wait_send()

        @pl.when(relays & (mine != worker))
        def _():
            for rank in range(group):
                for unit in units[0] + units[1]:
                    for hop in range(2):
                        pass_copy(unit, worker * group + rank, hop, 0).wait_send()


def on_device(states, conv_weight, skip_weight, bias, placement):
    sections = lax.axis_size("section")
    tiles = lax.axis_size("tile")
    micro, patches, side, _, chan = states.shape
    neighbour, rim_side, flip_flag = seam_tables(PR)
    assert not flip_flag.any()
    inner, outer = edge_plan(neighbour, rim_side, patches)
    early, late = tail_plan(patches, side, outer)
    pieces = early + late
    edges = [(p, k) for k in range(4) for p in outer[k]]
    send_row, _, recv_dev, recv_slot = off_device_routes(neighbour, rim_side, flip_flag, tiles, patches)
    slots = send_row.shape[2]
    number = np.zeros(patches * 4, np.int32)
    for e, (p, k) in enumerate(edges):
        number[p * 4 + k] = e
    take = [p * 4 + k for p, k in edges]
    whole = patches + patches % 2
    rows = whole * side
    corners, most, send, home, place, choices, second = ghost_plan(neighbour, rim_side, patches, outer)
    tables = [
        number[send_row].reshape(-1),
        recv_dev.reshape(tiles, -1)[:, take].reshape(-1),
        recv_slot.reshape(tiles, -1)[:, take].reshape(-1),
        send.reshape(-1), home.reshape(-1), place.reshape(-1), second.reshape(-1),
    ]
    starts = [int(x) for x in np.cumsum([0] + [t.size for t in tables])[:-1]]
    table = np.concatenate(tables)
    weights = conv_weight[0].reshape(LAYERS, 3, 3 * chan, chan)
    held = sections + sections // 2
    smem = pl.BlockSpec(memory_space=pltpu.SMEM)
    vmem = pl.BlockSpec(memory_space=pltpu.VMEM)
    wide = pltpu.VMEM((chan // LANES, side * rows, LANES), jnp.float32)
    got = pltpu.VMEM((tiles - 1, slots, side, chan), jnp.bfloat16)
    more = pltpu.VMEM((tiles - 1, slots + 1, side, chan), jnp.bfloat16)
    flops = 2 * micro * side * rows * chan * chan * (9 * LAYERS + 1)
    return pl.pallas_call(
        functools.partial(window_kernel, tiles, sections, patches, micro, slots, inner, outer, early, late, corners, most, choices, starts),
        out_shape=pltpu.VMEM((1,) + states.shape, jnp.bfloat16),
        in_specs=[smem] * 2 + [pl.BlockSpec(memory_space=pl.ANY)] * 2 + [vmem, vmem],
        out_specs=vmem,
        scratch_shapes=[
            pltpu.VMEM((sections,) + weights.shape, jnp.bfloat16),
            pltpu.VMEM((sections, chan, chan), jnp.bfloat16),
            pltpu.VMEM((sections, 8, chan), jnp.float32),
            pltpu.VMEM((8, chan), jnp.float32),
            pltpu.VMEM(states.shape[1:], jnp.bfloat16),
            pltpu.VMEM((held, side, rows, chan), jnp.bfloat16),
            pltpu.VMEM((sections,) + states.shape[1:], jnp.bfloat16),
            wide, wide,
            pltpu.VMEM((side + 2, rows, 3 * chan), jnp.bfloat16),
            pltpu.VMEM((len(edges), side, chan), jnp.bfloat16),
            pltpu.VMEM((len(edges), side, chan), jnp.bfloat16),
            pltpu.VMEM((len(edges) * side, chan), jnp.float32),
            pltpu.VMEM(((tiles - 1) * 8 + 16, chan), jnp.float32),
            got, got, more, more, got, got, more, more,
            pltpu.SMEM((tiles,), jnp.int32),
            pltpu.SMEM(((tiles - 1) * slots,), jnp.int32),
            pltpu.SMEM((len(edges),), jnp.int32),
            pltpu.SMEM((len(edges),), jnp.int32),
            pltpu.SMEM((tiles * most,), jnp.int32),
            pltpu.SMEM((len(corners),), jnp.int32),
            pltpu.SemaphoreType.DMA((2, 2, tiles - 1)),
            pltpu.SemaphoreType.DMA((2, 2, tiles - 1)),
            pltpu.SemaphoreType.DMA((micro, 4)),
            pltpu.SemaphoreType.DMA((sections, 4)),
            pltpu.SemaphoreType.DMA((4,)),
            pltpu.SemaphoreType.DMA((sections,)),
            pltpu.SemaphoreType.DMA((micro,)),
            pltpu.SemaphoreType.REGULAR((micro,)),
            pltpu.SemaphoreType.DMA((micro, 13)),
            pltpu.SemaphoreType.DMA((sections, 13)),
            pltpu.SemaphoreType.DMA((sections, 2, 13)),
            pltpu.SemaphoreType.DMA((sections, 2, 13)),
            pltpu.SemaphoreType.DMA((len(pieces),)),
            pltpu.SemaphoreType.DMA((micro, len(pieces))),
            pltpu.SemaphoreType.DMA((1,)),
        ],
        compiler_params=pltpu.CompilerParams(
            collective_id=0, has_side_effects=True, vmem_limit_bytes=56 * 1024 * 1024
        ),
        cost_estimate=pl.CostEstimate(flops=flops, bytes_accessed=2**24, transcendentals=0),
    )(
        placement, jnp.asarray(table, jnp.int32),
        states, weights, skip_weight, bias,
    )


def solution(mesh):
    in_specs = (
        P(None, "tile", None, None, None),
        P("section", None, None, None, None, None),
        P("section", None, None),
        P("section", None, None),
        P(),
    )
    out_specs = P("section", None, "tile", None, None, None)
    return jax.shard_map(
        on_device, mesh=mesh, in_specs=in_specs, out_specs=out_specs, check_vma=False
    )
```

```python
import functools

import jax
import jax.numpy as jnp
import numpy as np
from jax import lax
from jax.experimental import pallas as pl
from jax.experimental.pallas import tpu as pltpu
from jax.sharding import PartitionSpec as P

LAYERS = 2
PR = 4


def face_across(face_num, direction):
    cycle = face_num // 4
    column = face_num % 4
    if cycle == 0:
        table = [4 + column, 4 + (column + 1) % 4, (column + 1) % 4, (column + 3) % 4]
    elif cycle == 1:
        table = [8 + (column + 3) % 4, 8 + column, column, (column + 3) % 4]
    else:
        table = [8 + (column + 3) % 4, 8 + (column + 1) % 4, 4 + (column + 1) % 4, 4 + column]
    return table[direction]


def locate(face_num, coord_x, coord_y, face_span):
    if 0 <= coord_x < face_span and 0 <= coord_y < face_span:
        return (face_num, coord_x, coord_y)
    if coord_x < 0:
        direction = 0
    elif coord_y < 0:
        direction = 1
    elif coord_x >= face_span:
        direction = 2
    else:
        direction = 3
    cycle = face_num // 4
    target = face_across(face_num, direction)
    coord_x = coord_x % face_span
    coord_y = coord_y % face_span
    if cycle == 0 and direction == 2 or (cycle == 2 and direction == 0):
        coord_x, coord_y = (coord_y, face_span - 1 - coord_x)
    elif cycle == 0 and direction == 3 or (cycle == 2 and direction == 1):
        coord_x, coord_y = (face_span - 1 - coord_y, coord_x)
    return (target, coord_x, coord_y)


def seam_tables(tiles):
    cell_side = 2
    face_span = tiles * cell_side
    face_tiles = tiles * tiles
    total = 12 * face_tiles
    neighbour = np.zeros((total, 4), np.int32)
    rim_side = np.zeros((total, 4), np.int32)
    flip_flag = np.zeros((total, 4), np.int32)
    for patch_num in range(total):
        cycle = patch_num % 3
        rest = patch_num // 3
        column = rest // face_tiles
        tile_y = rest % face_tiles // tiles
        tile_x = rest % tiles
        face_num = 4 * cycle + column
        base_x = tile_x * cell_side
        base_y = tile_y * cell_side
        for side_num in range(4):
            found = []
            for step_num in range(2):
                if side_num == 0:
                    point = (base_x - 1, base_y + step_num)
                elif side_num == 1:
                    point = (base_x + cell_side, base_y + step_num)
                elif side_num == 2:
                    point = (base_x + step_num, base_y - 1)
                else:
                    point = (base_x + step_num, base_y + cell_side)
                found.append(locate(face_num, point[0], point[1], face_span))
            face_a, first_x, first_y = found[0]
            face_b, second_x, second_y = found[1]
            neighbour[patch_num, side_num] = (
                3 * (face_a % 4 * face_tiles + first_y // cell_side * tiles + first_x // cell_side)
                + face_a // 4
            )
            if first_x == second_x:
                rim_side[patch_num, side_num] = 0 if first_x % cell_side == 0 else 1
                flip_flag[patch_num, side_num] = 1 if second_y < first_y else 0
            else:
                rim_side[patch_num, side_num] = 2 if first_y % cell_side == 0 else 3
                flip_flag[patch_num, side_num] = 1 if second_x < first_x else 0
    return (neighbour, rim_side, flip_flag)


def off_device_routes(neighbour, rim_side, flip_flag, tile_count, per_dev):
    source_dev = (neighbour // per_dev).reshape(-1)
    dest_dev = np.repeat(np.arange(neighbour.shape[0]) // per_dev, 4)
    row = (neighbour % per_dev * 4 + rim_side).reshape(-1)
    away = source_dev != dest_dev
    slot_num = np.zeros(row.shape[0], np.int64)
    counts = np.zeros((tile_count, tile_count), np.int64)
    for e in np.flatnonzero(away):
        slot_num[e] = counts[source_dev[e], dest_dev[e]]
        counts[source_dev[e], dest_dev[e]] += 1
    send_row = np.zeros((tile_count, tile_count, int(counts.max())), np.int32)
    send_row[source_dev[away], dest_dev[away], slot_num[away]] = row[away]
    place = np.where(away, slot_num, row)
    recv_dev = source_dev.reshape(tile_count, per_dev, 4).astype(np.int32)
    recv_slot = place.reshape(tile_count, per_dev, 4).astype(np.int32)
    return (send_row, None, recv_dev, recv_slot)


MESH = pl.DeviceIdType.MESH
LANES = 128


def edge_plan(neighbour, rim_side, patches):
    blocks = neighbour.shape[0] // patches
    near = neighbour.reshape(blocks, patches, 4) // patches
    home = near == np.arange(blocks)[:, None, None]
    inner = [[None] * patches for _ in range(4)]
    outer = [[] for _ in range(4)]
    for p in range(patches):
        for k in range(4):
            local = neighbour.reshape(blocks, patches, 4)[:, p, k] % patches
            same = home[:, p, k].all() and (local == local[0]).all()
            facing = (rim_side.reshape(blocks, patches, 4)[:, p, k] == (k ^ 1)).all()
            if same and facing:
                inner[k][p] = int(local[0])
            else:
                assert not home[:, p, k].any()
                outer[k].append(p)
    for k in (2, 3):
        assert outer[k] == list(range(outer[k][0], outer[k][-1] + 1))
    return inner, outer


def ghost_plan(neighbour, rim_side, patches, outer):
    blocks = neighbour.shape[0] // patches
    edges = [(p, k) for k in range(4) for p in outer[k]]
    number = {edge: e for e, edge in enumerate(edges)}
    facing = np.zeros((blocks, len(edges)), np.int32)
    sent = [[[] for _ in range(blocks)] for _ in range(blocks)]
    found = {}
    for b in range(blocks):
        for e, (p, k) in enumerate(edges):
            q, t = neighbour[b * patches + p, k], rim_side[b * patches + p, k]
            facing[b, e] = t
            for end in range(2):
                across = (2 if t < 2 else 0) + end
                if (q % patches, across) in number:
                    other, side = neighbour[q, across], rim_side[q, across]
                    home = other // patches
                    row = number[(other % patches, side)] * 8 + (0 if t in (0, 2) else 7)
                    found[(b, e, end)] = (home, len(sent[home][b]))
                    sent[home][b].append(row)
    corners = sorted({(e, end) for _, e, end in found})
    most = max(len(x) for line in sent for x in line)
    assert most <= 8
    send = np.zeros((blocks, blocks, most), np.int32)
    for a in range(blocks):
        for b in range(blocks):
            send[a, b, :len(sent[a][b])] = sent[a][b]
    home = np.full((blocks, len(corners)), -1, np.int32)
    place = np.zeros((blocks, len(corners)), np.int32)
    for n, (e, end) in enumerate(corners):
        for b in range(blocks):
            if (b, e, end) in found:
                home[b, n], place[b, n] = found[(b, e, end)]
    choices = [sorted(set(facing[:, e].tolist())) for e in range(len(edges))]
    assert all(len(c) <= 2 for c in choices)
    second = np.stack([(facing[:, e] != choices[e][0]).astype(np.int32) for e in range(len(edges))], axis=1)
    return corners, most, send, home, place, choices, second


def tail_plan(patches, side, outer):
    early, late = [], []
    for p in range(patches):
        low = 1 if p in outer[2] else 0
        high = side - 1 if p in outer[3] else side
        clean = p not in outer[0] and p not in outer[1]
        for spans, low_row, high_row in ((early if clean else late, low, high), (late, 0, low), (late, high, side)):
            if low_row < high_row:
                spans.append((p, p + 1, low_row, high_row))
    plans = []
    for spans in (early, late):
        merged = []
        for p, end, low, high in sorted(spans, key=lambda piece: (piece[2], piece[3], piece[0])):
            if merged and merged[-1][1] == p and merged[-1][2:] == (low, high):
                merged[-1] = (merged[-1][0], end, low, high)
            else:
                merged.append((p, end, low, high))
        plans.append(merged)
    return plans


def joined(ref, span):
    return jnp.concatenate([ref[b, span, :] for b in range(ref.shape[0])], axis=1)


def split_store(ref, span, value):
    for b in range(ref.shape[0]):
        ref[b, span, :] = value[:, b * LANES:(b + 1) * LANES]


def window_kernel(
    tiles, sections, patches, micro, slots, inner, outer, early, late, corners, most, choices, starts,
    placement, table,
    states, weights, skip_w, biases,
    out,
    held, skip_held, bias_held, bias_own, given, stage, finished, hidden, summed, padded, rims, partial, across, corner_rows,
    outgoing_0, outgoing_1, onward_0, onward_1, received_0, received_1, gotten_0, gotten_1,
    behind, send_rows, edge_by, edge_slot, corner_send, corner_place,
    halo_send, halo_recv, weight_send, weight_recv, own_sem, out_send, out_recv, ready,
    relay_send, relay_recv, pass_send, pass_recv, tail_send, tail_recv, given_sem,
):
    tile = lax.axis_index("tile")
    section = lax.axis_index("section")
    half = sections // 2
    side = states.shape[2]
    chan = states.shape[4]
    rows = stage.shape[2]
    whole = rows // side
    outgoing, onward = (outgoing_0, outgoing_1), (onward_0, onward_1)
    received, gotten = (received_0, received_1), (gotten_0, gotten_1)
    edges = [(p, k) for k in range(4) for p in outer[k]]
    first_edge = [sum(len(outer[j]) for j in range(k)) for k in range(4)]

    def tile_at(by):
        return lax.rem(tile + by, tiles)

    partner = tile + 1 - 2 * lax.rem(tile, 2)
    partner_z = tile + 2 - 4 * lax.rem(tile // 2, 2)
    barrier = pltpu.get_barrier_semaphore()
    for by in range(1, tiles):
        pl.semaphore_signal(barrier, inc=1, device_id={"tile": tile_at(by)}, device_id_type=MESH)
    for by in range(1, sections):
        pl.semaphore_signal(
            barrier, inc=1, device_id={"section": lax.rem(section + by, sections)}, device_id_type=MESH
        )
        pl.semaphore_signal(
            barrier, inc=1, device_id={"tile": partner, "section": lax.rem(section + by, sections)},
            device_id_type=MESH,
        )
        pl.semaphore_signal(
            barrier, inc=1, device_id={"tile": partner_z, "section": lax.rem(section + by, sections)},
            device_id_type=MESH,
        )

    group = sections // micro
    works = lax.rem(section, group) == 0
    mine = section // group
    fetch = pltpu.make_async_copy(states.at[mine], given, given_sem.at[0])

    @pl.when(works)
    def _():
        fetch.start()

    bias_own[...] = jnp.zeros_like(bias_own)
    bias_own[0:LAYERS, :] = biases[0].astype(jnp.float32)

    assert group > 1 and tiles % 4 == 0 and sections % 2 == 0 and LAYERS == 2
    my_block = placement[tile]
    count = len(edges)
    sends, sources, places, corner_sends, corner_homes, corner_places, seconds = starts

    def find(block, _):
        def one(by, found):
            here = placement[lax.rem(tile - by + tiles, tiles)]
            return jnp.where(here == block, by, found)

        behind[block] = lax.fori_loop(0, tiles, one, jnp.int32(0))
        return 0

    local_row = (tiles - 1) * 8
    blank_row = local_row + 8
    corner_rows[blank_row:blank_row + 8, :] = jnp.zeros((8, chan), jnp.float32)

    lax.fori_loop(0, tiles, find, 0)

    def route(e, _):
        edge_by[e] = behind[table[sources + my_block * count + e]] - 1
        edge_slot[e] = table[places + my_block * count + e]
        return 0

    lax.fori_loop(0, count, route, 0)

    def fill(i, _):
        other = placement[tile_at(i // slots + 1)]
        send_rows[i] = table[sends + (my_block * tiles + other) * slots + lax.rem(i, slots)]
        return 0

    lax.fori_loop(0, (tiles - 1) * slots, fill, 0)

    def fill_corner(i, _):
        other = placement[tile_at(i // most)]
        corner_send[i] = table[corner_sends + (my_block * tiles + other) * most + lax.rem(i, most)]
        return 0

    lax.fori_loop(0, tiles * most, fill_corner, 0)

    def place_corner(n, _):
        home = table[corner_homes + my_block * len(corners) + n]
        by = behind[jnp.maximum(home, 0)]
        row = table[corner_places + my_block * len(corners) + n]
        row += jnp.where(by == 0, local_row, (by - 1) * 8)
        corner_place[n] = jnp.where(home < 0, blank_row, row)
        return 0

    lax.fori_loop(0, len(corners), place_corner, 0)

    pl.semaphore_wait(barrier, tiles - 1 + 3 * (sections - 1))

    column = lax.broadcasted_iota(jnp.int32, (whole, 8, chan), 1)
    first = column == 0
    last = column == 7

    def halo_copy(wave, turn, by):
        source, target = ((outgoing, received), (onward, gotten))[wave]
        return pltpu.make_async_remote_copy(
            src_ref=source[turn].at[by - 1],
            dst_ref=target[turn].at[by - 1],
            send_sem=halo_send.at[turn, wave, by - 1],
            recv_sem=halo_recv.at[turn, wave, by - 1],
            device_id={"tile": tile_at(by)},
            device_id_type=MESH,
        )

    pieces = (
        (weights.at[0], held, 0), (weights.at[1], held, 1), (skip_w.at[0], skip_held, None), (bias_own, bias_held, None)
    )

    def weight_copy(piece, source, worker):
        src, dst, layer = pieces[piece]
        return pltpu.make_async_remote_copy(
            src_ref=src,
            dst_ref=dst.at[source] if layer is None else dst.at[source, layer],
            send_sem=weight_send.at[worker, piece],
            recv_sem=weight_recv.at[source, piece],
            device_id={"section": worker * group},
            device_id_type=MESH,
        )

    def own_copy(piece):
        src, dst, layer = pieces[piece]
        return pltpu.make_async_copy(
            src, dst.at[section] if layer is None else dst.at[section, layer], own_sem.at[piece]
        )

    def out_copy(m, sec):
        return pltpu.make_async_remote_copy(
            src_ref=finished.at[sec], dst_ref=out.at[0, m],
            send_sem=out_send.at[sec], recv_sem=out_recv.at[m],
            device_id={"section": sec}, device_id_type=MESH,
        )

    units = {0: list(range(10)), 1: list(range(10, 19))}

    def unit_span(unit, other):
        if unit == 0:
            deep = chan // 2
            return (pl.ds(pl.multiple_of(lax.rem(tile + other, 2) * deep, LANES), deep),)
        layer, rest = (unit - 1) // 9, (unit - 1) % 9
        deep = 5 * chan // 8
        if straight(unit):
            return (layer, rest // 3, slice(4 * deep, 3 * chan))
        if by_z(unit):
            start = lax.rem(tile // 2 + other, 2) * deep
        else:
            start = 2 * deep + lax.rem(tile + other, 2) * deep
        return (layer, rest // 3, pl.ds(pl.multiple_of(start, 32), deep))

    def by_z(unit):
        return unit > 0 and (unit - 1) % 3 == 1

    def straight(unit):
        return unit > 0 and (unit - 1) % 3 == 2

    def place_of(unit, source, other):
        return (skip_held if unit == 0 else held).at[(source,) + unit_span(unit, other)]

    def relay_copy(unit, source, worker):
        own = (skip_w.at[0] if unit == 0 else weights).at[unit_span(unit, 0)]
        return pltpu.make_async_remote_copy(
            src_ref=own, dst_ref=place_of(unit, source, 0),
            send_sem=relay_send.at[worker, unit], recv_sem=relay_recv.at[source, unit],
            device_id={"section": worker * group + (0 if straight(unit) else 1)}, device_id_type=MESH,
        )

    def pass_copy(unit, source, hop, other):
        place = place_of(unit, source, other)
        device = {"section": mine * group}
        if hop == 1:
            device["tile"] = partner_z if by_z(unit) else partner
        return pltpu.make_async_remote_copy(
            src_ref=place, dst_ref=place,
            send_sem=pass_send.at[source, hop, unit], recv_sem=pass_recv.at[source, hop, unit],
            device_id=device, device_id_type=MESH,
        )

    def need(sec, layer):
        near = sec // group == mine
        for piece in ((3, 2, 0) if layer == 0 else (1,)):
            @pl.when(sec == section)
            def _():
                own_copy(piece).wait()

            @pl.when((sec != section) & (True if piece == 3 else near))
            def _():
                weight_copy(piece, sec, 0).wait_recv()

        @pl.when(jnp.logical_not(near))
        def _():
            for unit in units[layer]:
                if straight(unit):
                    relay_copy(unit, sec, 0).wait_recv()
                else:
                    for hop in range(2):
                        pass_copy(unit, sec, hop, hop).wait_recv()

    def gelu(z):
        return 0.5 * z * (1.0 + lax.erf(z * np.float32(0.5 ** 0.5)))

    def rolled(values, by):
        return pltpu.roll(values.reshape(values.shape[0] // 8, 8, chan), by, 1)

    def strided(values):
        height = values.shape[0]
        lower = jnp.where(first[:height // 8], 0.0, rolled(values, 1)).reshape(height, chan)
        upper = jnp.where(last[:height // 8], 0.0, rolled(values, 7)).reshape(height, chan)
        return jnp.concatenate([lower, values, upper], axis=1)

    def picked(cells, chosen):
        blank = jnp.zeros((1,) + cells.shape[1:], cells.dtype)
        parts = [blank if q is None else cells[q:q + 1] for q in chosen]
        parts += [blank] * (whole - len(chosen))
        return jnp.concatenate(parts, axis=0)

    def shifted_row(values):
        lower, upper = rolled(values, 1), rolled(values, 7)
        lower = jnp.where(first, picked(lower, inner[0]), lower).reshape(rows, chan)
        upper = jnp.where(last, picked(upper, inner[1]), upper).reshape(rows, chan)
        return jnp.concatenate([lower, values, upper], axis=1).astype(jnp.bfloat16)

    def across_row(values, chosen):
        moved = strided(values).reshape(whole, 8, 3 * chan)
        return picked(moved, chosen).reshape(rows, 3 * chan).astype(jnp.bfloat16)

    def rim_span(p, k):
        if k < 2:
            return pl.ds(p * 8 + 7 * k, 8, stride=rows)
        top = (k - 2) * (side - 1) * rows
        return slice(top + p * 8, top + p * 8 + 8)

    order = list(range(1, tiles))

    def send_rims(turn):
        for by in order:
            for q in range(slots):
                outgoing[turn][by - 1, q] = rims[send_rows[(by - 1) * slots + q]]
            halo_copy(0, turn, by).start()

    def wait_sent(turn):
        for wave in range(2):
            for by in range(1, tiles):
                halo_copy(wave, turn, by).wait_send()

    def side_dot(values, sec, layer, k):
        moved = strided(values).astype(jnp.bfloat16)
        if k >= 2:
            return jnp.dot(moved, held[sec, layer, k * 2 - 4], preferred_element_type=jnp.float32)
        total = jnp.zeros((values.shape[0], chan), jnp.float32)
        for i in range(3):
            total += jnp.dot(
                moved[:, i * chan:(i + 1) * chan],
                held[sec, layer, i, k * 2 * chan:(k * 2 + 1) * chan],
                preferred_element_type=jnp.float32,
            )
        return total

    def cross_seams(sec):
        made = {}
        for t in range(4):
            chosen = [e for e in range(count) if t in choices[e]]
            if chosen:
                values = jnp.concatenate([rims[e].astype(jnp.float32) for e in chosen], axis=0)
                total = side_dot(values, sec, 0, t)
                for n, e in enumerate(chosen):
                    made[e, t] = total[n * 8:n * 8 + 8]
        for e in range(count):
            value = made[e, choices[e][0]]
            if len(choices[e]) > 1:
                value = jnp.where(table[seconds + my_block * count + e] != 0, made[e, choices[e][1]], value)
            across[e * 8:e * 8 + 8, :] = value

    place_in = lax.broadcasted_iota(jnp.int32, (8, chan), 0)

    def corner_block(other):
        block = jnp.zeros((8, chan), jnp.float32)
        for j in range(most):
            row = across[pl.ds(corner_send[other * most + j], 1), :]
            block = jnp.where(place_in == j, row, block)
        return block

    def send_partial(turn):
        for e, (p, k) in enumerate(edges):
            partial[e] = joined(summed, rim_span(p, k)).astype(jnp.bfloat16)
        for by in order:
            for q in range(slots):
                onward[turn][by - 1, q] = partial[send_rows[(by - 1) * slots + q]]
            onward[turn][by - 1, slots] = corner_block(by).astype(jnp.bfloat16)
            halo_copy(1, turn, by).start()

    def take_corners(turn):
        for by in range(1, tiles):
            corner_rows[(by - 1) * 8:by * 8, :] = gotten[turn][by - 1, slots].astype(jnp.float32)

    def ghost(turn, e):
        z = gotten[turn][edge_by[e], edge_slot[e]].astype(jnp.float32) + across[e * 8:e * 8 + 8, :]
        for end in range(2):
            if (e, end) in corners:
                row = corner_rows[pl.ds(corner_place[corners.index((e, end))], 1), :]
                z += jnp.where(place_in == 7 * end, row, 0.0)
        return gelu(z)

    def keep(sec):
        for r in range(side):
            values = joined(hidden, slice(r * rows, (r + 1) * rows)).astype(jnp.bfloat16)
            stage[half + sec, r] = values
            finished[sec, :, r] = values.reshape(whole, 8, chan)[:patches]

        @pl.when(sec == section)
        def _():
            out[0, mine] = finished[sec]

        @pl.when(sec != section)
        def _():
            out_copy(mine, sec).start()

    def tail_copy(n, m):
        start, end, low, high = (early + late)[n]
        span = (slice(start, end), slice(low, high))
        return pltpu.make_async_remote_copy(
            src_ref=finished.at[(sections - 1,) + span], dst_ref=out.at[(0, m) + span],
            send_sem=tail_send.at[n], recv_sem=tail_recv.at[m, n],
            device_id={"section": sections - 1}, device_id_type=MESH,
        )

    def finish(which, begin):
        for start, end, low, high in which:
            for r in range(low, high):
                values = joined(hidden, slice(r * rows + start * 8, r * rows + end * 8))
                finished[sections - 1, start:end, r] = values.reshape(end - start, 8, chan).astype(jnp.bfloat16)
        for n in range(len(which)):
            tail_copy(begin + n, mine).start()

    def interior(sec, layer):
        for r in range(side):
            values = joined(hidden, slice(r * rows, (r + 1) * rows))
            padded[r + 1] = shifted_row(values)
            if r == 0:
                padded[side + 1] = across_row(values, inner[3])
            if r == side - 1:
                padded[0] = across_row(values, inner[2])

        step = 2
        need(sec, layer)

        @pl.loop(0, side // step)
        def _(part):
            r = part * step
            total = jnp.broadcast_to(bias_held[sec, layer:layer + 1, :], (step * rows, chan))
            for i in range(3):
                total += jnp.dot(
                    padded[pl.ds(r + i, step)].reshape(step * rows, 3 * chan),
                    held[sec, layer, i],
                    preferred_element_type=jnp.float32,
                )
            if layer == 0:
                total += jnp.dot(
                    stage[sec, pl.ds(r, step)].reshape(step * rows, chan),
                    skip_held[sec],
                    preferred_element_type=jnp.float32,
                )
            span = pl.ds(pl.multiple_of(r * rows, 8), step * rows)
            split_store(summed, span, total)
            split_store(hidden, span, gelu(total))

    def add_strips(sec, layer, strip):
        for k in (0, 1):
            values = [strip(first_edge[k] + n) for n in range(len(outer[k]))]
            added = side_dot(jnp.concatenate(values, axis=0), sec, layer, k)
            for n, p in enumerate(outer[k]):
                for b in range(chan // LANES):
                    summed[b, rim_span(p, k), :] += added[n * 8:n * 8 + 8, b * LANES:(b + 1) * LANES]
        for k in (2, 3):
            values = [strip(first_edge[k] + n) for n in range(len(outer[k]))]
            added = side_dot(jnp.concatenate(values, axis=0), sec, layer, k)
            top = (k - 2) * (side - 1) * rows
            span = slice(top + outer[k][0] * 8, top + outer[k][-1] * 8 + 8)
            total = joined(summed, span) + added
            split_store(summed, span, total)
            fresh = gelu(total)
            split_store(hidden, span, fresh)
            if layer == LAYERS - 1:
                for n in range(len(outer[k])):
                    rims[first_edge[k] + n] = fresh[n * 8:n * 8 + 8].astype(jnp.bfloat16)
        for k in (0, 1):
            for n, p in enumerate(outer[k]):
                fresh = gelu(joined(summed, rim_span(p, k)))
                split_store(hidden, rim_span(p, k), fresh)
                if layer == LAYERS - 1:
                    rims[first_edge[k] + n] = fresh.astype(jnp.bfloat16)

    def run_section(sec, turn):
        send_rims(turn)

        @pl.when(sec > 0)
        def _():
            keep(sec - 1)
            wait_sent(1 - turn)

        interior(sec, 0)
        cross_seams(sec)
        send_partial(turn)
        corner_rows[local_row:local_row + 8, :] = corner_block(0)

        for by in range(1, tiles):
            halo_copy(0, turn, by).wait_recv()
        add_strips(sec, 0, lambda e: received[turn][edge_by[e], edge_slot[e]].astype(jnp.float32))

        interior(sec, 1)

        if turn == 1:
            @pl.when(sec == sections - 1)
            def _():
                finish(early, 0)

        for by in range(1, tiles):
            halo_copy(1, turn, by).wait_recv()
        take_corners(turn)
        add_strips(sec, 1, lambda e: ghost(turn, e))

    def send_weights(worker, which):
        for piece in which:
            weight_copy(piece, section, worker).start()

    @pl.when(works)
    def _():
        for piece in (3, 2, 0, 1):
            own_copy(piece).start()

    def send_units(worker):
        for unit in units[0] + units[1]:
            relay_copy(unit, section, worker).start()

    for worker in range(micro):
        @pl.when((section != worker * group) & (mine == worker))
        def _():
            send_weights(worker, (3, 2, 0, 1))

        @pl.when(mine != worker)
        def _():
            send_weights(worker, (3,))

        @pl.when(works & (mine != worker))
        def _():
            send_units(worker)

    relays = lax.rem(section, group) == 1

    def pass_on(source, wanted):
        for unit in wanted:
            if straight(unit):
                continue
            relay_copy(unit, source, 0).wait_recv()
            for hop in (1, 0):
                pass_copy(unit, source, hop, 0).start()

    for rank in range(group):
        for worker in range(micro):
            source = worker * group + rank

            @pl.when(relays & (mine != worker))
            def _():
                pass_on(source, (units[0] + units[1])[:-5])
                if rank + 1 < group:
                    pl.semaphore_signal(
                        ready.at[mine], inc=1, device_id={"section": worker * group + rank + 1},
                        device_id_type=MESH,
                    )
                pass_on(source, (units[0] + units[1])[-5:])

        if rank + 1 < group:
            for worker in range(micro):
                @pl.when((lax.rem(section, group) == rank + 1) & (mine != worker))
                def _():
                    pl.semaphore_wait(ready.at[worker], 1)
                    send_units(worker)

    @pl.when(works)
    def _():
        fetch.wait()
        for r in range(side):
            values = given[:, r].astype(jnp.float32)
            if whole != patches:
                values = jnp.concatenate([values, jnp.zeros((whole - patches, 8, chan), jnp.float32)], axis=0)
            values = values.reshape(rows, chan)
            split_store(hidden, slice(r * rows, (r + 1) * rows), values)
            for i in range(half):
                stage[i, r] = values.astype(jnp.bfloat16)
        for e, (p, k) in enumerate(edges):
            rims[e] = joined(hidden, rim_span(p, k)).astype(jnp.bfloat16)

        @pl.loop(0, sections // 2)
        def _(pair):
            for turn in range(2):
                run_section(pair * 2 + turn, turn)

        finish(late, len(early))
        wait_sent(1)

        @pl.loop(0, sections - 1)
        def _(sec):
            @pl.when(sec != section)
            def _():
                out_copy(mine, sec).wait_send()

        for n in range(len(early) + len(late)):
            tail_copy(n, mine).wait_send()

    for worker in range(micro):
        @pl.when(section != worker * group)
        def _():
            weight_copy(3, section, worker).wait_send()

        @pl.when((section != worker * group) & (section != sections - 1))
        def _():
            out_copy(worker, section).wait_recv()

        @pl.when(section == sections - 1)
        def _():
            for n in range(len(early) + len(late)):
                tail_copy(n, worker).wait_recv()

        @pl.when((section != worker * group) & (mine == worker))
        def _():
            for piece in (2, 0, 1):
                weight_copy(piece, section, worker).wait_send()

        @pl.when(mine != worker)
        def _():
            for unit in units[0] + units[1]:
                relay_copy(unit, section, worker).wait_send()

        @pl.when(relays & (mine != worker))
        def _():
            for rank in range(group):
                for unit in units[0] + units[1]:
                    for hop in range(0 if straight(unit) else 2):
                        pass_copy(unit, worker * group + rank, hop, 0).wait_send()


def on_device(states, conv_weight, skip_weight, bias, placement):
    sections = lax.axis_size("section")
    tiles = lax.axis_size("tile")
    micro, patches, side, _, chan = states.shape
    neighbour, rim_side, flip_flag = seam_tables(PR)
    assert not flip_flag.any()
    inner, outer = edge_plan(neighbour, rim_side, patches)
    early, late = tail_plan(patches, side, outer)
    pieces = early + late
    edges = [(p, k) for k in range(4) for p in outer[k]]
    send_row, _, recv_dev, recv_slot = off_device_routes(neighbour, rim_side, flip_flag, tiles, patches)
    slots = send_row.shape[2]
    number = np.zeros(patches * 4, np.int32)
    for e, (p, k) in enumerate(edges):
        number[p * 4 + k] = e
    take = [p * 4 + k for p, k in edges]
    whole = patches + patches % 2
    rows = whole * side
    corners, most, send, home, place, choices, second = ghost_plan(neighbour, rim_side, patches, outer)
    tables = [
        number[send_row].reshape(-1),
        recv_dev.reshape(tiles, -1)[:, take].reshape(-1),
        recv_slot.reshape(tiles, -1)[:, take].reshape(-1),
        send.reshape(-1), home.reshape(-1), place.reshape(-1), second.reshape(-1),
    ]
    starts = [int(x) for x in np.cumsum([0] + [t.size for t in tables])[:-1]]
    table = np.concatenate(tables)
    weights = conv_weight[0].reshape(LAYERS, 3, 3 * chan, chan)
    held = sections + sections // 2
    smem = pl.BlockSpec(memory_space=pltpu.SMEM)
    vmem = pl.BlockSpec(memory_space=pltpu.VMEM)
    wide = pltpu.VMEM((chan // LANES, side * rows, LANES), jnp.float32)
    got = pltpu.VMEM((tiles - 1, slots, side, chan), jnp.bfloat16)
    more = pltpu.VMEM((tiles - 1, slots + 1, side, chan), jnp.bfloat16)
    flops = 2 * micro * side * rows * chan * chan * (9 * LAYERS + 1)
    return pl.pallas_call(
        functools.partial(window_kernel, tiles, sections, patches, micro, slots, inner, outer, early, late, corners, most, choices, starts),
        out_shape=pltpu.VMEM((1,) + states.shape, jnp.bfloat16),
        in_specs=[smem] * 2 + [pl.BlockSpec(memory_space=pl.ANY)] * 2 + [vmem, vmem],
        out_specs=vmem,
        scratch_shapes=[
            pltpu.VMEM((sections,) + weights.shape, jnp.bfloat16),
            pltpu.VMEM((sections, chan, chan), jnp.bfloat16),
            pltpu.VMEM((sections, 8, chan), jnp.float32),
            pltpu.VMEM((8, chan), jnp.float32),
            pltpu.VMEM(states.shape[1:], jnp.bfloat16),
            pltpu.VMEM((held, side, rows, chan), jnp.bfloat16),
            pltpu.VMEM((sections,) + states.shape[1:], jnp.bfloat16),
            wide, wide,
            pltpu.VMEM((side + 2, rows, 3 * chan), jnp.bfloat16),
            pltpu.VMEM((len(edges), side, chan), jnp.bfloat16),
            pltpu.VMEM((len(edges), side, chan), jnp.bfloat16),
            pltpu.VMEM((len(edges) * side, chan), jnp.float32),
            pltpu.VMEM(((tiles - 1) * 8 + 16, chan), jnp.float32),
            got, got, more, more, got, got, more, more,
            pltpu.SMEM((tiles,), jnp.int32),
            pltpu.SMEM(((tiles - 1) * slots,), jnp.int32),
            pltpu.SMEM((len(edges),), jnp.int32),
            pltpu.SMEM((len(edges),), jnp.int32),
            pltpu.SMEM((tiles * most,), jnp.int32),
            pltpu.SMEM((len(corners),), jnp.int32),
            pltpu.SemaphoreType.DMA((2, 2, tiles - 1)),
            pltpu.SemaphoreType.DMA((2, 2, tiles - 1)),
            pltpu.SemaphoreType.DMA((micro, 4)),
            pltpu.SemaphoreType.DMA((sections, 4)),
            pltpu.SemaphoreType.DMA((4,)),
            pltpu.SemaphoreType.DMA((sections,)),
            pltpu.SemaphoreType.DMA((micro,)),
            pltpu.SemaphoreType.REGULAR((micro,)),
            pltpu.SemaphoreType.DMA((micro, 19)),
            pltpu.SemaphoreType.DMA((sections, 19)),
            pltpu.SemaphoreType.DMA((sections, 2, 19)),
            pltpu.SemaphoreType.DMA((sections, 2, 19)),
            pltpu.SemaphoreType.DMA((len(pieces),)),
            pltpu.SemaphoreType.DMA((micro, len(pieces))),
            pltpu.SemaphoreType.DMA((1,)),
        ],
        compiler_params=pltpu.CompilerParams(
            collective_id=0, has_side_effects=True, vmem_limit_bytes=56 * 1024 * 1024
        ),
        cost_estimate=pl.CostEstimate(flops=flops, bytes_accessed=2**24, transcendentals=0),
    )(
        placement, jnp.asarray(table, jnp.int32),
        states, weights, skip_weight, bias,
    )


def solution(mesh):
    in_specs = (
        P(None, "tile", None, None, None),
        P("section", None, None, None, None, None),
        P("section", None, None),
        P("section", None, None),
        P(),
    )
    out_specs = P("section", None, "tile", None, None, None)
    return jax.shard_map(
        on_device, mesh=mesh, in_specs=in_specs, out_specs=out_specs, check_vma=False
    )
```
